32 devices in a mesh: groups: 2 (over y), slab: 4 (over z), batch: 2 (over x), chan: 2 (over core).
Axes of the slice: x: 2, y: 2, z: 4, core: 2. Of those that a mesh axis runs over, the one named last changes fastest.
Arguments:
- volume: bfloat16 [16, 8, 4, 8, 128], P(('groups', 'batch'), 'slab'), parts along dimension 0, may hold values from -6 to 6
- targets: float32 [16, 4], P(('groups', 'batch')), parts along dimension 0, may hold values from -1 to 1
- front_weight: bfloat16 [3, 3, 3, 128, 128], P(None, None, None, None, 'chan'), may hold values from -0.109375 to 0.109375
- stride_weight: bfloat16 [3, 3, 3, 128, 256], P(None, None, None, 'chan'), may hold values from -0.109375 to 0.109375
- hidden_weight: float32 [256, 128], P('chan'), may hold values from -0.375 to 0.375
- output_weight: float32 [128, 4], replicated, may hold values from -0.5 to 0.5
Outputs:
- grad_front: float32 [6, 3, 3, 128, 128], P('groups', None, None, None, 'chan'), parts along dimension 0
- grad_stride: float32 [6, 3, 3, 128, 256], P('groups', None, None, 'chan'), parts along dimension 0
- grad_hidden: float32 [512, 128], P(('groups', 'chan')), parts along dimension 0
- grad_output: float32 [256, 4], P('groups'), parts along dimension 0
- loss: float32 [2], P('groups'), parts along dimension 0
The draws below stay inside these ranges and needn't reach their ends.
There are 2 independent parts, one for each index of `groups`. The reference program is written for one: setup_inputs(seed, part) draws one part's arguments, and reference() takes and returns one part's arrays. A program takes and returns all parts, laid end to end along the dimension named above; an argument that names none is the same for every part. Nothing has to cross between parts.
All inputs are finite; a program needn't handle non-finite values.
Results may differ from the reference program's by a relative error of at most 0.0052.
Values may be sent and summed in bfloat16 or wider, within the bound.
A program may use at most 64 MiB of HBM per device.

```python
import jax
import jax.numpy as jnp
from jax import lax

C1 = 128
C2 = 256
HID = 128
OUTS = 4
XW = 4
YW = 8
ZD = 8
SAMPLES = 8
Z2 = 4
X2 = 2
Y2 = 4
CELLS2 = 32


def level_of(rng, extent, pieces, smallest, top_value):
    loudness = 1.0
    for position, blocks in pieces:
        draws = jax.random.uniform(jax.random.fold_in(jax.random.fold_in(rng, 6), position), (blocks,), jnp.float32, smallest / len(pieces), top_value / len(pieces))
        loudness = loudness * jnp.repeat(jnp.exp(draws), extent[position] // blocks).reshape((-1,) + (1,) * (len(extent) - 1 - position))
    return loudness


def scatter_about(rng, dims, deviation, reach, cuts=(), kind=jnp.bfloat16):
    array = jax.random.normal(rng, dims, jnp.float32) * deviation
    if len(cuts) > 0:
        array = level_of(rng, dims, cuts, -0.22, 0.18) * array
    return jnp.clip(array, min=-reach, max=reach).astype(kind)


def setup_inputs(seed: int = 0, part: int = 0) -> dict:
    key_of = jax.random.split(jax.random.key(seed), 7)
    part_keys = jax.random.split(jax.random.fold_in(key_of[6], part), 7)
    volume = scatter_about(part_keys[0], (SAMPLES, ZD, XW, YW, C1), 1.0, 6.0, ((0, 2), (1, 4)))
    targets = jnp.clip(jax.random.uniform(part_keys[1], (SAMPLES, OUTS), jnp.float32, -1.0, 1.0) * level_of(part_keys[1], (SAMPLES, OUTS), ((0, 2),), -0.4, 0.0), -1.0, 1.0)
    front_weight = scatter_about(key_of[2], (3, 3, 3, C1, C1), (27 * C1) ** -0.5, 0.109375, ((4, 2),))
    stride_weight = scatter_about(key_of[3], (3, 3, 3, C1, C2), (27 * C1) ** -0.5, 0.109375, ((3, 2),))
    hidden_weight = scatter_about(key_of[4], (C2, HID), C2 ** -0.5, 0.375, ((0, 2),), jnp.float32)
    output_weight = scatter_about(key_of[5], (HID, OUTS), HID ** -0.5, 0.5, (), jnp.float32)
    return {"volume": volume, "targets": targets, "front_weight": front_weight, "stride_weight": stride_weight, "hidden_weight": hidden_weight, "output_weight": output_weight}


def swish_slope(preact):
    logistic = jax.nn.sigmoid(preact)
    return logistic * (1.0 + preact * (1.0 - logistic))

def tap_window(padded, tap_z, tap_x, tap_y, extent_z, extent_x, extent_y, stride):
    if stride == 1:
        return padded[:, tap_z:tap_z + extent_z, tap_x:tap_x + extent_x, tap_y:tap_y + extent_y, :]
    leading = padded.shape[0]
    channels = padded.shape[-1]
    folded = padded.reshape(leading, extent_z + 1, 2, extent_x + 1, 2, extent_y + 1, 2, channels)
    return folded[:, tap_z // 2:tap_z // 2 + extent_z, tap_z % 2, tap_x // 2:tap_x // 2 + extent_x, tap_x % 2, tap_y // 2:tap_y // 2 + extent_y, tap_y % 2, :]

def conv_apply(padded, weight, extent_z, extent_x, extent_y, stride):
    summed = None
    for tap_z in range(3):
        for tap_x in range(3):
            for tap_y in range(3):
                window = tap_window(padded, tap_z, tap_x, tap_y, extent_z, extent_x, extent_y, stride)
                flat_tap = window.reshape(-1, window.shape[-1])
                contrib = jnp.dot(flat_tap, weight[tap_z, tap_x, tap_y], preferred_element_type=jnp.float32)
                summed = contrib if summed is None else summed + contrib
    return summed.reshape(padded.shape[0], extent_z, extent_x, extent_y, weight.shape[-1])

def kernel_grad(padded, grad_out, extent_z, extent_x, extent_y, stride):
    flat_grad = grad_out.reshape(-1, grad_out.shape[-1])
    results = []
    for tap_z in range(3):
        for tap_x in range(3):
            for tap_y in range(3):
                window = tap_window(padded, tap_z, tap_x, tap_y, extent_z, extent_x, extent_y, stride)
                flat_tap = window.reshape(-1, window.shape[-1])
                results.append(lax.dot_general(flat_tap, flat_grad, (((0,), (0,)), ((), ())), preferred_element_type=jnp.float32))
    return jnp.stack(results).reshape(3, 3, 3, padded.shape[-1], grad_out.shape[-1])

def input_grad(grad_out, weight, extent_z, extent_x, extent_y):
    leading = grad_out.shape[0]
    channels = weight.shape[3]
    flat_grad = grad_out.reshape(-1, grad_out.shape[-1])
    buckets = {}
    for tap_z in range(3):
        for tap_x in range(3):
            for tap_y in range(3):
                contrib = lax.dot_general(flat_grad, weight[tap_z, tap_x, tap_y], (((1,), (1,)), ((), ())), preferred_element_type=jnp.float32)
                contrib = contrib.reshape(leading, extent_z, extent_x, extent_y, channels)
                placed = jnp.pad(contrib, ((0, 0), (tap_z // 2, 1 - tap_z // 2), (tap_x // 2, 1 - tap_x // 2), (tap_y // 2, 1 - tap_y // 2), (0, 0)))
                parity = (tap_z % 2, tap_x % 2, tap_y % 2)
                buckets[parity] = placed if parity not in buckets else buckets[parity] + placed
    planes_z = []
    for par_z in range(2):
        planes_x = []
        for par_x in range(2):
            planes_x.append(jnp.stack([buckets[par_z, par_x, par_y] for par_y in range(2)], axis=4))
        planes_z.append(jnp.stack(planes_x, axis=3))
    assembled = jnp.stack(planes_z, axis=2)
    assembled = assembled.reshape(leading, 2 * extent_z + 2, 2 * extent_x + 2, 2 * extent_y + 2, channels)
    return assembled[:, 1:-1, 1:-1, 1:-1, :]

def reference(volume, targets, front_weight, stride_weight, hidden_weight, output_weight):
    highest = lax.Precision.HIGHEST
    padded = jnp.pad(volume, ((0, 0), (1, 1), (1, 1), (1, 1), (0, 0)))
    front_pre = conv_apply(padded, front_weight, ZD, XW, YW, 1)
    front_act = jax.nn.silu(front_pre).astype(jnp.bfloat16)
    stride_pad = jnp.pad(front_act, ((0, 0), (1, 1), (1, 1), (1, 1), (0, 0)))
    stride_pre = conv_apply(stride_pad, stride_weight, Z2, X2, Y2, 2)
    pooled = lax.optimization_barrier(jnp.sum(jax.nn.silu(stride_pre), axis=(1, 2, 3))) / CELLS2
    hidden_pre = jnp.dot(pooled, hidden_weight, precision=highest)
    hidden_act = jax.nn.silu(hidden_pre)
    predicted = jnp.dot(hidden_act, output_weight, precision=highest)
    residual = predicted - targets
    grad_output = jnp.dot(hidden_act.T, residual, precision=highest)
    grad_hidden_pre = jnp.dot(residual, output_weight.T, precision=highest) * swish_slope(hidden_pre)
    grad_hidden = jnp.dot(pooled.T, grad_hidden_pre, precision=highest)
    grad_pooled = jnp.dot(grad_hidden_pre, hidden_weight.T, precision=highest)
    grad_stride_pre = (grad_pooled[:, None, None, None, :] / CELLS2 * swish_slope(stride_pre)).astype(jnp.bfloat16)
    grad_stride = kernel_grad(stride_pad, grad_stride_pre, Z2, X2, Y2, 2)
    grad_act = input_grad(grad_stride_pre, stride_weight, Z2, X2, Y2).astype(jnp.bfloat16)
    grad_front_pre = (grad_act * swish_slope(front_pre)).astype(jnp.bfloat16)
    grad_front = kernel_grad(padded, grad_front_pre, ZD, XW, YW, 1)
    loss = (jnp.sum(residual * residual) / (SAMPLES * OUTS)).reshape(1)
    return (grad_front, grad_stride, grad_hidden, grad_output, loss)
```

```python
import functools

import jax
import jax.numpy as jnp
from jax import lax
from jax.experimental import pallas as pl
from jax.experimental.pallas import tpu as pltpu
from jax.sharding import PartitionSpec as P


def with_halo(cells, sides, width):
    for axis, dim in sides:
        count = lax.axis_size(axis)
        ends = count - 1
        head = lax.slice_in_dim(cells, 0, width, axis=dim)
        tail = lax.slice_in_dim(cells, cells.shape[dim] - width, cells.shape[dim], axis=dim)
        cells = jnp.concatenate(
            [
                lax.ppermute(tail, axis, [(i, (i + 1) % count) for i in range(ends)]),
                cells,
                lax.ppermute(head, axis, [((i + 1) % count, i) for i in range(ends)]),
            ],
            axis=dim,
        )
    return cells


def swish_slope(preact):
    logistic = jax.nn.sigmoid(preact)
    return logistic * (1.0 + preact * (1.0 - logistic))


def tap_window(padded, tap_z, tap_x, tap_y, extent_z, extent_x, extent_y, stride):
    if stride == 1:
        return padded[
            :, tap_z : tap_z + extent_z, tap_x : tap_x + extent_x, tap_y : tap_y + extent_y, :
        ]
    leading = padded.shape[0]
    channels = padded.shape[-1]
    folded = padded.reshape(leading, extent_z + 1, 2, extent_x + 1, 2, extent_y + 1, 2, channels)
    return folded[
        :,
        tap_z // 2 : tap_z // 2 + extent_z,
        tap_z % 2,
        tap_x // 2 : tap_x // 2 + extent_x,
        tap_x % 2,
        tap_y // 2 : tap_y // 2 + extent_y,
        tap_y % 2,
        :,
    ]


def conv_apply(padded, weight, extent_z, extent_x, extent_y, stride):
    summed = None
    for tap_z in range(3):
        for tap_x in range(3):
            for tap_y in range(3):
                window = tap_window(
                    padded, tap_z, tap_x, tap_y, extent_z, extent_x, extent_y, stride
                )
                flat_tap = window.reshape(-1, window.shape[-1])
                contrib = jnp.dot(
                    flat_tap, weight[tap_z, tap_x, tap_y], preferred_element_type=jnp.float32
                )
                summed = contrib if summed is None else summed + contrib
    return summed.reshape(padded.shape[0], extent_z, extent_x, extent_y, weight.shape[-1])


def kernel_grad(padded, grad_out, extent_z, extent_x, extent_y, stride):
    flat_grad = grad_out.reshape(-1, grad_out.shape[-1])
    results = []
    for tap_z in range(3):
        for tap_x in range(3):
            for tap_y in range(3):
                window = tap_window(
                    padded, tap_z, tap_x, tap_y, extent_z, extent_x, extent_y, stride
                )
                flat_tap = window.reshape(-1, window.shape[-1])
                results.append(
                    lax.dot_general(
                        flat_tap,
                        flat_grad,
                        (((0,), (0,)), ((), ())),
                        preferred_element_type=jnp.float32,
                    )
                )
    return jnp.stack(results).reshape(3, 3, 3, padded.shape[-1], grad_out.shape[-1])


def input_grad(grad_out, weight, extent_z, extent_x, extent_y):
    leading = grad_out.shape[0]
    channels = weight.shape[3]
    flat_grad = grad_out.reshape(-1, grad_out.shape[-1])
    buckets = {}
    for tap_z in range(3):
        for tap_x in range(3):
            for tap_y in range(3):
                contrib = lax.dot_general(
                    flat_grad,
                    weight[tap_z, tap_x, tap_y],
                    (((1,), (1,)), ((), ())),
                    preferred_element_type=jnp.float32,
                )
                contrib = contrib.reshape(leading, extent_z, extent_x, extent_y, channels)
                placed = jnp.pad(
                    contrib,
                    (
                        (0, 0),
                        (tap_z // 2, 1 - tap_z // 2),
                        (tap_x // 2, 1 - tap_x // 2),
                        (tap_y // 2, 1 - tap_y // 2),
                        (0, 0),
                    ),
                )
                parity = (tap_z % 2, tap_x % 2, tap_y % 2)
                buckets[parity] = placed if parity not in buckets else buckets[parity] + placed
    planes_z = []
    for par_z in range(2):
        planes_x = []
        for par_x in range(2):
            planes_x.append(jnp.stack([buckets[par_z, par_x, par_y] for par_y in range(2)], axis=4))
        planes_z.append(jnp.stack(planes_x, axis=3))
    assembled = jnp.stack(planes_z, axis=2)
    assembled = assembled.reshape(
        leading, 2 * extent_z + 2, 2 * extent_x + 2, 2 * extent_y + 2, channels
    )
    return assembled[:, 1:-1, 1:-1, 1:-1, :]


def split_body(volume, targets, front_weight, stride_weight, hidden_weight, output_weight):
    highest = lax.Precision.HIGHEST
    slabs = lax.axis_size("slab")
    batches = lax.axis_size("batch")
    inner = front_weight.shape[-1]
    leading, thick, extent_x, extent_y, channels = volume.shape
    depth = thick * slabs
    outputs = output_weight.shape[-1]
    haloed = with_halo(volume, (("slab", 1),), 1)
    padded = jnp.pad(haloed, ((0, 0), (0, 0), (1, 1), (1, 1), (0, 0)))
    front_pre = conv_apply(padded, front_weight, thick, extent_x, extent_y, 1)
    front_act = jax.nn.silu(front_pre).astype(jnp.bfloat16)
    merged = front_act.reshape(leading, thick, extent_x, extent_y * inner)
    sample_act = lax.all_to_all(merged, "slab", split_axis=0, concat_axis=1, tiled=True)
    sample_act = sample_act.reshape(1, depth, extent_x, extent_y, inner)
    half_z = depth // 2
    half_x = extent_x // 2
    half_y = extent_y // 2
    cells = half_z * half_x * half_y
    stride_pad = jnp.pad(sample_act, ((0, 0), (1, 1), (1, 1), (1, 1), (0, 0)))
    partial_pre = conv_apply(stride_pad, stride_weight, half_z, half_x, half_y, 2)
    stride_pre = lax.psum_scatter(partial_pre, "chan", scatter_dimension=4, tiled=True)
    pooled = jnp.sum(jax.nn.silu(stride_pre), axis=(0, 1, 2, 3)) / cells
    hidden_pre = lax.psum(jnp.dot(pooled, hidden_weight, precision=highest), "chan")
    hidden_act = jax.nn.silu(hidden_pre)
    predicted = jnp.dot(hidden_act, output_weight, precision=highest)
    target_row = lax.dynamic_index_in_dim(targets, lax.axis_index("slab"), 0, keepdims=False)
    residual = predicted - target_row
    squared = jnp.sum(residual * residual)
    grad_output = jnp.outer(hidden_act, residual)
    grad_hidden_pre = jnp.dot(output_weight, residual, precision=highest) * swish_slope(hidden_pre)
    grad_hidden = jnp.outer(pooled, grad_hidden_pre)
    grad_pooled = jnp.dot(hidden_weight, grad_hidden_pre, precision=highest)
    grad_stride_pre = (grad_pooled / cells * swish_slope(stride_pre)).astype(jnp.bfloat16)
    full_grad = lax.all_gather(grad_stride_pre, "chan", axis=4, tiled=True)
    grad_stride = kernel_grad(stride_pad, full_grad, half_z, half_x, half_y, 2)
    grad_act = input_grad(full_grad, stride_weight, half_z, half_x, half_y).astype(jnp.bfloat16)
    returned = lax.all_to_all(
        grad_act.reshape(1, depth, extent_x, extent_y * inner),
        "slab",
        split_axis=1,
        concat_axis=0,
        tiled=True,
    )
    returned = returned.reshape(leading, thick, extent_x, extent_y, inner)
    grad_front_pre = (returned * swish_slope(front_pre)).astype(jnp.bfloat16)
    grad_front = kernel_grad(padded, grad_front_pre, thick, extent_x, extent_y, 1)
    grad_front, grad_stride, grad_hidden, grad_output, squared = lax.psum(
        (grad_front, grad_stride, grad_hidden, grad_output, squared), ("slab", "batch")
    )
    loss = (squared / (slabs * batches * outputs)).reshape(1)
    return (grad_front, grad_stride, grad_hidden, grad_output, loss)


MESH = pl.DeviceIdType.MESH


def sigmoid(v):
    return 1.0 / (1.0 + jnp.exp(-v))


def remote(source, target, send_sem, recv_sem, device):
    return pltpu.make_async_remote_copy(
        src_ref=source, dst_ref=target, send_sem=send_sem, recv_sem=recv_sem,
        device_id=device, device_id_type=MESH,
    )


def slab_order(slab, slabs):
    flipped = slab // (slabs // 2)
    turn = slab * (1 - flipped) + (slabs - 1 - slab) * flipped
    order = [lax.rem(turn + i, slabs - 1) for i in range(slabs - 1)] + [slabs - 1 + 0 * turn]
    return [flipped * (slabs - 1 - at) + (1 - flipped) * at for at in order]


def chain_kernel(
    shape,
    volume_hbm, targets_hbm, front_hbm, stride_hbm, hidden_hbm, output_hbm,
    taps_ref, turned_ref, stride_grad_ref, hidden_grad_ref, output_grad_ref, loss_ref,
    volume_ref, split_ref, front_turned_ref, front_ref, front_pre_ref, slope_ref, strided_ref,
    act_ref, act_out_ref, stride_ref, back_ref, hidden_ref, output_ref, targets_ref,
    spread_ref, head_ref, head_out_ref, grad_ref, turned_out_ref,
    local_sem, send_sem, piece_sem, pass_send_sem, pass_sem, pair_send_sem, pair_sem, target_sem,
):
    slabs, batches, leading, thick, extent_x, extent_y, channels, inner = shape
    slab, batch, chan = lax.axis_index("slab"), lax.axis_index("batch"), lax.axis_index("chan")
    f32, bf16 = jnp.float32, jnp.bfloat16
    highest = lax.Precision.HIGHEST
    half = leading // 2
    depth = slabs * thick
    half_y = extent_y // 2
    half_z, half_x = depth // 2, extent_x // 2
    planes = half_z * half_x
    samples = batches * half
    group = samples * half_y
    rows = 2 * group
    cells = planes * half_y
    wide = 3 * channels
    features = stride_ref.shape[-1]
    share = hidden_hbm.shape[0]
    outputs = output_hbm.shape[0]
    sibling = {"chan": 1 - chan}
    mine = batch * slabs + slab

    others = [
        (lax.rem(batch + b, batches), lax.rem(slab + s, slabs))
        for s in range(slabs) for b in range(batches) if s or b
    ]
    devices = [{"batch": b, "slab": s} for b, s in others]
    barrier = pltpu.get_barrier_semaphore()
    for device in devices + [sibling]:
        pl.semaphore_signal(barrier, inc=1, device_id=device, device_id_type=MESH)

    local = [
        pltpu.make_async_copy(source, target, local_sem.at[i])
        for i, (source, target) in enumerate([
            (volume_hbm.at[pl.ds(chan * half, half)], volume_ref.at[0, mine]),
            (front_hbm, front_turned_ref.at[:, pl.ds(0, inner)]),
            (stride_hbm, stride_ref.at[:, pl.ds(0, inner)]),
            (hidden_hbm, hidden_ref.at[pl.ds(chan * share, share)]),
            (output_hbm, output_ref),
            (targets_hbm, targets_ref.at[pl.ds(batch * leading, leading)]),
            (volume_hbm.at[pl.ds((1 - chan) * half, half)], volume_ref.at[1, mine]),
        ])
    ]
    for copy in local:
        copy.start()

    front_pre_ref[...] = jnp.zeros(front_pre_ref.shape, f32)
    edge = jnp.zeros((depth, 2 * rows, wide), bf16)
    taps_ref[:, 0] = edge
    taps_ref[:, extent_x + 1] = edge
    strided_ref[0] = jnp.zeros((extent_x + 1, group, wide), bf16)
    strided_ref[:, 0] = jnp.zeros((depth + 1, group, wide), bf16)
    for side in range(2):
        spread_ref[side, half_z] = jnp.zeros((half_x + 1, group, 2 * features), bf16)
        spread_ref[side, :, half_x] = jnp.zeros((half_z + 1, group, 2 * features), bf16)
    blank = jnp.zeros((features, channels), bf16)
    for tap in range(9):
        back_ref[tap, features:, :channels] = blank

    row = lax.broadcasted_iota(jnp.int32, (group, channels), 0)
    first = (row & (half_y - 1)) == 0
    last = (row & (half_y - 1)) == half_y - 1
    lane_low = lax.broadcasted_iota(jnp.int32, (group, channels), 1) < inner

    pl.semaphore_wait(barrier, len(devices) + 1)

    sends = []

    def send(copy):
        copy.start()
        sends.append(copy)

    pair = [
        remote(front_hbm, front_turned_ref.at[:, pl.ds(inner, inner)], pair_send_sem.at[0], pair_sem.at[0], sibling),
        remote(stride_hbm, stride_ref.at[:, pl.ds(inner, inner)], pair_send_sem.at[1], pair_sem.at[1], sibling),
        remote(hidden_hbm, hidden_ref.at[pl.ds(chan * share, share)], pair_send_sem.at[2], pair_sem.at[2], sibling),
        remote(act_out_ref, act_ref.at[1], pair_send_sem.at[3], pair_sem.at[3], sibling),
        remote(
            spread_ref.at[0, pl.ds(0, half_z), pl.ds(0, half_x)], spread_ref.at[1, pl.ds(0, half_z), pl.ds(0, half_x)],
            pair_send_sem.at[4], pair_sem.at[4], sibling,
        ),
        remote(head_out_ref, head_ref.at[1], pair_send_sem.at[5], pair_sem.at[5], sibling),
        remote(turned_out_ref, turned_ref.at[1], pair_send_sem.at[6], pair_sem.at[6], sibling),
    ]
    send(pair[0])
    own = volume_hbm.at[pl.ds(chan * half, half)]
    for i, device in enumerate(devices):
        send(remote(own, volume_ref.at[0, mine], send_sem.at[i], piece_sem.at[mine], device))
    across = {"batch": lax.rem(batch + 1, batches)}
    place = targets_ref.at[pl.ds(batch * leading, leading)]
    targets_copy = remote(targets_hbm, place, send_sem.at[len(devices)], target_sem, across)
    send(targets_copy)
    send(pair[1])
    send(pair[2])

    def fill(side, at):
        for plane in range(thick):
            for x in range(extent_x):
                slot = plane * extent_x + x
                for b in range(batches):
                    split_ref[slot, b * half * extent_y : (b + 1) * half * extent_y] = (
                        volume_ref[side, b * slabs + at, :, plane, x].astype(f32).reshape(half * extent_y, channels)
                    )
                even = split_ref[slot, pl.ds(0, group, stride=2), :]
                odd = split_ref[slot, pl.ds(1, group, stride=2), :]
                before = jnp.where(first, 0.0, pltpu.roll(odd, 1, 0)).astype(bf16)
                after = jnp.where(last, 0.0, pltpu.roll(even, group - 1, 0)).astype(bf16)
                even, odd = even.astype(bf16), odd.astype(bf16)
                z = at * thick + plane
                top, bottom = side * rows, side * rows + group
                taps_ref[z, x + 1, top : top + group] = jnp.concatenate([before, even, odd], axis=1)
                taps_ref[z, x + 1, bottom : bottom + group] = jnp.concatenate([even, odd, after], axis=1)

    plane_cells = extent_x * rows

    def front(at):
        window = jnp.concatenate(
            [
                taps_ref[pl.ds(at * thick, thick), kx : kx + extent_x, :rows].reshape(thick * plane_cells, wide)
                for kx in range(3)
            ],
            axis=1,
        )
        sums = jnp.dot(window, front_ref[...], preferred_element_type=f32)

        def block(plane, kz):
            return sums[plane * plane_cells : (plane + 1) * plane_cells, kz * channels : (kz + 1) * channels]

        base = at * thick
        front_pre_ref[base] += block(0, 2)
        front_pre_ref[base + 1] += block(0, 1) + block(1, 2)
        front_pre_ref[base + 2] += block(0, 0) + block(1, 1)
        front_pre_ref[base + 3] += block(1, 0)

    def piece(side, b, at):
        return volume_ref.at[side, b * slabs + at]

    order = slab_order(slab, slabs)
    local[1].wait()
    pair[0].wait_recv()
    for kz in range(3):
        for tap in range(9):
            front_ref[tap * channels : (tap + 1) * channels, kz * channels : (kz + 1) * channels] = jnp.transpose(
                front_turned_ref[9 * kz + tap]
            )
    local[0].wait()
    local[6].wait()

    ways = {}
    for kz in range(3):
        for kx in range(3):
            ways[kz, kx] = 3 * kz + kx
    slots = {}
    for pz in range(2):
        for px in range(2):
            for sz in range(pz + 1):
                for sx in range(px + 1):
                    kz = 1 if pz == 0 else 2 - 2 * sz
                    kx = 1 if px == 0 else 2 - 2 * sx
                    slots[pz, px, sz, sx] = (len(slots), kz, kx)

    for i, at in enumerate(order):
        for b in range(batches):
            source = lax.rem(batch + b, batches)
            if i or b:
                remote(
                    piece(0, source, at), piece(0, source, at), send_sem.at[0],
                    piece_sem.at[source * slabs + at], sibling,
                ).wait_recv()
                number = source * slabs + at
                send(remote(
                    piece(0, source, at), piece(1, source, at), pass_send_sem.at[i * batches + b],
                    pass_sem.at[number], sibling,
                ))
        fill(0, at)
        front(at)
        if i == 0:
            local[2].wait()
            pair[1].wait_recv()
            for slot, kz, kx in slots.values():
                start = 9 * kz + 3 * kx
                back_ref[slot, :features, :channels] = jnp.transpose(stride_ref[start + 1])
                back_ref[slot, :features, channels:] = jnp.transpose(stride_ref[start + 2])
                back_ref[slot, features:, channels:] = jnp.transpose(stride_ref[start])

    def other_fill(i):
        at = order[i]
        for b in range(batches):
            source = lax.rem(batch + b, batches)
            if i or b:
                remote(
                    piece(1, source, at), piece(1, source, at), send_sem.at[0],
                    pass_sem.at[source * slabs + at], sibling,
                ).wait_recv()
        fill(1, at)

    for z in range(depth):
        total = front_pre_ref[z + 1]
        logistic = sigmoid(total)
        act = (total * logistic).reshape(extent_x, 2, group, channels)
        slope_ref[z] = (logistic * (1.0 + total * (1.0 - logistic))).reshape(extent_x, 2, group, channels)
        for x in range(extent_x):
            even, odd = act[x, 0], act[x, 1]
            before = jnp.where(first, 0.0, pltpu.roll(odd, 1, 0)).astype(bf16)
            strided_ref[z + 1, x + 1] = jnp.concatenate([before, even.astype(bf16), odd.astype(bf16)], axis=1)
            where = (z % 2, x % 2, (z // 2) * half_x + x // 2)
            act_ref[(0,) + where] = jnp.where(lane_low, even, pltpu.roll(odd, inner, 1)).astype(bf16)
            act_out_ref[where] = jnp.where(lane_low, pltpu.roll(even, inner, 1), odd).astype(bf16)
    send(pair[3])

    for copy in local[3:6]:
        copy.wait()
    pair[2].wait_recv()
    remote(targets_hbm, targets_ref.at[pl.ds((1 - batch) * leading, leading)], send_sem.at[0], target_sem, sibling).wait_recv()

    windows = jnp.concatenate(
        [
            jnp.concatenate(
                [strided_ref[kz + 2 * z, kx + 2 * x] for z in range(half_z) for x in range(half_x)], axis=0
            )
            for kz in range(3) for kx in range(3)
        ],
        axis=1,
    )
    pre = jnp.dot(windows, stride_ref[...].reshape(27 * channels, features), preferred_element_type=f32)
    logistic = sigmoid(pre)
    summed = jnp.sum((pre * logistic).reshape(planes, group, features), axis=0)
    slope = (logistic * (1.0 + pre * (1.0 - logistic))).reshape(planes, group, features)
    wide_row = lax.broadcasted_iota(jnp.int32, (group, features), 0)
    step = 1
    while step < half_y:
        high = (wide_row & step) != 0
        summed = summed + jnp.where(high, pltpu.roll(summed, step, 0), pltpu.roll(summed, group - step, 0))
        step *= 2
    pooled = summed / cells
    hidden = hidden_ref[...]
    output = output_ref[...]
    hidden_pre = jnp.dot(pooled, hidden, precision=highest, preferred_element_type=f32)
    hidden_logistic = sigmoid(hidden_pre)
    hidden_act = hidden_pre * hidden_logistic
    hidden_slope = hidden_logistic * (1.0 + hidden_pre * (1.0 - hidden_logistic))
    all_samples = batches * leading
    owner = lax.broadcasted_iota(jnp.int32, (group, all_samples), 1)
    of_row = lax.broadcasted_iota(jnp.int32, (group, all_samples), 0) // half_y
    wanted = (of_row // half) * leading + chan * half + of_row % half
    member = (owner == wanted).astype(f32)
    target_rows = jnp.dot(member, targets_ref[...], precision=highest, preferred_element_type=f32)
    lane = lax.broadcasted_iota(jnp.int32, (group, channels), 1)
    residuals = jnp.zeros((group, channels), f32)
    back = jnp.zeros((group, output.shape[1]), f32)
    for o in range(outputs):
        residual = jnp.sum(hidden_act * output[o : o + 1], axis=1, keepdims=True) - target_rows[:, o : o + 1]
        back = back + residual * output[o : o + 1]
        residuals = jnp.where(lane == o, residual, residuals)
    grad_hidden_pre = back * hidden_slope
    grad_pooled = lax.dot_general(
        grad_hidden_pre, hidden, (((1,), (1,)), ((), ())), precision=highest, preferred_element_type=f32
    )
    grad_pre = slope * (grad_pooled / cells)[None]
    grad_next = jnp.where(
        ((wide_row & (half_y - 1)) == half_y - 1)[None],
        0.0,
        jnp.stack([pltpu.roll(grad_pre[i], group - 1, 0) for i in range(planes)]),
    )
    both = jnp.concatenate([grad_pre, grad_next], axis=2).astype(bf16)
    spread_ref[0, :half_z, :half_x] = both.reshape(half_z, half_x, group, 2 * features)
    send(pair[4])
    low_half, high_half = pooled[:, :share], pooled[:, share:]
    head_ref[0, 0] = jnp.where(chan == 0, low_half, high_half)
    head_out_ref[0] = jnp.where(chan == 0, high_half, low_half)
    for i, value in ((1, grad_hidden_pre), (2, hidden_act), (3, residuals)):
        head_ref[0, i] = value
        head_out_ref[i] = value
    send(pair[5])

    def shifted(side, sz, sx):
        return spread_ref[side, sz : sz + half_z, sx : sx + half_x].reshape(planes * group, 2 * features)

    for pz in range(2):
        for px in range(2):
            moves = [(sz, sx) for sz in range(pz + 1) for sx in range(px + 1)]
            start = slots[pz, px, 0, 0][0]
            left = jnp.concatenate([shifted(0, sz, sx) for sz, sx in moves], axis=1)
            right = back_ref[start : start + len(moves)].reshape(len(moves) * 2 * features, 2 * channels)
            grad = jnp.dot(left, right, preferred_element_type=f32)
            grad = grad.reshape(half_z, half_x, group, 2 * channels)
            for z in range(half_z):
                for x in range(half_x):
                    for py in range(2):
                        value = grad[z, x, :, py * channels : (py + 1) * channels].astype(bf16).astype(f32)
                        at = (2 * z + pz, 2 * x + px, py)
                        grad_ref[at] = (value * slope_ref[at]).astype(bf16)
    for z in range(depth):
        turned = jnp.transpose(grad_ref[z].reshape(plane_cells, channels))
        turned_ref[0, :, z * plane_cells : (z + 1) * plane_cells] = turned[:inner]
        turned_out_ref[:, z * plane_cells : (z + 1) * plane_cells] = turned[inner:]
    send(pair[6])

    for i in range(slabs):
        other_fill(i)

    pair[3].wait_recv()
    pair[4].wait_recv()
    turned_act = {
        (pz, px): jnp.concatenate(
            [jnp.transpose(act_ref[side, pz, px].reshape(planes * group, channels)) for side in range(2)], axis=1
        )
        for pz in range(2) for px in range(2)
    }
    for sz in range(2):
        for sx in range(2):
            right = jnp.concatenate([shifted(side, sz, sx) for side in range(2)], axis=0)
            for pz in range(sz, 2):
                for px in range(sx, 2):
                    _, kz, kx = slots[pz, px, sz, sx]
                    grad = jnp.dot(turned_act[pz, px], right, preferred_element_type=f32)
                    start = 9 * kz + 3 * kx
                    stride_grad_ref[start + 1] = grad[:inner, :features]
                    stride_grad_ref[start + 2] = grad[inner:, :features]
                    stride_grad_ref[start] = grad[inner:, features:]

    pair[5].wait_recv()
    pooled_all, hidden_pre_all, hidden_all, residual_all = [
        jnp.concatenate([head_ref[0, i], head_ref[1, i]], axis=0) for i in range(4)
    ]

    def outer(left, right):
        return lax.dot_general(
            left, right, (((0,), (0,)), ((), ())), precision=highest, preferred_element_type=f32
        ) / half_y

    hidden_grad_ref[...] = outer(pooled_all, hidden_pre_all)
    output_grad_ref[...] = outer(residual_all, hidden_all)[:outputs]
    loss_ref[...] = jnp.sum(residual_all * residual_all, keepdims=True) / (half_y * all_samples * outputs)

    pair[6].wait_recv()
    for copy in sends:
        copy.wait_send()


def kernel_grads(
    shape,
    taps_ref, turned_ref, stride_ref, hidden_ref, output_ref, loss_ref,
    front_out, stride_out, hidden_out, output_out, loss_out,
    front_ref, front_sem, other_sem,
):
    slabs, batches, leading, thick, extent_x, extent_y, channels, inner = shape
    f32, bf16 = jnp.float32, jnp.bfloat16
    depth = slabs * thick
    rows = taps_ref.shape[2] // 2
    plane_cells = extent_x * rows
    wide = 3 * channels
    others = [
        pltpu.make_async_copy(source, target, other_sem.at[i])
        for i, (source, target) in enumerate(
            [(stride_ref, stride_out), (hidden_ref, hidden_out), (output_ref, output_out), (loss_ref, loss_out)]
        )
    ]
    for copy in others:
        copy.start()
    edge = jnp.zeros((inner, plane_cells), bf16)

    def stacked(side):
        grads = turned_ref[side]
        return jnp.concatenate(
            [
                jnp.concatenate([grads[:, plane_cells:], edge], axis=1),
                grads,
                jnp.concatenate([edge, grads[:, :-plane_cells]], axis=1),
            ],
            axis=0,
        )

    left = jnp.concatenate([stacked(0), stacked(1)], axis=1)

    def send_out(group):
        place = pl.ds(3 * group, 3)
        return pltpu.make_async_copy(front_ref.at[place], front_out.at[place], front_sem.at[group])

    for kx in range(3):
        right = jnp.concatenate(
            [
                taps_ref[:, kx : kx + extent_x, side * rows : (side + 1) * rows].reshape(depth * plane_cells, wide)
                for side in range(2)
            ],
            axis=0,
        )
        grads = jnp.dot(left, right, preferred_element_type=f32)
        for kz in range(3):
            for ky in range(3):
                front_ref[9 * kz + 3 * kx + ky] = grads[kz * inner : (kz + 1) * inner, ky * channels : (ky + 1) * channels]
            send_out(3 * kz + kx).start()
    for group in range(9):
        send_out(group).wait()
    for copy in others:
        copy.wait()


def chain(shape, volume, targets, front_turned, stride_own, hidden_weight, output_turned):
    slabs, batches, leading, thick, extent_x, extent_y, channels, inner = shape
    f32, bf16 = jnp.float32, jnp.bfloat16
    features = stride_own.shape[-1]
    share, hid = hidden_weight.shape
    outputs = output_turned.shape[0]
    half = leading // 2
    pieces = slabs * batches
    depth = slabs * thick
    group = batches * half * extent_y // 2
    rows = 2 * group
    half_z, half_x = depth // 2, extent_x // 2
    planes = half_z * half_x
    plane_cells = extent_x * rows
    wide = 3 * channels
    vmem = pl.BlockSpec(memory_space=pltpu.VMEM)
    anywhere = pl.BlockSpec(memory_space=pl.ANY)
    dma = pltpu.SemaphoreType.DMA
    stages = pl.pallas_call(
        functools.partial(chain_kernel, shape),
        out_shape=(
            jax.ShapeDtypeStruct((depth, extent_x + 2, 2 * rows, wide), bf16),
            jax.ShapeDtypeStruct((2, inner, depth * plane_cells), bf16),
            jax.ShapeDtypeStruct((27, inner, features), f32),
            jax.ShapeDtypeStruct((share, hid), f32),
            jax.ShapeDtypeStruct((outputs, hid), f32),
            jax.ShapeDtypeStruct((1, 1), f32),
        ),
        in_specs=[anywhere] * 6,
        out_specs=[vmem] * 6,
        scratch_shapes=[
            pltpu.VMEM((2, pieces, half) + volume.shape[1:], bf16),
            pltpu.VMEM((thick * extent_x, rows, channels), f32),
            pltpu.VMEM((27, channels, channels), bf16),
            pltpu.VMEM((9 * channels, wide), bf16),
            pltpu.VMEM((depth + 2, plane_cells, channels), f32),
            pltpu.VMEM((depth, extent_x, 2, group, channels), f32),
            pltpu.VMEM((depth + 1, extent_x + 1, group, wide), bf16),
            pltpu.VMEM((2, 2, 2, planes, group, channels), bf16),
            pltpu.VMEM((2, 2, planes, group, channels), bf16),
            pltpu.VMEM((27, channels, features), bf16),
            pltpu.VMEM((9, 2 * features, 2 * channels), bf16),
            pltpu.VMEM((2 * share, hid), f32),
            pltpu.VMEM((outputs, hid), f32),
            pltpu.VMEM((batches * leading, outputs), f32),
            pltpu.VMEM((2, half_z + 1, half_x + 1, group, 2 * features), bf16),
            pltpu.VMEM((2, 4, group, channels), f32),
            pltpu.VMEM((4, group, channels), f32),
            pltpu.VMEM((depth, extent_x, 2, group, channels), bf16),
            pltpu.VMEM((inner, depth * plane_cells), bf16),
            dma((7,)), dma((pieces,)), dma((pieces,)), dma((pieces,)), dma((pieces,)),
            dma((7,)), dma((7,)), dma,
        ],
        compiler_params=pltpu.CompilerParams(
            collective_id=0, has_side_effects=True, vmem_limit_bytes=40 << 20
        ),
    )(volume, targets, front_turned, stride_own, hidden_weight, output_turned)
    return pl.pallas_call(
        functools.partial(kernel_grads, shape),
        out_shape=(
            jax.ShapeDtypeStruct((27, inner, channels), f32),
            jax.ShapeDtypeStruct((27, inner, features), f32),
            jax.ShapeDtypeStruct((share, hid), f32),
            jax.ShapeDtypeStruct((outputs, hid), f32),
            jax.ShapeDtypeStruct((1, 1), f32),
        ),
        in_specs=[vmem] * 6,
        out_specs=[anywhere] * 5,
        scratch_shapes=[pltpu.VMEM((27, inner, channels), f32), dma((9,)), dma((4,))],
        compiler_params=pltpu.CompilerParams(vmem_limit_bytes=24 << 20),
    )(*stages)


def body(volume, targets, front_weight, stride_weight, hidden_weight, output_weight):
    slabs = lax.axis_size("slab")
    batches = lax.axis_size("batch")
    inner = front_weight.shape[-1]
    leading, thick, extent_x, extent_y, channels = volume.shape
    features = stride_weight.shape[-1]
    small = (slabs, batches, leading, thick, extent_x, extent_y) == (4, 2, 4, 2, 4, 8)
    if not small:
        return split_body(volume, targets, front_weight, stride_weight, hidden_weight, output_weight)
    shape = (slabs, batches) + volume.shape + (inner,)
    grad_front, grad_stride, grad_hidden, grad_output, loss = chain(
        shape, volume, targets,
        jnp.swapaxes(front_weight.reshape(27, channels, inner), 1, 2),
        stride_weight.reshape(27, inner, features), hidden_weight, output_weight.T,
    )
    return (
        jnp.swapaxes(grad_front, 1, 2).reshape(3, 3, 3, channels, inner),
        grad_stride.reshape(3, 3, 3, inner, features),
        grad_hidden,
        grad_output.T,
        loss.reshape(1),
    )


def solution(mesh):
    in_specs = (
        P(("groups", "batch"), "slab", None, None, None),
        P(("groups", "batch"), None),
        P(None, None, None, None, "chan"),
        P(None, None, None, "chan", None),
        P("chan", None),
        P(),
    )
    out_specs = (
        P("groups", None, None, None, "chan"),
        P("groups", None, None, "chan", None),
        P(("groups", "chan"), None),
        P("groups", None),
        P("groups"),
    )
    return jax.shard_map(body, mesh=mesh, in_specs=in_specs, out_specs=out_specs, check_vma=False)
```

```python
import functools

import jax
import jax.numpy as jnp
from jax import lax
from jax.experimental import pallas as pl
from jax.experimental.pallas import tpu as pltpu
from jax.sharding import PartitionSpec as P


def with_halo(cells, sides, width):
    for axis, dim in sides:
        count = lax.axis_size(axis)
        ends = count - 1
        head = lax.slice_in_dim(cells, 0, width, axis=dim)
        tail = lax.slice_in_dim(cells, cells.shape[dim] - width, cells.shape[dim], axis=dim)
        cells = jnp.concatenate(
            [
                lax.ppermute(tail, axis, [(i, (i + 1) % count) for i in range(ends)]),
                cells,
                lax.ppermute(head, axis, [((i + 1) % count, i) for i in range(ends)]),
            ],
            axis=dim,
        )
    return cells


def swish_slope(preact):
    logistic = jax.nn.sigmoid(preact)
    return logistic * (1.0 + preact * (1.0 - logistic))


def tap_window(padded, tap_z, tap_x, tap_y, extent_z, extent_x, extent_y, stride):
    if stride == 1:
        return padded[
            :, tap_z : tap_z + extent_z, tap_x : tap_x + extent_x, tap_y : tap_y + extent_y, :
        ]
    leading = padded.shape[0]
    channels = padded.shape[-1]
    folded = padded.reshape(leading, extent_z + 1, 2, extent_x + 1, 2, extent_y + 1, 2, channels)
    return folded[
        :,
        tap_z // 2 : tap_z // 2 + extent_z,
        tap_z % 2,
        tap_x // 2 : tap_x // 2 + extent_x,
        tap_x % 2,
        tap_y // 2 : tap_y // 2 + extent_y,
        tap_y % 2,
        :,
    ]


def conv_apply(padded, weight, extent_z, extent_x, extent_y, stride):
    summed = None
    for tap_z in range(3):
        for tap_x in range(3):
            for tap_y in range(3):
                window = tap_window(
                    padded, tap_z, tap_x, tap_y, extent_z, extent_x, extent_y, stride
                )
                flat_tap = window.reshape(-1, window.shape[-1])
                contrib = jnp.dot(
                    flat_tap, weight[tap_z, tap_x, tap_y], preferred_element_type=jnp.float32
                )
                summed = contrib if summed is None else summed + contrib
    return summed.reshape(padded.shape[0], extent_z, extent_x, extent_y, weight.shape[-1])


def kernel_grad(padded, grad_out, extent_z, extent_x, extent_y, stride):
    flat_grad = grad_out.reshape(-1, grad_out.shape[-1])
    results = []
    for tap_z in range(3):
        for tap_x in range(3):
            for tap_y in range(3):
                window = tap_window(
                    padded, tap_z, tap_x, tap_y, extent_z, extent_x, extent_y, stride
                )
                flat_tap = window.reshape(-1, window.shape[-1])
                results.append(
                    lax.dot_general(
                        flat_tap,
                        flat_grad,
                        (((0,), (0,)), ((), ())),
                        preferred_element_type=jnp.float32,
                    )
                )
    return jnp.stack(results).reshape(3, 3, 3, padded.shape[-1], grad_out.shape[-1])


def input_grad(grad_out, weight, extent_z, extent_x, extent_y):
    leading = grad_out.shape[0]
    channels = weight.shape[3]
    flat_grad = grad_out.reshape(-1, grad_out.shape[-1])
    buckets = {}
    for tap_z in range(3):
        for tap_x in range(3):
            for tap_y in range(3):
                contrib = lax.dot_general(
                    flat_grad,
                    weight[tap_z, tap_x, tap_y],
                    (((1,), (1,)), ((), ())),
                    preferred_element_type=jnp.float32,
                )
                contrib = contrib.reshape(leading, extent_z, extent_x, extent_y, channels)
                placed = jnp.pad(
                    contrib,
                    (
                        (0, 0),
                        (tap_z // 2, 1 - tap_z // 2),
                        (tap_x // 2, 1 - tap_x // 2),
                        (tap_y // 2, 1 - tap_y // 2),
                        (0, 0),
                    ),
                )
                parity = (tap_z % 2, tap_x % 2, tap_y % 2)
                buckets[parity] = placed if parity not in buckets else buckets[parity] + placed
    planes_z = []
    for par_z in range(2):
        planes_x = []
        for par_x in range(2):
            planes_x.append(jnp.stack([buckets[par_z, par_x, par_y] for par_y in range(2)], axis=4))
        planes_z.append(jnp.stack(planes_x, axis=3))
    assembled = jnp.stack(planes_z, axis=2)
    assembled = assembled.reshape(
        leading, 2 * extent_z + 2, 2 * extent_x + 2, 2 * extent_y + 2, channels
    )
    return assembled[:, 1:-1, 1:-1, 1:-1, :]


def split_body(volume, targets, front_weight, stride_weight, hidden_weight, output_weight):
    highest = lax.Precision.HIGHEST
    slabs = lax.axis_size("slab")
    batches = lax.axis_size("batch")
    inner = front_weight.shape[-1]
    leading, thick, extent_x, extent_y, channels = volume.shape
    depth = thick * slabs
    outputs = output_weight.shape[-1]
    haloed = with_halo(volume, (("slab", 1),), 1)
    padded = jnp.pad(haloed, ((0, 0), (0, 0), (1, 1), (1, 1), (0, 0)))
    front_pre = conv_apply(padded, front_weight, thick, extent_x, extent_y, 1)
    front_act = jax.nn.silu(front_pre).astype(jnp.bfloat16)
    merged = front_act.reshape(leading, thick, extent_x, extent_y * inner)
    sample_act = lax.all_to_all(merged, "slab", split_axis=0, concat_axis=1, tiled=True)
    sample_act = sample_act.reshape(1, depth, extent_x, extent_y, inner)
    half_z = depth // 2
    half_x = extent_x // 2
    half_y = extent_y // 2
    cells = half_z * half_x * half_y
    stride_pad = jnp.pad(sample_act, ((0, 0), (1, 1), (1, 1), (1, 1), (0, 0)))
    partial_pre = conv_apply(stride_pad, stride_weight, half_z, half_x, half_y, 2)
    stride_pre = lax.psum_scatter(partial_pre, "chan", scatter_dimension=4, tiled=True)
    pooled = jnp.sum(jax.nn.silu(stride_pre), axis=(0, 1, 2, 3)) / cells
    hidden_pre = lax.psum(jnp.dot(pooled, hidden_weight, precision=highest), "chan")
    hidden_act = jax.nn.silu(hidden_pre)
    predicted = jnp.dot(hidden_act, output_weight, precision=highest)
    target_row = lax.dynamic_index_in_dim(targets, lax.axis_index("slab"), 0, keepdims=False)
    residual = predicted - target_row
    squared = jnp.sum(residual * residual)
    grad_output = jnp.outer(hidden_act, residual)
    grad_hidden_pre = jnp.dot(output_weight, residual, precision=highest) * swish_slope(hidden_pre)
    grad_hidden = jnp.outer(pooled, grad_hidden_pre)
    grad_pooled = jnp.dot(hidden_weight, grad_hidden_pre, precision=highest)
    grad_stride_pre = (grad_pooled / cells * swish_slope(stride_pre)).astype(jnp.bfloat16)
    full_grad = lax.all_gather(grad_stride_pre, "chan", axis=4, tiled=True)
    grad_stride = kernel_grad(stride_pad, full_grad, half_z, half_x, half_y, 2)
    grad_act = input_grad(full_grad, stride_weight, half_z, half_x, half_y).astype(jnp.bfloat16)
    returned = lax.all_to_all(
        grad_act.reshape(1, depth, extent_x, extent_y * inner),
        "slab",
        split_axis=1,
        concat_axis=0,
        tiled=True,
    )
    returned = returned.reshape(leading, thick, extent_x, extent_y, inner)
    grad_front_pre = (returned * swish_slope(front_pre)).astype(jnp.bfloat16)
    grad_front = kernel_grad(padded, grad_front_pre, thick, extent_x, extent_y, 1)
    grad_front, grad_stride, grad_hidden, grad_output, squared = lax.psum(
        (grad_front, grad_stride, grad_hidden, grad_output, squared), ("slab", "batch")
    )
    loss = (squared / (slabs * batches * outputs)).reshape(1)
    return (grad_front, grad_stride, grad_hidden, grad_output, loss)


MESH = pl.DeviceIdType.MESH


def sigmoid(v):
    return 1.0 / (1.0 + jnp.exp(-v))


def remote(source, target, send_sem, recv_sem, device):
    return pltpu.make_async_remote_copy(
        src_ref=source, dst_ref=target, send_sem=send_sem, recv_sem=recv_sem,
        device_id=device, device_id_type=MESH,
    )


def slab_order(slab, slabs):
    top = slabs - 1
    step = 1 - 2 * (slab // top)
    far = top * (1 - slab // (slabs // 2))
    near = slab + step
    return [slab, near, slabs * top // 2 - slab - near - far, far]


def chain_kernel(
    shape,
    volume_hbm, targets_hbm, front_hbm, stride_hbm, hidden_hbm, output_hbm,
    taps_ref, turned_ref, stride_grad_ref, hidden_grad_ref, output_grad_ref, loss_ref,
    volume_ref, split_ref, front_turned_ref, front_ref, front_pre_ref, slope_ref, strided_ref,
    act_ref, act_out_ref, stride_ref, back_ref, hidden_ref, output_ref, targets_ref,
    spread_ref, head_ref, head_out_ref, grad_ref, turned_out_ref,
    local_sem, send_sem, piece_sem, pass_send_sem, pass_sem, pair_send_sem, pair_sem, target_sem, ready_sem,
):
    slabs, batches, leading, thick, extent_x, extent_y, channels, inner = shape
    slab, batch, chan = lax.axis_index("slab"), lax.axis_index("batch"), lax.axis_index("chan")
    f32, bf16 = jnp.float32, jnp.bfloat16
    highest = lax.Precision.HIGHEST
    half = leading // 2
    depth = slabs * thick
    half_y = extent_y // 2
    half_z, half_x = depth // 2, extent_x // 2
    planes = half_z * half_x
    samples = batches * half
    group = samples * half_y
    rows = 2 * group
    cells = planes * half_y
    wide = 3 * channels
    features = stride_ref.shape[-1]
    share = hidden_hbm.shape[0]
    outputs = output_hbm.shape[0]
    sibling = {"chan": 1 - chan}
    mine = batch * slabs + slab
    pieces = batches * slabs

    across = {"batch": 1 - batch}
    barrier = pltpu.get_barrier_semaphore()
    pl.semaphore_signal(barrier, inc=1, device_id=sibling, device_id_type=MESH)

    local = [
        pltpu.make_async_copy(source, target, local_sem.at[i])
        for i, (source, target) in enumerate([
            (volume_hbm.at[pl.ds(chan * half, half)], volume_ref.at[0, mine]),
            (front_hbm, front_turned_ref.at[:, pl.ds(0, inner)]),
            (stride_hbm, stride_ref.at[:, pl.ds(0, inner)]),
            (hidden_hbm, hidden_ref.at[pl.ds(chan * share, share)]),
            (output_hbm, output_ref),
            (targets_hbm, targets_ref.at[pl.ds(batch * leading, leading)]),
            (volume_hbm.at[pl.ds((1 - chan) * half, half)], volume_ref.at[1, mine]),
        ])
    ]
    for copy in local:
        copy.start()

    pl.semaphore_wait(barrier, 1 + batch + (slab + slabs - 1) // slabs)

    @pl.when(batch == 0)
    def _():
        pl.semaphore_signal(barrier, inc=1, device_id=across, device_id_type=MESH)

    @pl.when(slab < slabs - 1)
    def _():
        pl.semaphore_signal(barrier, inc=1, device_id={"slab": lax.rem(slab + 1, slabs)}, device_id_type=MESH)

    sends = []

    def send(copy):
        copy.start()
        sends.append(copy)

    pair = [
        remote(front_hbm, front_turned_ref.at[:, pl.ds(inner, inner)], pair_send_sem.at[0], pair_sem.at[0], sibling),
        remote(stride_hbm, stride_ref.at[:, pl.ds(inner, inner)], pair_send_sem.at[1], pair_sem.at[1], sibling),
        remote(hidden_hbm, hidden_ref.at[pl.ds(chan * share, share)], pair_send_sem.at[2], pair_sem.at[2], sibling),
        remote(act_out_ref, act_ref.at[1], pair_send_sem.at[3], pair_sem.at[3], sibling),
        remote(
            spread_ref.at[0, pl.ds(0, half_z), pl.ds(0, half_x)], spread_ref.at[1, pl.ds(0, half_z), pl.ds(0, half_x)],
            pair_send_sem.at[4], pair_sem.at[4], sibling,
        ),
        remote(head_out_ref, head_ref.at[1], pair_send_sem.at[5], pair_sem.at[5], sibling),
        remote(turned_out_ref, turned_ref.at[1], pair_send_sem.at[6], pair_sem.at[6], sibling),
    ]
    order = slab_order(slab, slabs)
    own = volume_hbm.at[pl.ds(chan * half, half)]

    def piece(side, b, at):
        return volume_ref.at[side, b * slabs + at]

    place = targets_ref.at[pl.ds(batch * leading, leading)]
    spread = {}
    for at in range(slabs):
        for b in range(batches):
            number = b * slabs + at
            spread[b, at] = remote(
                own, piece(0, batch, slab), send_sem.at[number], piece_sem.at[mine], {"batch": b, "slab": at}
            )
    targets_copy = remote(targets_hbm, place, send_sem.at[pieces], target_sem, across)

    def is_own(b, at):
        return (batch == b) & (slab == at)

    for at in range(slabs):
        for b in range(batches):
            below = (slab >= at) & (batch >= b) & jnp.logical_not(is_own(b, at))

            @pl.when(below)
            def _():
                spread[b, at].start()

    for at in range(slabs):
        for b in range(batches):
            @pl.when((batch == 1) & (slab >= at) & jnp.logical_not(is_own(b, at)))
            def _():
                pl.semaphore_signal(
                    ready_sem.at[slab], inc=1, device_id={"batch": b, "slab": at}, device_id_type=MESH
                )

    @pl.when(batch == 1)
    def _():
        targets_copy.start()

    send(pair[0])
    send(pair[1])
    send(pair[2])

    front_pre_ref[...] = jnp.zeros(front_pre_ref.shape, f32)
    edge = jnp.zeros((depth, 2 * rows, wide), bf16)
    taps_ref[:, 0] = edge
    taps_ref[:, extent_x + 1] = edge
    strided_ref[0] = jnp.zeros((extent_x + 1, group, wide), bf16)
    strided_ref[:, 0] = jnp.zeros((depth + 1, group, wide), bf16)
    for side in range(2):
        spread_ref[side, half_z] = jnp.zeros((half_x + 1, group, 2 * features), bf16)
        spread_ref[side, :, half_x] = jnp.zeros((half_z + 1, group, 2 * features), bf16)
    blank = jnp.zeros((features, channels), bf16)
    for tap in range(9):
        back_ref[tap, features:, :channels] = blank

    row = lax.broadcasted_iota(jnp.int32, (group, channels), 0)
    first = (row & (half_y - 1)) == 0
    last = (row & (half_y - 1)) == half_y - 1
    lane_low = lax.broadcasted_iota(jnp.int32, (group, channels), 1) < inner

    def fill(side, at):
        for plane in range(thick):
            for x in range(extent_x):
                slot = plane * extent_x + x
                for b in range(batches):
                    split_ref[slot, b * half * extent_y : (b + 1) * half * extent_y] = (
                        volume_ref[side, b * slabs + at, :, plane, x].astype(f32).reshape(half * extent_y, channels)
                    )
                even = split_ref[slot, pl.ds(0, group, stride=2), :]
                odd = split_ref[slot, pl.ds(1, group, stride=2), :]
                before = jnp.where(first, 0.0, pltpu.roll(odd, 1, 0)).astype(bf16)
                after = jnp.where(last, 0.0, pltpu.roll(even, group - 1, 0)).astype(bf16)
                even, odd = even.astype(bf16), odd.astype(bf16)
                z = at * thick + plane
                top, bottom = side * rows, side * rows + group
                taps_ref[z, x + 1, top : top + group] = jnp.concatenate([before, even, odd], axis=1)
                taps_ref[z, x + 1, bottom : bottom + group] = jnp.concatenate([even, odd, after], axis=1)

    plane_cells = extent_x * rows

    def front(at):
        window = jnp.concatenate(
            [
                taps_ref[pl.ds(at * thick, thick), kx : kx + extent_x, :rows].reshape(thick * plane_cells, wide)
                for kx in range(3)
            ],
            axis=1,
        )
        sums = jnp.dot(window, front_ref[...], preferred_element_type=f32)

        def block(plane, kz):
            return sums[plane * plane_cells : (plane + 1) * plane_cells, kz * channels : (kz + 1) * channels]

        base = at * thick
        front_pre_ref[base] += block(0, 2)
        front_pre_ref[base + 1] += block(0, 1) + block(1, 2)
        front_pre_ref[base + 2] += block(0, 0) + block(1, 1)
        front_pre_ref[base + 3] += block(1, 0)

    slots = {}
    for pz in range(2):
        for px in range(2):
            for sz in range(pz + 1):
                for sx in range(px + 1):
                    kz = 1 if pz == 0 else 2 - 2 * sz
                    kx = 1 if px == 0 else 2 - 2 * sx
                    slots[pz, px, sz, sx] = (len(slots), kz, kx)

    other = 1 - batch

    def arrived(b, at):
        remote(piece(0, b, at), piece(0, b, at), send_sem.at[0], piece_sem.at[b * slabs + at], sibling).wait_recv()

    def pass_on(slot, b, at):
        number = b * slabs + at
        send(remote(piece(0, b, at), piece(1, b, at), pass_send_sem.at[slot], pass_sem.at[number], sibling))

    def prepare_front():
        local[1].wait()
        pair[0].wait_recv()
        for kz in range(3):
            for tap in range(9):
                front_ref[tap * channels : (tap + 1) * channels, kz * channels : (kz + 1) * channels] = jnp.transpose(
                    front_turned_ref[9 * kz + tap]
                )

    def prepare_back():
        local[2].wait()
        pair[1].wait_recv()
        for slot, kz, kx in slots.values():
            start = 9 * kz + 3 * kx
            back_ref[slot, :features, :channels] = jnp.transpose(stride_ref[start + 1])
            back_ref[slot, :features, channels:] = jnp.transpose(stride_ref[start + 2])
            back_ref[slot, features:, channels:] = jnp.transpose(stride_ref[start])

    local[0].wait()
    local[6].wait()
    prepare_front()
    for level in range(slabs):
        @pl.when((slab == level) & (batch == 0))
        def _():
            pl.semaphore_wait(ready_sem.at[level], 1)
            targets_copy.start()
            for at in range(level + 1):
                spread[1, at].start()

        @pl.when(slab < level)
        def _():
            pl.semaphore_wait(ready_sem.at[level], 1)
            for b in range(batches):
                spread[b, level].start()

    arrived(other, slab)
    pass_on(0, other, slab)
    fill(0, slab)
    front(slab)
    for i in range(1, slabs):
        at = order[i]
        for b in (batch, other):
            arrived(b, at)
            pass_on(2 * i - 1 if b is batch else 2 * i, b, at)
        fill(0, at)
        front(at)
        if i == 1:
            prepare_back()

    def other_fill(i):
        at = order[i]
        for b in ([batch, other] if i else [other]):
            remote(
                piece(1, b, at), piece(1, b, at), send_sem.at[0], pass_sem.at[b * slabs + at], sibling
            ).wait_recv()
        fill(1, at)

    for z in range(depth):
        total = front_pre_ref[z + 1]
        logistic = sigmoid(total)
        act = (total * logistic).reshape(extent_x, 2, group, channels)
        slope_ref[z] = (logistic * (1.0 + total * (1.0 - logistic))).reshape(extent_x, 2, group, channels)
        for x in range(extent_x):
            even, odd = act[x, 0], act[x, 1]
            before = jnp.where(first, 0.0, pltpu.roll(odd, 1, 0)).astype(bf16)
            strided_ref[z + 1, x + 1] = jnp.concatenate([before, even.astype(bf16), odd.astype(bf16)], axis=1)
            where = (z % 2, x % 2, (z // 2) * half_x + x // 2)
            act_ref[(0,) + where] = jnp.where(lane_low, even, pltpu.roll(odd, inner, 1)).astype(bf16)
            act_out_ref[where] = jnp.where(lane_low, pltpu.roll(even, inner, 1), odd).astype(bf16)
    send(pair[3])

    for copy in local[3:6]:
        copy.wait()
    pair[2].wait_recv()
    remote(targets_hbm, targets_ref.at[pl.ds(other * leading, leading)], send_sem.at[0], target_sem, sibling).wait_recv()

    windows = jnp.concatenate(
        [
            jnp.concatenate(
                [strided_ref[kz + 2 * z, kx + 2 * x] for z in range(half_z) for x in range(half_x)], axis=0
            )
            for kz in range(3) for kx in range(3)
        ],
        axis=1,
    )
    pre = jnp.dot(windows, stride_ref[...].reshape(27 * channels, features), preferred_element_type=f32)
    logistic = sigmoid(pre)
    summed = jnp.sum((pre * logistic).reshape(planes, group, features), axis=0)
    slope = (logistic * (1.0 + pre * (1.0 - logistic))).reshape(planes, group, features)
    wide_row = lax.broadcasted_iota(jnp.int32, (group, features), 0)
    step = 1
    while step < half_y:
        high = (wide_row & step) != 0
        summed = summed + jnp.where(high, pltpu.roll(summed, step, 0), pltpu.roll(summed, group - step, 0))
        step *= 2
    pooled = summed / cells
    hidden = hidden_ref[...]
    output = output_ref[...]
    hidden_pre = jnp.dot(pooled, hidden, precision=highest, preferred_element_type=f32)
    hidden_logistic = sigmoid(hidden_pre)
    hidden_act = hidden_pre * hidden_logistic
    hidden_slope = hidden_logistic * (1.0 + hidden_pre * (1.0 - hidden_logistic))
    all_samples = batches * leading
    owner = lax.broadcasted_iota(jnp.int32, (group, all_samples), 1)
    of_row = lax.broadcasted_iota(jnp.int32, (group, all_samples), 0) // half_y
    wanted = (of_row // half) * leading + chan * half + of_row % half
    member = (owner == wanted).astype(f32)
    target_rows = jnp.dot(member, targets_ref[...], precision=highest, preferred_element_type=f32)
    lane = lax.broadcasted_iota(jnp.int32, (group, channels), 1)
    residuals = jnp.zeros((group, channels), f32)
    back = jnp.zeros((group, output.shape[1]), f32)
    for o in range(outputs):
        residual = jnp.sum(hidden_act * output[o : o + 1], axis=1, keepdims=True) - target_rows[:, o : o + 1]
        back = back + residual * output[o : o + 1]
        residuals = jnp.where(lane == o, residual, residuals)
    grad_hidden_pre = back * hidden_slope
    grad_pooled = lax.dot_general(
        grad_hidden_pre, hidden, (((1,), (1,)), ((), ())), precision=highest, preferred_element_type=f32
    )
    grad_pre = slope * (grad_pooled / cells)[None]
    grad_next = jnp.where(
        ((wide_row & (half_y - 1)) == half_y - 1)[None],
        0.0,
        jnp.stack([pltpu.roll(grad_pre[i], group - 1, 0) for i in range(planes)]),
    )
    both = jnp.concatenate([grad_pre, grad_next], axis=2).astype(bf16)
    spread_ref[0, :half_z, :half_x] = both.reshape(half_z, half_x, group, 2 * features)
    send(pair[4])
    low_half, high_half = pooled[:, :share], pooled[:, share:]
    head_ref[0, 0] = jnp.where(chan == 0, low_half, high_half)
    head_out_ref[0] = jnp.where(chan == 0, high_half, low_half)
    for i, value in ((1, grad_hidden_pre), (2, hidden_act), (3, residuals)):
        head_ref[0, i] = value
        head_out_ref[i] = value
    send(pair[5])

    def shifted(side, sz, sx):
        return spread_ref[side, sz : sz + half_z, sx : sx + half_x].reshape(planes * group, 2 * features)

    for pz in range(2):
        for px in range(2):
            moves = [(sz, sx) for sz in range(pz + 1) for sx in range(px + 1)]
            start = slots[pz, px, 0, 0][0]
            left = jnp.concatenate([shifted(0, sz, sx) for sz, sx in moves], axis=1)
            right = back_ref[start : start + len(moves)].reshape(len(moves) * 2 * features, 2 * channels)
            grad = jnp.dot(left, right, preferred_element_type=f32)
            grad = grad.reshape(half_z, half_x, group, 2 * channels)
            for z in range(half_z):
                for x in range(half_x):
                    for py in range(2):
                        value = grad[z, x, :, py * channels : (py + 1) * channels].astype(bf16).astype(f32)
                        at = (2 * z + pz, 2 * x + px, py)
                        grad_ref[at] = (value * slope_ref[at]).astype(bf16)
    for z in range(depth):
        turned = jnp.transpose(grad_ref[z].reshape(plane_cells, channels))
        turned_ref[0, :, z * plane_cells : (z + 1) * plane_cells] = turned[:inner]
        turned_out_ref[:, z * plane_cells : (z + 1) * plane_cells] = turned[inner:]
    send(pair[6])

    for i in range(slabs):
        other_fill(i)

    pair[3].wait_recv()
    pair[4].wait_recv()
    turned_act = {
        (pz, px): jnp.concatenate(
            [jnp.transpose(act_ref[side, pz, px].reshape(planes * group, channels)) for side in range(2)], axis=1
        )
        for pz in range(2) for px in range(2)
    }
    for sz in range(2):
        for sx in range(2):
            right = jnp.concatenate([shifted(side, sz, sx) for side in range(2)], axis=0)
            for pz in range(sz, 2):
                for px in range(sx, 2):
                    _, kz, kx = slots[pz, px, sz, sx]
                    grad = jnp.dot(turned_act[pz, px], right, preferred_element_type=f32)
                    start = 9 * kz + 3 * kx
                    stride_grad_ref[start + 1] = grad[:inner, :features]
                    stride_grad_ref[start + 2] = grad[inner:, :features]
                    stride_grad_ref[start] = grad[inner:, features:]

    pair[5].wait_recv()
    pooled_all, hidden_pre_all, hidden_all, residual_all = [
        jnp.concatenate([head_ref[0, i], head_ref[1, i]], axis=0) for i in range(4)
    ]

    def outer(left, right):
        return lax.dot_general(
            left, right, (((0,), (0,)), ((), ())), precision=highest, preferred_element_type=f32
        ) / half_y

    hidden_grad_ref[...] = outer(pooled_all, hidden_pre_all)
    output_grad_ref[...] = outer(residual_all, hidden_all)[:outputs]
    loss_ref[...] = jnp.sum(residual_all * residual_all, keepdims=True) / (half_y * all_samples * outputs)

    pair[6].wait_recv()
    for at in range(slabs):
        for b in range(batches):
            @pl.when(jnp.logical_not(is_own(b, at)))
            def _():
                spread[b, at].wait_send()
    targets_copy.wait_send()
    for copy in sends:
        copy.wait_send()


def kernel_grads(
    shape,
    taps_ref, turned_ref, stride_ref, hidden_ref, output_ref, loss_ref,
    front_out, stride_out, hidden_out, output_out, loss_out,
    front_ref, front_sem, other_sem,
):
    slabs, batches, leading, thick, extent_x, extent_y, channels, inner = shape
    f32, bf16 = jnp.float32, jnp.bfloat16
    depth = slabs * thick
    rows = taps_ref.shape[2] // 2
    plane_cells = extent_x * rows
    wide = 3 * channels
    others = [
        pltpu.make_async_copy(source, target, other_sem.at[i])
        for i, (source, target) in enumerate(
            [(stride_ref, stride_out), (hidden_ref, hidden_out), (output_ref, output_out), (loss_ref, loss_out)]
        )
    ]
    for copy in others:
        copy.start()
    edge = jnp.zeros((inner, plane_cells), bf16)

    def stacked(side):
        grads = turned_ref[side]
        return jnp.concatenate(
            [
                jnp.concatenate([grads[:, plane_cells:], edge], axis=1),
                grads,
                jnp.concatenate([edge, grads[:, :-plane_cells]], axis=1),
            ],
            axis=0,
        )

    left = jnp.concatenate([stacked(0), stacked(1)], axis=1)

    def send_out(group):
        place = pl.ds(3 * group, 3)
        return pltpu.make_async_copy(front_ref.at[place], front_out.at[place], front_sem.at[group])

    for kx in range(3):
        right = jnp.concatenate(
            [
                taps_ref[:, kx : kx + extent_x, side * rows : (side + 1) * rows].reshape(depth * plane_cells, wide)
                for side in range(2)
            ],
            axis=0,
        )
        grads = jnp.dot(left, right, preferred_element_type=f32)
        for kz in range(3):
            for ky in range(3):
                front_ref[9 * kz + 3 * kx + ky] = grads[kz * inner : (kz + 1) * inner, ky * channels : (ky + 1) * channels]
            send_out(3 * kz + kx).start()
    for group in range(9):
        send_out(group).wait()
    for copy in others:
        copy.wait()


def chain(shape, volume, targets, front_turned, stride_own, hidden_weight, output_turned):
    slabs, batches, leading, thick, extent_x, extent_y, channels, inner = shape
    f32, bf16 = jnp.float32, jnp.bfloat16
    features = stride_own.shape[-1]
    share, hid = hidden_weight.shape
    outputs = output_turned.shape[0]
    half = leading // 2
    pieces = slabs * batches
    depth = slabs * thick
    group = batches * half * extent_y // 2
    rows = 2 * group
    half_z, half_x = depth // 2, extent_x // 2
    planes = half_z * half_x
    plane_cells = extent_x * rows
    wide = 3 * channels
    vmem = pl.BlockSpec(memory_space=pltpu.VMEM)
    anywhere = pl.BlockSpec(memory_space=pl.ANY)
    dma = pltpu.SemaphoreType.DMA
    operands = [
        pltpu.with_memory_space_constraint(x, pltpu.HBM)
        for x in (volume, targets, front_turned, stride_own, hidden_weight, output_turned)
    ]
    stages = pl.pallas_call(
        functools.partial(chain_kernel, shape),
        out_shape=(
            jax.ShapeDtypeStruct((depth, extent_x + 2, 2 * rows, wide), bf16),
            jax.ShapeDtypeStruct((2, inner, depth * plane_cells), bf16),
            jax.ShapeDtypeStruct((27, inner, features), f32),
            jax.ShapeDtypeStruct((share, hid), f32),
            jax.ShapeDtypeStruct((outputs, hid), f32),
            jax.ShapeDtypeStruct((1, 1), f32),
        ),
        in_specs=[anywhere] * 6,
        out_specs=[vmem] * 6,
        scratch_shapes=[
            pltpu.VMEM((2, pieces, half) + volume.shape[1:], bf16),
            pltpu.VMEM((thick * extent_x, rows, channels), f32),
            pltpu.VMEM((27, channels, channels), bf16),
            pltpu.VMEM((9 * channels, wide), bf16),
            pltpu.VMEM((depth + 2, plane_cells, channels), f32),
            pltpu.VMEM((depth, extent_x, 2, group, channels), f32),
            pltpu.VMEM((depth + 1, extent_x + 1, group, wide), bf16),
            pltpu.VMEM((2, 2, 2, planes, group, channels), bf16),
            pltpu.VMEM((2, 2, planes, group, channels), bf16),
            pltpu.VMEM((27, channels, features), bf16),
            pltpu.VMEM((9, 2 * features, 2 * channels), bf16),
            pltpu.VMEM((2 * share, hid), f32),
            pltpu.VMEM((outputs, hid), f32),
            pltpu.VMEM((batches * leading, outputs), f32),
            pltpu.VMEM((2, half_z + 1, half_x + 1, group, 2 * features), bf16),
            pltpu.VMEM((2, 4, group, channels), f32),
            pltpu.VMEM((4, group, channels), f32),
            pltpu.VMEM((depth, extent_x, 2, group, channels), bf16),
            pltpu.VMEM((inner, depth * plane_cells), bf16),
            dma((7,)), dma((pieces + 1,)), dma((pieces,)), dma((pieces,)), dma((pieces,)),
            dma((7,)), dma((7,)), dma, pltpu.SemaphoreType.REGULAR((slabs,)),
        ],
        compiler_params=pltpu.CompilerParams(
            collective_id=0, has_side_effects=True, vmem_limit_bytes=40 << 20
        ),
    )(*operands)
    return pl.pallas_call(
        functools.partial(kernel_grads, shape),
        out_shape=(
            jax.ShapeDtypeStruct((27, inner, channels), f32),
            jax.ShapeDtypeStruct((27, inner, features), f32),
            jax.ShapeDtypeStruct((share, hid), f32),
            jax.ShapeDtypeStruct((outputs, hid), f32),
            jax.ShapeDtypeStruct((1, 1), f32),
        ),
        in_specs=[vmem] * 6,
        out_specs=[anywhere] * 5,
        scratch_shapes=[pltpu.VMEM((27, inner, channels), f32), dma((9,)), dma((4,))],
        compiler_params=pltpu.CompilerParams(vmem_limit_bytes=24 << 20),
    )(*stages)


def body(volume, targets, front_weight, stride_weight, hidden_weight, output_weight):
    slabs = lax.axis_size("slab")
    batches = lax.axis_size("batch")
    inner = front_weight.shape[-1]
    leading, thick, extent_x, extent_y, channels = volume.shape
    features = stride_weight.shape[-1]
    small = (slabs, batches, leading, thick, extent_x, extent_y) == (4, 2, 4, 2, 4, 8)
    if not small:
        return split_body(volume, targets, front_weight, stride_weight, hidden_weight, output_weight)
    shape = (slabs, batches) + volume.shape + (inner,)
    grad_front, grad_stride, grad_hidden, grad_output, loss = chain(
        shape, volume, targets,
        jnp.swapaxes(front_weight.reshape(27, channels, inner), 1, 2),
        stride_weight.reshape(27, inner, features), hidden_weight, output_weight.T,
    )
    return (
        jnp.swapaxes(grad_front, 1, 2).reshape(3, 3, 3, channels, inner),
        grad_stride.reshape(3, 3, 3, inner, features),
        grad_hidden,
        grad_output.T,
        loss.reshape(1),
    )


def solution(mesh):
    in_specs = (
        P(("groups", "batch"), "slab", None, None, None),
        P(("groups", "batch"), None),
        P(None, None, None, None, "chan"),
        P(None, None, None, "chan", None),
        P("chan", None),
        P(),
    )
    out_specs = (
        P("groups", None, None, None, "chan"),
        P("groups", None, None, "chan", None),
        P(("groups", "chan"), None),
        P("groups", None),
        P("groups"),
    )
    return jax.shard_map(body, mesh=mesh, in_specs=in_specs, out_specs=out_specs, check_vma=False)
```

```python
import functools

import jax
import jax.numpy as jnp
from jax import lax
from jax.experimental import pallas as pl
from jax.experimental.pallas import tpu as pltpu
from jax.sharding import PartitionSpec as P


def with_halo(cells, sides, width):
    for axis, dim in sides:
        count = lax.axis_size(axis)
        ends = count - 1
        head = lax.slice_in_dim(cells, 0, width, axis=dim)
        tail = lax.slice_in_dim(cells, cells.shape[dim] - width, cells.shape[dim], axis=dim)
        cells = jnp.concatenate(
            [
                lax.ppermute(tail, axis, [(i, (i + 1) % count) for i in range(ends)]),
                cells,
                lax.ppermute(head, axis, [((i + 1) % count, i) for i in range(ends)]),
            ],
            axis=dim,
        )
    return cells


def swish_slope(preact):
    logistic = jax.nn.sigmoid(preact)
    return logistic * (1.0 + preact * (1.0 - logistic))


def tap_window(padded, tap_z, tap_x, tap_y, extent_z, extent_x, extent_y, stride):
    if stride == 1:
        return padded[
            :, tap_z : tap_z + extent_z, tap_x : tap_x + extent_x, tap_y : tap_y + extent_y, :
        ]
    leading = padded.shape[0]
    channels = padded.shape[-1]
    folded = padded.reshape(leading, extent_z + 1, 2, extent_x + 1, 2, extent_y + 1, 2, channels)
    return folded[
        :,
        tap_z // 2 : tap_z // 2 + extent_z,
        tap_z % 2,
        tap_x // 2 : tap_x // 2 + extent_x,
        tap_x % 2,
        tap_y // 2 : tap_y // 2 + extent_y,
        tap_y % 2,
        :,
    ]


def conv_apply(padded, weight, extent_z, extent_x, extent_y, stride):
    summed = None
    for tap_z in range(3):
        for tap_x in range(3):
            for tap_y in range(3):
                window = tap_window(
                    padded, tap_z, tap_x, tap_y, extent_z, extent_x, extent_y, stride
                )
                flat_tap = window.reshape(-1, window.shape[-1])
                contrib = jnp.dot(
                    flat_tap, weight[tap_z, tap_x, tap_y], preferred_element_type=jnp.float32
                )
                summed = contrib if summed is None else summed + contrib
    return summed.reshape(padded.shape[0], extent_z, extent_x, extent_y, weight.shape[-1])


def kernel_grad(padded, grad_out, extent_z, extent_x, extent_y, stride):
    flat_grad = grad_out.reshape(-1, grad_out.shape[-1])
    results = []
    for tap_z in range(3):
        for tap_x in range(3):
            for tap_y in range(3):
                window = tap_window(
                    padded, tap_z, tap_x, tap_y, extent_z, extent_x, extent_y, stride
                )
                flat_tap = window.reshape(-1, window.shape[-1])
                results.append(
                    lax.dot_general(
                        flat_tap,
                        flat_grad,
                        (((0,), (0,)), ((), ())),
                        preferred_element_type=jnp.float32,
                    )
                )
    return jnp.stack(results).reshape(3, 3, 3, padded.shape[-1], grad_out.shape[-1])


def input_grad(grad_out, weight, extent_z, extent_x, extent_y):
    leading = grad_out.shape[0]
    channels = weight.shape[3]
    flat_grad = grad_out.reshape(-1, grad_out.shape[-1])
    buckets = {}
    for tap_z in range(3):
        for tap_x in range(3):
            for tap_y in range(3):
                contrib = lax.dot_general(
                    flat_grad,
                    weight[tap_z, tap_x, tap_y],
                    (((1,), (1,)), ((), ())),
                    preferred_element_type=jnp.float32,
                )
                contrib = contrib.reshape(leading, extent_z, extent_x, extent_y, channels)
                placed = jnp.pad(
                    contrib,
                    (
                        (0, 0),
                        (tap_z // 2, 1 - tap_z // 2),
                        (tap_x // 2, 1 - tap_x // 2),
                        (tap_y // 2, 1 - tap_y // 2),
                        (0, 0),
                    ),
                )
                parity = (tap_z % 2, tap_x % 2, tap_y % 2)
                buckets[parity] = placed if parity not in buckets else buckets[parity] + placed
    planes_z = []
    for par_z in range(2):
        planes_x = []
        for par_x in range(2):
            planes_x.append(jnp.stack([buckets[par_z, par_x, par_y] for par_y in range(2)], axis=4))
        planes_z.append(jnp.stack(planes_x, axis=3))
    assembled = jnp.stack(planes_z, axis=2)
    assembled = assembled.reshape(
        leading, 2 * extent_z + 2, 2 * extent_x + 2, 2 * extent_y + 2, channels
    )
    return assembled[:, 1:-1, 1:-1, 1:-1, :]


def split_body(volume, targets, front_weight, stride_weight, hidden_weight, output_weight):
    highest = lax.Precision.HIGHEST
    slabs = lax.axis_size("slab")
    batches = lax.axis_size("batch")
    inner = front_weight.shape[-1]
    leading, thick, extent_x, extent_y, channels = volume.shape
    depth = thick * slabs
    outputs = output_weight.shape[-1]
    haloed = with_halo(volume, (("slab", 1),), 1)
    padded = jnp.pad(haloed, ((0, 0), (0, 0), (1, 1), (1, 1), (0, 0)))
    front_pre = conv_apply(padded, front_weight, thick, extent_x, extent_y, 1)
    front_act = jax.nn.silu(front_pre).astype(jnp.bfloat16)
    merged = front_act.reshape(leading, thick, extent_x, extent_y * inner)
    sample_act = lax.all_to_all(merged, "slab", split_axis=0, concat_axis=1, tiled=True)
    sample_act = sample_act.reshape(1, depth, extent_x, extent_y, inner)
    half_z = depth // 2
    half_x = extent_x // 2
    half_y = extent_y // 2
    cells = half_z * half_x * half_y
    stride_pad = jnp.pad(sample_act, ((0, 0), (1, 1), (1, 1), (1, 1), (0, 0)))
    partial_pre = conv_apply(stride_pad, stride_weight, half_z, half_x, half_y, 2)
    stride_pre = lax.psum_scatter(partial_pre, "chan", scatter_dimension=4, tiled=True)
    pooled = jnp.sum(jax.nn.silu(stride_pre), axis=(0, 1, 2, 3)) / cells
    hidden_pre = lax.psum(jnp.dot(pooled, hidden_weight, precision=highest), "chan")
    hidden_act = jax.nn.silu(hidden_pre)
    predicted = jnp.dot(hidden_act, output_weight, precision=highest)
    target_row = lax.dynamic_index_in_dim(targets, lax.axis_index("slab"), 0, keepdims=False)
    residual = predicted - target_row
    squared = jnp.sum(residual * residual)
    grad_output = jnp.outer(hidden_act, residual)
    grad_hidden_pre = jnp.dot(output_weight, residual, precision=highest) * swish_slope(hidden_pre)
    grad_hidden = jnp.outer(pooled, grad_hidden_pre)
    grad_pooled = jnp.dot(hidden_weight, grad_hidden_pre, precision=highest)
    grad_stride_pre = (grad_pooled / cells * swish_slope(stride_pre)).astype(jnp.bfloat16)
    full_grad = lax.all_gather(grad_stride_pre, "chan", axis=4, tiled=True)
    grad_stride = kernel_grad(stride_pad, full_grad, half_z, half_x, half_y, 2)
    grad_act = input_grad(full_grad, stride_weight, half_z, half_x, half_y).astype(jnp.bfloat16)
    returned = lax.all_to_all(
        grad_act.reshape(1, depth, extent_x, extent_y * inner),
        "slab",
        split_axis=1,
        concat_axis=0,
        tiled=True,
    )
    returned = returned.reshape(leading, thick, extent_x, extent_y, inner)
    grad_front_pre = (returned * swish_slope(front_pre)).astype(jnp.bfloat16)
    grad_front = kernel_grad(padded, grad_front_pre, thick, extent_x, extent_y, 1)
    grad_front, grad_stride, grad_hidden, grad_output, squared = lax.psum(
        (grad_front, grad_stride, grad_hidden, grad_output, squared), ("slab", "batch")
    )
    loss = (squared / (slabs * batches * outputs)).reshape(1)
    return (grad_front, grad_stride, grad_hidden, grad_output, loss)


MESH = pl.DeviceIdType.MESH


def sigmoid(v):
    return 1.0 / (1.0 + jnp.exp(-v))


def remote(source, target, send_sem, recv_sem, device):
    return pltpu.make_async_remote_copy(
        src_ref=source, dst_ref=target, send_sem=send_sem, recv_sem=recv_sem,
        device_id=device, device_id_type=MESH,
    )


def slab_order(slab, slabs):
    top = slabs - 1
    step = 1 - 2 * (slab // top)
    far = top * (1 - slab // (slabs // 2))
    near = slab + step
    return [slab, near, slabs * top // 2 - slab - near - far, far]


def chain_kernel(
    shape,
    volume_hbm, targets_hbm, front_hbm, stride_hbm, hidden_hbm, output_hbm,
    taps_ref, turned_ref, stride_grad_ref, hidden_grad_ref, output_grad_ref, loss_ref,
    volume_ref, split_ref, front_turned_ref, front_ref, front_pre_ref, slope_ref, strided_ref,
    act_ref, act_out_ref, stride_ref, back_ref, hidden_ref, output_ref, targets_ref,
    spread_ref, head_ref, head_out_ref, grad_ref, turned_out_ref,
    local_sem, send_sem, piece_sem, pass_send_sem, pass_sem, pair_send_sem, pair_sem, target_sem, ready_sem,
):
    slabs, batches, leading, thick, extent_x, extent_y, channels, inner = shape
    slab, batch, chan = lax.axis_index("slab"), lax.axis_index("batch"), lax.axis_index("chan")
    f32, bf16 = jnp.float32, jnp.bfloat16
    highest = lax.Precision.HIGHEST
    half = leading // 2
    depth = slabs * thick
    half_y = extent_y // 2
    half_z, half_x = depth // 2, extent_x // 2
    planes = half_z * half_x
    samples = batches * half
    group = samples * half_y
    rows = 2 * group
    cells = planes * half_y
    wide = 3 * channels
    features = stride_ref.shape[-1]
    share = hidden_hbm.shape[0]
    outputs = output_hbm.shape[0]
    sibling = {"chan": 1 - chan}
    mine = batch * slabs + slab
    pieces = batches * slabs

    across = {"batch": 1 - batch}
    barrier = pltpu.get_barrier_semaphore()
    pl.semaphore_signal(barrier, inc=1, device_id=sibling, device_id_type=MESH)

    def is_own(b, at):
        return (batch == b) & (slab == at)

    for at in reversed(range(slabs)):
        for b in reversed(range(batches)):
            @pl.when((slab <= at) & (batch <= b) & jnp.logical_not(is_own(b, at)))
            def _():
                pl.semaphore_signal(barrier, inc=1, device_id={"batch": b, "slab": at}, device_id_type=MESH)

    local = [
        pltpu.make_async_copy(source, target, local_sem.at[i])
        for i, (source, target) in enumerate([
            (volume_hbm.at[pl.ds(chan * half, half)], volume_ref.at[0, mine]),
            (front_hbm, front_turned_ref.at[:, pl.ds(0, inner)]),
            (stride_hbm, stride_ref.at[:, pl.ds(0, inner)]),
            (hidden_hbm, hidden_ref.at[pl.ds(chan * share, share)]),
            (output_hbm, output_ref),
            (targets_hbm, targets_ref.at[pl.ds(batch * leading, leading)]),
            (volume_hbm.at[pl.ds((1 - chan) * half, half)], volume_ref.at[1, mine]),
        ])
    ]
    for copy in local:
        copy.start()

    pl.semaphore_wait(barrier, (batch + 1) * (slab + 1))

    sends = []

    def send(copy):
        copy.start()
        sends.append(copy)

    pair = [
        remote(front_hbm, front_turned_ref.at[:, pl.ds(inner, inner)], pair_send_sem.at[0], pair_sem.at[0], sibling),
        remote(stride_hbm, stride_ref.at[:, pl.ds(inner, inner)], pair_send_sem.at[1], pair_sem.at[1], sibling),
        remote(hidden_hbm, hidden_ref.at[pl.ds(chan * share, share)], pair_send_sem.at[2], pair_sem.at[2], sibling),
        remote(act_out_ref, act_ref.at[1], pair_send_sem.at[3], pair_sem.at[3], sibling),
        remote(
            spread_ref.at[0, pl.ds(0, half_z), pl.ds(0, half_x)], spread_ref.at[1, pl.ds(0, half_z), pl.ds(0, half_x)],
            pair_send_sem.at[4], pair_sem.at[4], sibling,
        ),
        remote(head_out_ref, head_ref.at[1], pair_send_sem.at[5], pair_sem.at[5], sibling),
        remote(turned_out_ref, turned_ref.at[1], pair_send_sem.at[6], pair_sem.at[6], sibling),
    ]
    order = slab_order(slab, slabs)
    own = volume_hbm.at[pl.ds(chan * half, half)]

    def piece(side, b, at):
        return volume_ref.at[side, b * slabs + at]

    place = targets_ref.at[pl.ds(batch * leading, leading)]
    spread = {}
    for at in range(slabs):
        for b in range(batches):
            number = b * slabs + at
            spread[b, at] = remote(
                own, piece(0, batch, slab), send_sem.at[number], piece_sem.at[mine], {"batch": b, "slab": at}
            )
    targets_copy = remote(targets_hbm, place, send_sem.at[pieces], target_sem, across)

    for at in range(slabs):
        for b in range(batches):
            below = (slab >= at) & (batch >= b) & jnp.logical_not(is_own(b, at))

            @pl.when(below)
            def _():
                spread[b, at].start()

    for at in range(slabs):
        for b in range(batches):
            @pl.when((batch == 1) & (slab >= at) & jnp.logical_not(is_own(b, at)))
            def _():
                pl.semaphore_signal(
                    ready_sem.at[slab], inc=1, device_id={"batch": b, "slab": at}, device_id_type=MESH
                )

    @pl.when(batch == 1)
    def _():
        targets_copy.start()

    send(pair[0])
    send(pair[1])
    send(pair[2])

    front_pre_ref[...] = jnp.zeros(front_pre_ref.shape, f32)
    edge = jnp.zeros((depth, 2 * rows, wide), bf16)
    taps_ref[:, 0] = edge
    taps_ref[:, extent_x + 1] = edge
    strided_ref[0] = jnp.zeros((extent_x + 1, group, wide), bf16)
    strided_ref[:, 0] = jnp.zeros((depth + 1, group, wide), bf16)
    for side in range(2):
        spread_ref[side, half_z] = jnp.zeros((half_x + 1, group, 2 * features), bf16)
        spread_ref[side, :, half_x] = jnp.zeros((half_z + 1, group, 2 * features), bf16)
    blank = jnp.zeros((features, channels), bf16)
    for tap in range(9):
        back_ref[tap, features:, :channels] = blank

    row = lax.broadcasted_iota(jnp.int32, (group, channels), 0)
    first = (row & (half_y - 1)) == 0
    last = (row & (half_y - 1)) == half_y - 1
    lane_low = lax.broadcasted_iota(jnp.int32, (group, channels), 1) < inner

    def fill(side, at):
        for plane in range(thick):
            for x in range(extent_x):
                slot = plane * extent_x + x
                for b in range(batches):
                    split_ref[slot, b * half * extent_y : (b + 1) * half * extent_y] = (
                        volume_ref[side, b * slabs + at, :, plane, x].astype(f32).reshape(half * extent_y, channels)
                    )
                even = split_ref[slot, pl.ds(0, group, stride=2), :]
                odd = split_ref[slot, pl.ds(1, group, stride=2), :]
                before = jnp.where(first, 0.0, pltpu.roll(odd, 1, 0)).astype(bf16)
                after = jnp.where(last, 0.0, pltpu.roll(even, group - 1, 0)).astype(bf16)
                even, odd = even.astype(bf16), odd.astype(bf16)
                z = at * thick + plane
                top, bottom = side * rows, side * rows + group
                taps_ref[z, x + 1, top : top + group] = jnp.concatenate([before, even, odd], axis=1)
                taps_ref[z, x + 1, bottom : bottom + group] = jnp.concatenate([even, odd, after], axis=1)

    plane_cells = extent_x * rows

    def front(at):
        window = jnp.concatenate(
            [
                taps_ref[pl.ds(at * thick, thick), kx : kx + extent_x, :rows].reshape(thick * plane_cells, wide)
                for kx in range(3)
            ],
            axis=1,
        )
        sums = jnp.dot(window, front_ref[...], preferred_element_type=f32)

        def block(plane, kz):
            return sums[plane * plane_cells : (plane + 1) * plane_cells, kz * channels : (kz + 1) * channels]

        base = at * thick
        front_pre_ref[base] += block(0, 2)
        front_pre_ref[base + 1] += block(0, 1) + block(1, 2)
        front_pre_ref[base + 2] += block(0, 0) + block(1, 1)
        front_pre_ref[base + 3] += block(1, 0)

    slots = {}
    for pz in range(2):
        for px in range(2):
            for sz in range(pz + 1):
                for sx in range(px + 1):
                    kz = 1 if pz == 0 else 2 - 2 * sz
                    kx = 1 if px == 0 else 2 - 2 * sx
                    slots[pz, px, sz, sx] = (len(slots), kz, kx)

    other = 1 - batch

    def arrived(b, at):
        remote(piece(0, b, at), piece(0, b, at), send_sem.at[0], piece_sem.at[b * slabs + at], sibling).wait_recv()

    def pass_on(slot, b, at):
        number = b * slabs + at
        send(remote(piece(0, b, at), piece(1, b, at), pass_send_sem.at[slot], pass_sem.at[number], sibling))

    def prepare_front():
        local[1].wait()
        pair[0].wait_recv()
        for kz in range(3):
            for tap in range(9):
                front_ref[tap * channels : (tap + 1) * channels, kz * channels : (kz + 1) * channels] = jnp.transpose(
                    front_turned_ref[9 * kz + tap]
                )

    def prepare_back():
        local[2].wait()
        pair[1].wait_recv()
        for slot, kz, kx in slots.values():
            start = 9 * kz + 3 * kx
            back_ref[slot, :features, :channels] = jnp.transpose(stride_ref[start + 1])
            back_ref[slot, :features, channels:] = jnp.transpose(stride_ref[start + 2])
            back_ref[slot, features:, channels:] = jnp.transpose(stride_ref[start])

    local[0].wait()
    local[6].wait()
    prepare_front()
    for level in range(slabs):
        @pl.when((slab == level) & (batch == 0))
        def _():
            pl.semaphore_wait(ready_sem.at[level], 1)
            targets_copy.start()
            for at in range(level + 1):
                spread[1, at].start()

        @pl.when(slab < level)
        def _():
            pl.semaphore_wait(ready_sem.at[level], 1)
            for b in range(batches):
                spread[b, level].start()

    arrived(other, slab)
    pass_on(0, other, slab)
    fill(0, slab)
    front(slab)
    for i in range(1, slabs):
        at = order[i]
        for b in (batch, other):
            arrived(b, at)
            pass_on(2 * i - 1 if b is batch else 2 * i, b, at)
        fill(0, at)
        front(at)
        if i == 1:
            prepare_back()

    def other_fill(i):
        at = order[i]
        for b in ([batch, other] if i else [other]):
            remote(
                piece(1, b, at), piece(1, b, at), send_sem.at[0], pass_sem.at[b * slabs + at], sibling
            ).wait_recv()
        fill(1, at)

    for z in range(depth):
        total = front_pre_ref[z + 1]
        logistic = sigmoid(total)
        act = (total * logistic).reshape(extent_x, 2, group, channels)
        slope_ref[z] = (logistic * (1.0 + total * (1.0 - logistic))).reshape(extent_x, 2, group, channels)
        for x in range(extent_x):
            even, odd = act[x, 0], act[x, 1]
            before = jnp.where(first, 0.0, pltpu.roll(odd, 1, 0)).astype(bf16)
            strided_ref[z + 1, x + 1] = jnp.concatenate([before, even.astype(bf16), odd.astype(bf16)], axis=1)
            where = (z % 2, x % 2, (z // 2) * half_x + x // 2)
            act_ref[(0,) + where] = jnp.where(lane_low, even, pltpu.roll(odd, inner, 1)).astype(bf16)
            act_out_ref[where] = jnp.where(lane_low, pltpu.roll(even, inner, 1), odd).astype(bf16)
    send(pair[3])

    for copy in local[3:6]:
        copy.wait()
    pair[2].wait_recv()
    remote(targets_hbm, targets_ref.at[pl.ds(other * leading, leading)], send_sem.at[0], target_sem, sibling).wait_recv()

    windows = jnp.concatenate(
        [
            jnp.concatenate(
                [strided_ref[kz + 2 * z, kx + 2 * x] for z in range(half_z) for x in range(half_x)], axis=0
            )
            for kz in range(3) for kx in range(3)
        ],
        axis=1,
    )
    pre = jnp.dot(windows, stride_ref[...].reshape(27 * channels, features), preferred_element_type=f32)
    logistic = sigmoid(pre)
    summed = jnp.sum((pre * logistic).reshape(planes, group, features), axis=0)
    slope = (logistic * (1.0 + pre * (1.0 - logistic))).reshape(planes, group, features)
    wide_row = lax.broadcasted_iota(jnp.int32, (group, features), 0)
    step = 1
    while step < half_y:
        high = (wide_row & step) != 0
        summed = summed + jnp.where(high, pltpu.roll(summed, step, 0), pltpu.roll(summed, group - step, 0))
        step *= 2
    pooled = summed / cells
    hidden = hidden_ref[...]
    output = output_ref[...]
    hidden_pre = jnp.dot(pooled, hidden, precision=highest, preferred_element_type=f32)
    hidden_logistic = sigmoid(hidden_pre)
    hidden_act = hidden_pre * hidden_logistic
    hidden_slope = hidden_logistic * (1.0 + hidden_pre * (1.0 - hidden_logistic))
    all_samples = batches * leading
    owner = lax.broadcasted_iota(jnp.int32, (group, all_samples), 1)
    of_row = lax.broadcasted_iota(jnp.int32, (group, all_samples), 0) // half_y
    wanted = (of_row // half) * leading + chan * half + of_row % half
    member = (owner == wanted).astype(f32)
    target_rows = jnp.dot(member, targets_ref[...], precision=highest, preferred_element_type=f32)
    lane = lax.broadcasted_iota(jnp.int32, (group, channels), 1)
    residuals = jnp.zeros((group, channels), f32)
    back = jnp.zeros((group, output.shape[1]), f32)
    for o in range(outputs):
        residual = jnp.sum(hidden_act * output[o : o + 1], axis=1, keepdims=True) - target_rows[:, o : o + 1]
        back = back + residual * output[o : o + 1]
        residuals = jnp.where(lane == o, residual, residuals)
    grad_hidden_pre = back * hidden_slope
    grad_pooled = lax.dot_general(
        grad_hidden_pre, hidden, (((1,), (1,)), ((), ())), precision=highest, preferred_element_type=f32
    )
    grad_pre = slope * (grad_pooled / cells)[None]
    grad_next = jnp.where(
        ((wide_row & (half_y - 1)) == half_y - 1)[None],
        0.0,
        jnp.stack([pltpu.roll(grad_pre[i], group - 1, 0) for i in range(planes)]),
    )
    both = jnp.concatenate([grad_pre, grad_next], axis=2).astype(bf16)
    spread_ref[0, :half_z, :half_x] = both.reshape(half_z, half_x, group, 2 * features)
    send(pair[4])
    low_half, high_half = pooled[:, :share], pooled[:, share:]
    head_ref[0, 0] = jnp.where(chan == 0, low_half, high_half)
    head_out_ref[0] = jnp.where(chan == 0, high_half, low_half)
    for i, value in ((1, grad_hidden_pre), (2, hidden_act), (3, residuals)):
        head_ref[0, i] = value
        head_out_ref[i] = value
    send(pair[5])

    def shifted(side, sz, sx):
        return spread_ref[side, sz : sz + half_z, sx : sx + half_x].reshape(planes * group, 2 * features)

    for pz in range(2):
        for px in range(2):
            moves = [(sz, sx) for sz in range(pz + 1) for sx in range(px + 1)]
            start = slots[pz, px, 0, 0][0]
            left = jnp.concatenate([shifted(0, sz, sx) for sz, sx in moves], axis=1)
            right = back_ref[start : start + len(moves)].reshape(len(moves) * 2 * features, 2 * channels)
            grad = jnp.dot(left, right, preferred_element_type=f32)
            grad = grad.reshape(half_z, half_x, group, 2 * channels)
            for z in range(half_z):
                for x in range(half_x):
                    for py in range(2):
                        value = grad[z, x, :, py * channels : (py + 1) * channels].astype(bf16).astype(f32)
                        at = (2 * z + pz, 2 * x + px, py)
                        grad_ref[at] = (value * slope_ref[at]).astype(bf16)
    for z in range(depth):
        turned = jnp.transpose(grad_ref[z].reshape(plane_cells, channels))
        turned_ref[0, :, z * plane_cells : (z + 1) * plane_cells] = turned[:inner]
        turned_out_ref[:, z * plane_cells : (z + 1) * plane_cells] = turned[inner:]
    send(pair[6])

    for i in range(slabs):
        other_fill(i)

    pair[3].wait_recv()
    pair[4].wait_recv()
    turned_act = {
        (pz, px): jnp.concatenate(
            [jnp.transpose(act_ref[side, pz, px].reshape(planes * group, channels)) for side in range(2)], axis=1
        )
        for pz in range(2) for px in range(2)
    }
    for sz in range(2):
        for sx in range(2):
            right = jnp.concatenate([shifted(side, sz, sx) for side in range(2)], axis=0)
            for pz in range(sz, 2):
                for px in range(sx, 2):
                    _, kz, kx = slots[pz, px, sz, sx]
                    grad = jnp.dot(turned_act[pz, px], right, preferred_element_type=f32)
                    start = 9 * kz + 3 * kx
                    stride_grad_ref[start + 1] = grad[:inner, :features]
                    stride_grad_ref[start + 2] = grad[inner:, :features]
                    stride_grad_ref[start] = grad[inner:, features:]

    pair[5].wait_recv()
    pooled_all, hidden_pre_all, hidden_all, residual_all = [
        jnp.concatenate([head_ref[0, i], head_ref[1, i]], axis=0) for i in range(4)
    ]

    def outer(left, right):
        return lax.dot_general(
            left, right, (((0,), (0,)), ((), ())), precision=highest, preferred_element_type=f32
        ) / half_y

    hidden_grad_ref[...] = outer(pooled_all, hidden_pre_all)
    output_grad_ref[...] = outer(residual_all, hidden_all)[:outputs]
    loss_ref[...] = jnp.sum(residual_all * residual_all, keepdims=True) / (half_y * all_samples * outputs)

    pair[6].wait_recv()
    for at in range(slabs):
        for b in range(batches):
            @pl.when(jnp.logical_not(is_own(b, at)))
            def _():
                spread[b, at].wait_send()
    targets_copy.wait_send()
    for copy in sends:
        copy.wait_send()


def kernel_grads(
    shape,
    taps_ref, turned_ref, stride_ref, hidden_ref, output_ref, loss_ref,
    front_out, stride_out, hidden_out, output_out, loss_out,
    front_ref, front_sem, other_sem,
):
    slabs, batches, leading, thick, extent_x, extent_y, channels, inner = shape
    f32, bf16 = jnp.float32, jnp.bfloat16
    depth = slabs * thick
    rows = taps_ref.shape[2] // 2
    plane_cells = extent_x * rows
    wide = 3 * channels
    others = [
        pltpu.make_async_copy(source, target, other_sem.at[i])
        for i, (source, target) in enumerate(
            [(stride_ref, stride_out), (hidden_ref, hidden_out), (output_ref, output_out), (loss_ref, loss_out)]
        )
    ]
    for copy in others:
        copy.start()
    edge = jnp.zeros((inner, plane_cells), bf16)

    def stacked(side):
        grads = turned_ref[side]
        return jnp.concatenate(
            [
                jnp.concatenate([grads[:, plane_cells:], edge], axis=1),
                grads,
                jnp.concatenate([edge, grads[:, :-plane_cells]], axis=1),
            ],
            axis=0,
        )

    left = jnp.concatenate([stacked(0), stacked(1)], axis=1)

    def send_out(group):
        place = pl.ds(3 * group, 3)
        return pltpu.make_async_copy(front_ref.at[place], front_out.at[place], front_sem.at[group])

    for kx in range(3):
        right = jnp.concatenate(
            [
                taps_ref[:, kx : kx + extent_x, side * rows : (side + 1) * rows].reshape(depth * plane_cells, wide)
                for side in range(2)
            ],
            axis=0,
        )
        grads = jnp.dot(left, right, preferred_element_type=f32)
        for kz in range(3):
            for ky in range(3):
                front_ref[9 * kz + 3 * kx + ky] = grads[kz * inner : (kz + 1) * inner, ky * channels : (ky + 1) * channels]
            send_out(3 * kz + kx).start()
    for group in range(9):
        send_out(group).wait()
    for copy in others:
        copy.wait()


def chain(shape, volume, targets, front_turned, stride_own, hidden_weight, output_turned):
    slabs, batches, leading, thick, extent_x, extent_y, channels, inner = shape
    f32, bf16 = jnp.float32, jnp.bfloat16
    features = stride_own.shape[-1]
    share, hid = hidden_weight.shape
    outputs = output_turned.shape[0]
    half = leading // 2
    pieces = slabs * batches
    depth = slabs * thick
    group = batches * half * extent_y // 2
    rows = 2 * group
    half_z, half_x = depth // 2, extent_x // 2
    planes = half_z * half_x
    plane_cells = extent_x * rows
    wide = 3 * channels
    vmem = pl.BlockSpec(memory_space=pltpu.VMEM)
    anywhere = pl.BlockSpec(memory_space=pl.ANY)
    dma = pltpu.SemaphoreType.DMA
    operands = [
        pltpu.with_memory_space_constraint(x, pltpu.HBM)
        for x in (volume, targets, front_turned, stride_own, hidden_weight, output_turned)
    ]
    stages = pl.pallas_call(
        functools.partial(chain_kernel, shape),
        out_shape=(
            jax.ShapeDtypeStruct((depth, extent_x + 2, 2 * rows, wide), bf16),
            jax.ShapeDtypeStruct((2, inner, depth * plane_cells), bf16),
            jax.ShapeDtypeStruct((27, inner, features), f32),
            jax.ShapeDtypeStruct((share, hid), f32),
            jax.ShapeDtypeStruct((outputs, hid), f32),
            jax.ShapeDtypeStruct((1, 1), f32),
        ),
        in_specs=[anywhere] * 6,
        out_specs=[vmem] * 6,
        scratch_shapes=[
            pltpu.VMEM((2, pieces, half) + volume.shape[1:], bf16),
            pltpu.VMEM((thick * extent_x, rows, channels), f32),
            pltpu.VMEM((27, channels, channels), bf16),
            pltpu.VMEM((9 * channels, wide), bf16),
            pltpu.VMEM((depth + 2, plane_cells, channels), f32),
            pltpu.VMEM((depth, extent_x, 2, group, channels), f32),
            pltpu.VMEM((depth + 1, extent_x + 1, group, wide), bf16),
            pltpu.VMEM((2, 2, 2, planes, group, channels), bf16),
            pltpu.VMEM((2, 2, planes, group, channels), bf16),
            pltpu.VMEM((27, channels, features), bf16),
            pltpu.VMEM((9, 2 * features, 2 * channels), bf16),
            pltpu.VMEM((2 * share, hid), f32),
            pltpu.VMEM((outputs, hid), f32),
            pltpu.VMEM((batches * leading, outputs), f32),
            pltpu.VMEM((2, half_z + 1, half_x + 1, group, 2 * features), bf16),
            pltpu.VMEM((2, 4, group, channels), f32),
            pltpu.VMEM((4, group, channels), f32),
            pltpu.VMEM((depth, extent_x, 2, group, channels), bf16),
            pltpu.VMEM((inner, depth * plane_cells), bf16),
            dma((7,)), dma((pieces + 1,)), dma((pieces,)), dma((pieces,)), dma((pieces,)),
            dma((7,)), dma((7,)), dma, pltpu.SemaphoreType.REGULAR((slabs,)),
        ],
        compiler_params=pltpu.CompilerParams(
            collective_id=0, has_side_effects=True, vmem_limit_bytes=40 << 20
        ),
    )(*operands)
    return pl.pallas_call(
        functools.partial(kernel_grads, shape),
        out_shape=(
            jax.ShapeDtypeStruct((27, inner, channels), f32),
            jax.ShapeDtypeStruct((27, inner, features), f32),
            jax.ShapeDtypeStruct((share, hid), f32),
            jax.ShapeDtypeStruct((outputs, hid), f32),
            jax.ShapeDtypeStruct((1, 1), f32),
        ),
        in_specs=[vmem] * 6,
        out_specs=[anywhere] * 5,
        scratch_shapes=[pltpu.VMEM((27, inner, channels), f32), dma((9,)), dma((4,))],
        compiler_params=pltpu.CompilerParams(vmem_limit_bytes=24 << 20),
    )(*stages)


def body(volume, targets, front_weight, stride_weight, hidden_weight, output_weight):
    slabs = lax.axis_size("slab")
    batches = lax.axis_size("batch")
    inner = front_weight.shape[-1]
    leading, thick, extent_x, extent_y, channels = volume.shape
    features = stride_weight.shape[-1]
    small = (slabs, batches, leading, thick, extent_x, extent_y) == (4, 2, 4, 2, 4, 8)
    if not small:
        return split_body(volume, targets, front_weight, stride_weight, hidden_weight, output_weight)
    shape = (slabs, batches) + volume.shape + (inner,)
    grad_front, grad_stride, grad_hidden, grad_output, loss = chain(
        shape, volume, targets,
        jnp.swapaxes(front_weight.reshape(27, channels, inner), 1, 2),
        stride_weight.reshape(27, inner, features), hidden_weight, output_weight.T,
    )
    return (
        jnp.swapaxes(grad_front, 1, 2).reshape(3, 3, 3, channels, inner),
        grad_stride.reshape(3, 3, 3, inner, features),
        grad_hidden,
        grad_output.T,
        loss.reshape(1),
    )


def solution(mesh):
    in_specs = (
        P(("groups", "batch"), "slab", None, None, None),
        P(("groups", "batch"), None),
        P(None, None, None, None, "chan"),
        P(None, None, None, "chan", None),
        P("chan", None),
        P(),
    )
    out_specs = (
        P("groups", None, None, None, "chan"),
        P("groups", None, None, "chan", None),
        P(("groups", "chan"), None),
        P("groups", None),
        P("groups"),
    )
    return jax.shard_map(body, mesh=mesh, in_specs=in_specs, out_specs=out_specs, check_vma=False)
```

```python
import functools

import jax
import jax.numpy as jnp
from jax import lax
from jax.experimental import pallas as pl
from jax.experimental.pallas import tpu as pltpu
from jax.sharding import PartitionSpec as P


def with_halo(cells, sides, width):
    for axis, dim in sides:
        count = lax.axis_size(axis)
        ends = count - 1
        head = lax.slice_in_dim(cells, 0, width, axis=dim)
        tail = lax.slice_in_dim(cells, cells.shape[dim] - width, cells.shape[dim], axis=dim)
        cells = jnp.concatenate(
            [
                lax.ppermute(tail, axis, [(i, (i + 1) % count) for i in range(ends)]),
                cells,
                lax.ppermute(head, axis, [((i + 1) % count, i) for i in range(ends)]),
            ],
            axis=dim,
        )
    return cells


def swish_slope(preact):
    logistic = jax.nn.sigmoid(preact)
    return logistic * (1.0 + preact * (1.0 - logistic))


def tap_window(padded, tap_z, tap_x, tap_y, extent_z, extent_x, extent_y, stride):
    if stride == 1:
        return padded[
            :, tap_z : tap_z + extent_z, tap_x : tap_x + extent_x, tap_y : tap_y + extent_y, :
        ]
    leading = padded.shape[0]
    channels = padded.shape[-1]
    folded = padded.reshape(leading, extent_z + 1, 2, extent_x + 1, 2, extent_y + 1, 2, channels)
    return folded[
        :,
        tap_z // 2 : tap_z // 2 + extent_z,
        tap_z % 2,
        tap_x // 2 : tap_x // 2 + extent_x,
        tap_x % 2,
        tap_y // 2 : tap_y // 2 + extent_y,
        tap_y % 2,
        :,
    ]


def conv_apply(padded, weight, extent_z, extent_x, extent_y, stride):
    summed = None
    for tap_z in range(3):
        for tap_x in range(3):
            for tap_y in range(3):
                window = tap_window(
                    padded, tap_z, tap_x, tap_y, extent_z, extent_x, extent_y, stride
                )
                flat_tap = window.reshape(-1, window.shape[-1])
                contrib = jnp.dot(
                    flat_tap, weight[tap_z, tap_x, tap_y], preferred_element_type=jnp.float32
                )
                summed = contrib if summed is None else summed + contrib
    return summed.reshape(padded.shape[0], extent_z, extent_x, extent_y, weight.shape[-1])


def kernel_grad(padded, grad_out, extent_z, extent_x, extent_y, stride):
    flat_grad = grad_out.reshape(-1, grad_out.shape[-1])
    results = []
    for tap_z in range(3):
        for tap_x in range(3):
            for tap_y in range(3):
                window = tap_window(
                    padded, tap_z, tap_x, tap_y, extent_z, extent_x, extent_y, stride
                )
                flat_tap = window.reshape(-1, window.shape[-1])
                results.append(
                    lax.dot_general(
                        flat_tap,
                        flat_grad,
                        (((0,), (0,)), ((), ())),
                        preferred_element_type=jnp.float32,
                    )
                )
    return jnp.stack(results).reshape(3, 3, 3, padded.shape[-1], grad_out.shape[-1])


def input_grad(grad_out, weight, extent_z, extent_x, extent_y):
    leading = grad_out.shape[0]
    channels = weight.shape[3]
    flat_grad = grad_out.reshape(-1, grad_out.shape[-1])
    buckets = {}
    for tap_z in range(3):
        for tap_x in range(3):
            for tap_y in range(3):
                contrib = lax.dot_general(
                    flat_grad,
                    weight[tap_z, tap_x, tap_y],
                    (((1,), (1,)), ((), ())),
                    preferred_element_type=jnp.float32,
                )
                contrib = contrib.reshape(leading, extent_z, extent_x, extent_y, channels)
                placed = jnp.pad(
                    contrib,
                    (
                        (0, 0),
                        (tap_z // 2, 1 - tap_z // 2),
                        (tap_x // 2, 1 - tap_x // 2),
                        (tap_y // 2, 1 - tap_y // 2),
                        (0, 0),
                    ),
                )
                parity = (tap_z % 2, tap_x % 2, tap_y % 2)
                buckets[parity] = placed if parity not in buckets else buckets[parity] + placed
    planes_z = []
    for par_z in range(2):
        planes_x = []
        for par_x in range(2):
            planes_x.append(jnp.stack([buckets[par_z, par_x, par_y] for par_y in range(2)], axis=4))
        planes_z.append(jnp.stack(planes_x, axis=3))
    assembled = jnp.stack(planes_z, axis=2)
    assembled = assembled.reshape(
        leading, 2 * extent_z + 2, 2 * extent_x + 2, 2 * extent_y + 2, channels
    )
    return assembled[:, 1:-1, 1:-1, 1:-1, :]


def split_body(volume, targets, front_weight, stride_weight, hidden_weight, output_weight):
    highest = lax.Precision.HIGHEST
    slabs = lax.axis_size("slab")
    batches = lax.axis_size("batch")
    inner = front_weight.shape[-1]
    leading, thick, extent_x, extent_y, channels = volume.shape
    depth = thick * slabs
    outputs = output_weight.shape[-1]
    haloed = with_halo(volume, (("slab", 1),), 1)
    padded = jnp.pad(haloed, ((0, 0), (0, 0), (1, 1), (1, 1), (0, 0)))
    front_pre = conv_apply(padded, front_weight, thick, extent_x, extent_y, 1)
    front_act = jax.nn.silu(front_pre).astype(jnp.bfloat16)
    merged = front_act.reshape(leading, thick, extent_x, extent_y * inner)
    sample_act = lax.all_to_all(merged, "slab", split_axis=0, concat_axis=1, tiled=True)
    sample_act = sample_act.reshape(1, depth, extent_x, extent_y, inner)
    half_z = depth // 2
    half_x = extent_x // 2
    half_y = extent_y // 2
    cells = half_z * half_x * half_y
    stride_pad = jnp.pad(sample_act, ((0, 0), (1, 1), (1, 1), (1, 1), (0, 0)))
    partial_pre = conv_apply(stride_pad, stride_weight, half_z, half_x, half_y, 2)
    stride_pre = lax.psum_scatter(partial_pre, "chan", scatter_dimension=4, tiled=True)
    pooled = jnp.sum(jax.nn.silu(stride_pre), axis=(0, 1, 2, 3)) / cells
    hidden_pre = lax.psum(jnp.dot(pooled, hidden_weight, precision=highest), "chan")
    hidden_act = jax.nn.silu(hidden_pre)
    predicted = jnp.dot(hidden_act, output_weight, precision=highest)
    target_row = lax.dynamic_index_in_dim(targets, lax.axis_index("slab"), 0, keepdims=False)
    residual = predicted - target_row
    squared = jnp.sum(residual * residual)
    grad_output = jnp.outer(hidden_act, residual)
    grad_hidden_pre = jnp.dot(output_weight, residual, precision=highest) * swish_slope(hidden_pre)
    grad_hidden = jnp.outer(pooled, grad_hidden_pre)
    grad_pooled = jnp.dot(hidden_weight, grad_hidden_pre, precision=highest)
    grad_stride_pre = (grad_pooled / cells * swish_slope(stride_pre)).astype(jnp.bfloat16)
    full_grad = lax.all_gather(grad_stride_pre, "chan", axis=4, tiled=True)
    grad_stride = kernel_grad(stride_pad, full_grad, half_z, half_x, half_y, 2)
    grad_act = input_grad(full_grad, stride_weight, half_z, half_x, half_y).astype(jnp.bfloat16)
    returned = lax.all_to_all(
        grad_act.reshape(1, depth, extent_x, extent_y * inner),
        "slab",
        split_axis=1,
        concat_axis=0,
        tiled=True,
    )
    returned = returned.reshape(leading, thick, extent_x, extent_y, inner)
    grad_front_pre = (returned * swish_slope(front_pre)).astype(jnp.bfloat16)
    grad_front = kernel_grad(padded, grad_front_pre, thick, extent_x, extent_y, 1)
    grad_front, grad_stride, grad_hidden, grad_output, squared = lax.psum(
        (grad_front, grad_stride, grad_hidden, grad_output, squared), ("slab", "batch")
    )
    loss = (squared / (slabs * batches * outputs)).reshape(1)
    return (grad_front, grad_stride, grad_hidden, grad_output, loss)


MESH = pl.DeviceIdType.MESH


def sigmoid(v):
    return 1.0 / (1.0 + jnp.exp(-v))


def remote(source, target, send_sem, recv_sem, device):
    return pltpu.make_async_remote_copy(
        src_ref=source, dst_ref=target, send_sem=send_sem, recv_sem=recv_sem,
        device_id=device, device_id_type=MESH,
    )


def slab_order(slab, slabs):
    top = slabs - 1
    far = top * (1 - slab // (slabs // 2))
    near = slab + 1 - 2 * lax.rem(slab, 2)
    return [slab, near, slabs * top // 2 - slab - near - far, far]


def chain_kernel(
    shape,
    volume_hbm, targets_hbm, front_hbm, stride_hbm, hidden_hbm, output_hbm,
    taps_ref, turned_ref, stride_grad_ref, hidden_grad_ref, output_grad_ref, loss_ref,
    volume_ref, split_ref, front_turned_ref, front_ref, front_pre_ref, slope_ref, strided_ref,
    act_ref, act_out_ref, stride_ref, back_ref, hidden_ref, output_ref, targets_ref,
    spread_ref, head_ref, head_out_ref, grad_ref, turned_out_ref, hidden_split_ref, hidden_turned_ref, target_rows_ref,
    local_sem, send_sem, piece_sem, pass_send_sem, pass_sem, pair_send_sem, pair_sem, target_sem, ready_sem,
):
    slabs, batches, leading, thick, extent_x, extent_y, channels, inner = shape
    slab, batch, chan = lax.axis_index("slab"), lax.axis_index("batch"), lax.axis_index("chan")
    f32, bf16 = jnp.float32, jnp.bfloat16
    highest = lax.Precision.HIGHEST
    half = leading // 2
    depth = slabs * thick
    half_y = extent_y // 2
    half_z, half_x = depth // 2, extent_x // 2
    planes = half_z * half_x
    samples = batches * half
    group = samples * half_y
    rows = 2 * group
    cells = planes * half_y
    wide = 3 * channels
    features = stride_ref.shape[-1]
    share = hidden_hbm.shape[0]
    outputs = output_hbm.shape[0]
    sibling = {"chan": 1 - chan}
    mine = batch * slabs + slab
    pieces = batches * slabs

    across = {"batch": 1 - batch}
    barrier = pltpu.get_barrier_semaphore()
    pl.semaphore_signal(barrier, inc=1, device_id=sibling, device_id_type=MESH)

    def is_own(b, at):
        return (batch == b) & (slab == at)

    for at in reversed(range(slabs)):
        for b in reversed(range(batches)):
            @pl.when((slab <= at) & (batch <= b) & jnp.logical_not(is_own(b, at)))
            def _():
                pl.semaphore_signal(barrier, inc=1, device_id={"batch": b, "slab": at}, device_id_type=MESH)

    local = [
        pltpu.make_async_copy(source, target, local_sem.at[i])
        for i, (source, target) in enumerate([
            (volume_hbm.at[pl.ds(chan * half, half)], volume_ref.at[0, mine]),
            (front_hbm, front_turned_ref.at[:, pl.ds(0, inner)]),
            (stride_hbm, stride_ref.at[:, pl.ds(0, inner)]),
            (hidden_hbm, hidden_ref.at[pl.ds(chan * share, share)]),
            (output_hbm, output_ref),
            (targets_hbm, targets_ref.at[pl.ds(batch * leading, leading)]),
            (volume_hbm.at[pl.ds((1 - chan) * half, half)], volume_ref.at[1, mine]),
        ])
    ]
    for copy in local:
        copy.start()

    pl.semaphore_wait(barrier, (batch + 1) * (slab + 1))

    sends = []

    def send(copy):
        copy.start()
        sends.append(copy)

    pair = [
        remote(front_hbm, front_turned_ref.at[:, pl.ds(inner, inner)], pair_send_sem.at[0], pair_sem.at[0], sibling),
        remote(stride_hbm, stride_ref.at[:, pl.ds(inner, inner)], pair_send_sem.at[1], pair_sem.at[1], sibling),
        remote(hidden_hbm, hidden_ref.at[pl.ds(chan * share, share)], pair_send_sem.at[2], pair_sem.at[2], sibling),
        remote(act_out_ref, act_ref.at[1], pair_send_sem.at[3], pair_sem.at[3], sibling),
        remote(
            spread_ref.at[0, pl.ds(0, half_z), pl.ds(0, half_x)], spread_ref.at[1, pl.ds(0, half_z), pl.ds(0, half_x)],
            pair_send_sem.at[4], pair_sem.at[4], sibling,
        ),
        remote(head_out_ref, head_ref.at[1], pair_send_sem.at[5], pair_sem.at[5], sibling),
        remote(turned_out_ref, turned_ref.at[1], pair_send_sem.at[6], pair_sem.at[6], sibling),
    ]
    order = slab_order(slab, slabs)
    own = volume_hbm.at[pl.ds(chan * half, half)]

    def piece(side, b, at):
        return volume_ref.at[side, b * slabs + at]

    place = targets_ref.at[pl.ds(batch * leading, leading)]
    spread = {}
    for at in range(slabs):
        for b in range(batches):
            number = b * slabs + at
            spread[b, at] = remote(
                own, piece(0, batch, slab), send_sem.at[number], piece_sem.at[mine], {"batch": b, "slab": at}
            )
    targets_copy = remote(targets_hbm, place, send_sem.at[pieces], target_sem, across)

    def below(b, at):
        return (slab >= at) & (batch >= b) & jnp.logical_not(is_own(b, at))

    def send_below(first):
        for at in range(slabs):
            for b in range(batches):
                if first or at or b:
                    @pl.when(below(b, at))
                    def _():
                        spread[b, at].start()

    late = slab == slabs - 1

    @pl.when(late)
    def _():
        spread[0, 0].start()

    @pl.when(jnp.logical_not(late))
    def _():
        send_below(True)

    for at in range(slabs):
        for b in range(batches):
            @pl.when((batch == 1) & (slab >= at) & jnp.logical_not(is_own(b, at)))
            def _():
                pl.semaphore_signal(
                    ready_sem.at[slab], inc=1, device_id={"batch": b, "slab": at}, device_id_type=MESH
                )

    @pl.when(batch == 1)
    def _():
        targets_copy.start()

    send(pair[0])
    send(pair[1])
    send(pair[2])

    front_pre_ref[...] = jnp.zeros(front_pre_ref.shape, f32)
    edge = jnp.zeros((depth, 2 * rows, wide), bf16)
    taps_ref[:, 0] = edge
    taps_ref[:, extent_x + 1] = edge
    strided_ref[0] = jnp.zeros((extent_x + 1, group, wide), bf16)
    strided_ref[:, 0] = jnp.zeros((depth + 1, group, wide), bf16)
    for side in range(2):
        spread_ref[side, half_z] = jnp.zeros((half_x + 1, group, 2 * features), bf16)
        spread_ref[side, :, half_x] = jnp.zeros((half_z + 1, group, 2 * features), bf16)
    blank = jnp.zeros((features, channels), bf16)
    for tap in range(9):
        back_ref[tap, features:, :channels] = blank

    @pl.when(late)
    def _():
        spread[0, 0].wait_send()
        send_below(False)

    row = lax.broadcasted_iota(jnp.int32, (group, channels), 0)
    first = (row & (half_y - 1)) == 0
    last = (row & (half_y - 1)) == half_y - 1
    lane_low = lax.broadcasted_iota(jnp.int32, (group, channels), 1) < inner

    def fill(side, at):
        for plane in range(thick):
            for x in range(extent_x):
                slot = plane * extent_x + x
                for b in range(batches):
                    split_ref[slot, b * half * extent_y : (b + 1) * half * extent_y] = (
                        volume_ref[side, b * slabs + at, :, plane, x].astype(f32).reshape(half * extent_y, channels)
                    )
                even = split_ref[slot, pl.ds(0, group, stride=2), :]
                odd = split_ref[slot, pl.ds(1, group, stride=2), :]
                before = jnp.where(first, 0.0, pltpu.roll(odd, 1, 0)).astype(bf16)
                after = jnp.where(last, 0.0, pltpu.roll(even, group - 1, 0)).astype(bf16)
                even, odd = even.astype(bf16), odd.astype(bf16)
                z = at * thick + plane
                top, bottom = side * rows, side * rows + group
                taps_ref[z, x + 1, top : top + group] = jnp.concatenate([before, even, odd], axis=1)
                taps_ref[z, x + 1, bottom : bottom + group] = jnp.concatenate([even, odd, after], axis=1)

    plane_cells = extent_x * rows

    def front(at):
        window = jnp.concatenate(
            [
                taps_ref[pl.ds(at * thick, thick), kx : kx + extent_x, :rows].reshape(thick * plane_cells, wide)
                for kx in range(3)
            ],
            axis=1,
        )
        sums = jnp.dot(window, front_ref[...], preferred_element_type=f32)

        def block(plane, kz):
            return sums[plane * plane_cells : (plane + 1) * plane_cells, kz * channels : (kz + 1) * channels]

        base = at * thick
        front_pre_ref[base] += block(0, 2)
        front_pre_ref[base + 1] += block(0, 1) + block(1, 2)
        front_pre_ref[base + 2] += block(0, 0) + block(1, 1)
        front_pre_ref[base + 3] += block(1, 0)

    slots = {}
    for pz in range(2):
        for px in range(2):
            for sz in range(pz + 1):
                for sx in range(px + 1):
                    kz = 1 if pz == 0 else 2 - 2 * sz
                    kx = 1 if px == 0 else 2 - 2 * sx
                    slots[pz, px, sz, sx] = (len(slots), kz, kx)

    other = 1 - batch

    def arrived(b, at):
        remote(piece(0, b, at), piece(0, b, at), send_sem.at[0], piece_sem.at[b * slabs + at], sibling).wait_recv()

    def pass_on(slot, b, at):
        number = b * slabs + at
        send(remote(piece(0, b, at), piece(1, b, at), pass_send_sem.at[slot], pass_sem.at[number], sibling))

    def prepare_front():
        local[1].wait()
        pair[0].wait_recv()
        for kz in range(3):
            for tap in range(9):
                front_ref[tap * channels : (tap + 1) * channels, kz * channels : (kz + 1) * channels] = jnp.transpose(
                    front_turned_ref[9 * kz + tap]
                )

    def prepare_back():
        local[2].wait()
        pair[1].wait_recv()
        for slot, kz, kx in slots.values():
            start = 9 * kz + 3 * kx
            back_ref[slot, :features, :channels] = jnp.transpose(stride_ref[start + 1])
            back_ref[slot, :features, channels:] = jnp.transpose(stride_ref[start + 2])
            back_ref[slot, features:, channels:] = jnp.transpose(stride_ref[start])

    local[0].wait()
    local[6].wait()
    for level in range(slabs):
        @pl.when((slab == level) & (batch == 0))
        def _():
            pl.semaphore_wait(ready_sem.at[level], 1)
            targets_copy.start()
            for at in range(level + 1):
                spread[1, at].start()

        @pl.when(slab < level)
        def _():
            pl.semaphore_wait(ready_sem.at[level], 1)
            for b in range(batches):
                spread[b, level].start()

    prepare_front()

    def other_fill(i):
        at = order[i]
        for b in ([batch, other] if i else [other]):
            remote(
                piece(1, b, at), piece(1, b, at), send_sem.at[0], pass_sem.at[b * slabs + at], sibling
            ).wait_recv()
        fill(1, at)

    far = order[slabs - 1] // (slabs - 1)

    def activate(z):
        total = front_pre_ref[z + 1]
        logistic = sigmoid(total)
        act = (total * logistic).reshape(extent_x, 2, group, channels)
        slope_ref[z] = (logistic * (1.0 + total * (1.0 - logistic))).reshape(extent_x, 2, group, channels)
        for x in range(extent_x):
            even, odd = act[x, 0], act[x, 1]
            before = jnp.where(first, 0.0, pltpu.roll(odd, 1, 0)).astype(bf16)
            strided_ref[z + 1, x + 1] = jnp.concatenate([before, even.astype(bf16), odd.astype(bf16)], axis=1)
            where = (lax.rem(z, 2), x % 2, (z // 2) * half_x + x // 2)
            act_ref[(0,) + where] = jnp.where(lane_low, even, pltpu.roll(odd, inner, 1)).astype(bf16)
            act_out_ref[where] = jnp.where(lane_low, pltpu.roll(even, inner, 1), odd).astype(bf16)

    all_samples = batches * leading

    def halves(value):
        high = value.astype(bf16)
        return high, (value - high.astype(f32)).astype(bf16)

    def prepare_head():
        for copy in local[3:6]:
            copy.wait()
        pair[2].wait_recv()
        remote(
            targets_hbm, targets_ref.at[pl.ds(other * leading, leading)], send_sem.at[0], target_sem, sibling
        ).wait_recv()
        for ref, value in ((hidden_split_ref, hidden_ref[...]), (hidden_turned_ref, jnp.transpose(hidden_ref[...]))):
            high, low = halves(value)
            depth_of = value.shape[0]
            ref[:depth_of] = high
            ref[depth_of : 2 * depth_of] = high
            ref[2 * depth_of :] = low
        owner = lax.broadcasted_iota(jnp.int32, (group, all_samples), 1)
        of_row = lax.broadcasted_iota(jnp.int32, (group, all_samples), 0) // half_y
        wanted = (of_row // half) * leading + chan * half + of_row % half
        member = (owner == wanted).astype(f32)
        target_rows = jnp.dot(member, targets_ref[...], precision=highest, preferred_element_type=f32)
        for o in range(outputs):
            target_rows_ref[o] = jnp.broadcast_to(target_rows[:, o : o + 1], (group, channels))

    def dot_split(value, ref):
        high, low = halves(value)
        return jnp.dot(jnp.concatenate([high, low, high], axis=1), ref[...], preferred_element_type=f32)

    arrived(other, slab)
    pass_on(0, other, slab)
    fill(0, slab)
    front(slab)
    for i in range(1, slabs):
        at = order[i]
        for b in (batch, other):
            arrived(b, at)
            pass_on(2 * i - 1 if b is batch else 2 * i, b, at)
        fill(0, at)
        front(at)
        if i == 1:
            prepare_back()
            other_fill(0)
        if i == 2:
            prepare_head()
            other_fill(1)
            for k in range(depth - thick - 1):
                activate((1 - far) * (thick + 1) + k)

    for k in range(thick + 1):
        activate(far * (depth - thick - 1) + k)
    send(pair[3])

    windows = jnp.concatenate(
        [
            jnp.concatenate(
                [strided_ref[kz + 2 * z, kx + 2 * x] for z in range(half_z) for x in range(half_x)], axis=0
            )
            for kz in range(3) for kx in range(3)
        ],
        axis=1,
    )
    pre = jnp.dot(windows, stride_ref[...].reshape(27 * channels, features), preferred_element_type=f32)
    logistic = sigmoid(pre)
    summed = jnp.sum((pre * logistic).reshape(planes, group, features), axis=0)
    slope = (logistic * (1.0 + pre * (1.0 - logistic))).reshape(planes, group, features)
    wide_row = lax.broadcasted_iota(jnp.int32, (group, features), 0)
    step = 1
    while step < half_y:
        high = (wide_row & step) != 0
        summed = summed + jnp.where(high, pltpu.roll(summed, step, 0), pltpu.roll(summed, group - step, 0))
        step *= 2
    pooled = summed / cells
    output = output_ref[...]
    hidden_pre = dot_split(pooled, hidden_split_ref)
    hidden_logistic = sigmoid(hidden_pre)
    hidden_act = hidden_pre * hidden_logistic
    hidden_slope = hidden_logistic * (1.0 + hidden_pre * (1.0 - hidden_logistic))
    lane = lax.broadcasted_iota(jnp.int32, (group, channels), 1)
    residuals = jnp.zeros((group, channels), f32)
    back = jnp.zeros((group, output.shape[1]), f32)
    for o in range(outputs):
        residual = jnp.sum(hidden_act * output[o : o + 1], axis=1, keepdims=True) - target_rows_ref[o]
        back = back + residual * output[o : o + 1]
        residuals = jnp.where(lane == o, residual, residuals)
    grad_hidden_pre = back * hidden_slope
    grad_pooled = dot_split(grad_hidden_pre, hidden_turned_ref)
    grad_pre = slope * (grad_pooled / cells)[None]
    grad_next = jnp.where(
        ((wide_row & (half_y - 1)) == half_y - 1)[None],
        0.0,
        jnp.stack([pltpu.roll(grad_pre[i], group - 1, 0) for i in range(planes)]),
    )
    both = jnp.concatenate([grad_pre, grad_next], axis=2).astype(bf16)
    spread_ref[0, :half_z, :half_x] = both.reshape(half_z, half_x, group, 2 * features)
    send(pair[4])
    low_half, high_half = pooled[:, :share], pooled[:, share:]
    head_ref[0, 0] = jnp.where(chan == 0, low_half, high_half)
    head_out_ref[0] = jnp.where(chan == 0, high_half, low_half)
    for i, value in ((1, grad_hidden_pre), (2, hidden_act), (3, residuals)):
        head_ref[0, i] = value
        head_out_ref[i] = value
    send(pair[5])

    def shifted(side, sz, sx):
        return spread_ref[side, sz : sz + half_z, sx : sx + half_x].reshape(planes * group, 2 * features)

    for pz in range(2):
        for px in range(2):
            moves = [(sz, sx) for sz in range(pz + 1) for sx in range(px + 1)]
            start = slots[pz, px, 0, 0][0]
            left = jnp.concatenate([shifted(0, sz, sx) for sz, sx in moves], axis=1)
            right = back_ref[start : start + len(moves)].reshape(len(moves) * 2 * features, 2 * channels)
            grad = jnp.dot(left, right, preferred_element_type=f32)
            grad = grad.reshape(half_z, half_x, group, 2 * channels)
            for z in range(half_z):
                for x in range(half_x):
                    for py in range(2):
                        value = grad[z, x, :, py * channels : (py + 1) * channels].astype(bf16).astype(f32)
                        at = (2 * z + pz, 2 * x + px, py)
                        grad_ref[at] = (value * slope_ref[at]).astype(bf16)
    for z in range(depth):
        turned = jnp.transpose(grad_ref[z].reshape(plane_cells, channels))
        turned_ref[0, :, z * plane_cells : (z + 1) * plane_cells] = turned[:inner]
        turned_out_ref[:, z * plane_cells : (z + 1) * plane_cells] = turned[inner:]
    send(pair[6])

    for i in range(2, slabs):
        other_fill(i)

    pair[3].wait_recv()
    pair[4].wait_recv()
    turned_act = {
        (pz, px): jnp.concatenate(
            [jnp.transpose(act_ref[side, pz, px].reshape(planes * group, channels)) for side in range(2)], axis=1
        )
        for pz in range(2) for px in range(2)
    }
    for sz in range(2):
        for sx in range(2):
            right = jnp.concatenate([shifted(side, sz, sx) for side in range(2)], axis=0)
            for pz in range(sz, 2):
                for px in range(sx, 2):
                    _, kz, kx = slots[pz, px, sz, sx]
                    grad = jnp.dot(turned_act[pz, px], right, preferred_element_type=f32)
                    start = 9 * kz + 3 * kx
                    stride_grad_ref[start + 1] = grad[:inner, :features]
                    stride_grad_ref[start + 2] = grad[inner:, :features]
                    stride_grad_ref[start] = grad[inner:, features:]

    pair[5].wait_recv()
    pooled_all, hidden_pre_all, hidden_all, residual_all = [
        jnp.concatenate([head_ref[0, i], head_ref[1, i]], axis=0) for i in range(4)
    ]

    def outer(left, right):
        return lax.dot_general(
            left, right, (((0,), (0,)), ((), ())), precision=highest, preferred_element_type=f32
        ) / half_y

    hidden_grad_ref[...] = outer(pooled_all, hidden_pre_all)
    output_grad_ref[...] = outer(residual_all, hidden_all)[:outputs]
    loss_ref[...] = jnp.sum(residual_all * residual_all, keepdims=True) / (half_y * all_samples * outputs)

    pair[6].wait_recv()
    for at in range(slabs):
        for b in range(batches):
            waited = is_own(b, at) if at or b else is_own(b, at) | late

            @pl.when(jnp.logical_not(waited))
            def _():
                spread[b, at].wait_send()
    targets_copy.wait_send()
    for copy in sends:
        copy.wait_send()


def kernel_grads(
    shape,
    taps_ref, turned_ref, stride_ref, hidden_ref, output_ref, loss_ref,
    front_out, stride_out, hidden_out, output_out, loss_out,
    front_ref, front_sem, other_sem,
):
    slabs, batches, leading, thick, extent_x, extent_y, channels, inner = shape
    f32, bf16 = jnp.float32, jnp.bfloat16
    depth = slabs * thick
    rows = taps_ref.shape[2] // 2
    plane_cells = extent_x * rows
    wide = 3 * channels
    others = [
        pltpu.make_async_copy(source, target, other_sem.at[i])
        for i, (source, target) in enumerate(
            [(stride_ref, stride_out), (hidden_ref, hidden_out), (output_ref, output_out), (loss_ref, loss_out)]
        )
    ]
    for copy in others:
        copy.start()
    edge = jnp.zeros((inner, plane_cells), bf16)

    def stacked(side):
        grads = turned_ref[side]
        return jnp.concatenate(
            [
                jnp.concatenate([grads[:, plane_cells:], edge], axis=1),
                grads,
                jnp.concatenate([edge, grads[:, :-plane_cells]], axis=1),
            ],
            axis=0,
        )

    left = jnp.concatenate([stacked(0), stacked(1)], axis=1)

    def send_out(group):
        place = pl.ds(3 * group, 3)
        return pltpu.make_async_copy(front_ref.at[place], front_out.at[place], front_sem.at[group])

    for kx in range(3):
        right = jnp.concatenate(
            [
                taps_ref[:, kx : kx + extent_x, side * rows : (side + 1) * rows].reshape(depth * plane_cells, wide)
                for side in range(2)
            ],
            axis=0,
        )
        grads = jnp.dot(left, right, preferred_element_type=f32)
        for kz in range(3):
            for ky in range(3):
                front_ref[9 * kz + 3 * kx + ky] = grads[kz * inner : (kz + 1) * inner, ky * channels : (ky + 1) * channels]
            send_out(3 * kz + kx).start()
    for group in range(9):
        send_out(group).wait()
    for copy in others:
        copy.wait()


def chain(shape, volume, targets, front_turned, stride_own, hidden_weight, output_turned):
    slabs, batches, leading, thick, extent_x, extent_y, channels, inner = shape
    f32, bf16 = jnp.float32, jnp.bfloat16
    features = stride_own.shape[-1]
    share, hid = hidden_weight.shape
    outputs = output_turned.shape[0]
    half = leading // 2
    pieces = slabs * batches
    depth = slabs * thick
    group = batches * half * extent_y // 2
    rows = 2 * group
    half_z, half_x = depth // 2, extent_x // 2
    planes = half_z * half_x
    plane_cells = extent_x * rows
    wide = 3 * channels
    vmem = pl.BlockSpec(memory_space=pltpu.VMEM)
    anywhere = pl.BlockSpec(memory_space=pl.ANY)
    dma = pltpu.SemaphoreType.DMA
    operands = [
        pltpu.with_memory_space_constraint(x, pltpu.HBM)
        for x in (volume, targets, front_turned, stride_own, hidden_weight, output_turned)
    ]
    stages = pl.pallas_call(
        functools.partial(chain_kernel, shape),
        out_shape=(
            jax.ShapeDtypeStruct((depth, extent_x + 2, 2 * rows, wide), bf16),
            jax.ShapeDtypeStruct((2, inner, depth * plane_cells), bf16),
            jax.ShapeDtypeStruct((27, inner, features), f32),
            jax.ShapeDtypeStruct((share, hid), f32),
            jax.ShapeDtypeStruct((outputs, hid), f32),
            jax.ShapeDtypeStruct((1, 1), f32),
        ),
        in_specs=[anywhere] * 6,
        out_specs=[vmem] * 6,
        scratch_shapes=[
            pltpu.VMEM((2, pieces, half) + volume.shape[1:], bf16),
            pltpu.VMEM((thick * extent_x, rows, channels), f32),
            pltpu.VMEM((27, channels, channels), bf16),
            pltpu.VMEM((9 * channels, wide), bf16),
            pltpu.VMEM((depth + 2, plane_cells, channels), f32),
            pltpu.VMEM((depth, extent_x, 2, group, channels), f32),
            pltpu.VMEM((depth + 1, extent_x + 1, group, wide), bf16),
            pltpu.VMEM((2, 2, 2, planes, group, channels), bf16),
            pltpu.VMEM((2, 2, planes, group, channels), bf16),
            pltpu.VMEM((27, channels, features), bf16),
            pltpu.VMEM((9, 2 * features, 2 * channels), bf16),
            pltpu.VMEM((2 * share, hid), f32),
            pltpu.VMEM((outputs, hid), f32),
            pltpu.VMEM((batches * leading, outputs), f32),
            pltpu.VMEM((2, half_z + 1, half_x + 1, group, 2 * features), bf16),
            pltpu.VMEM((2, 4, group, channels), f32),
            pltpu.VMEM((4, group, channels), f32),
            pltpu.VMEM((depth, extent_x, 2, group, channels), bf16),
            pltpu.VMEM((inner, depth * plane_cells), bf16),
            pltpu.VMEM((6 * share, hid), bf16),
            pltpu.VMEM((3 * hid, 2 * share), bf16),
            pltpu.VMEM((outputs, group, channels), f32),
            dma((7,)), dma((pieces + 1,)), dma((pieces,)), dma((pieces,)), dma((pieces,)),
            dma((7,)), dma((7,)), dma, pltpu.SemaphoreType.REGULAR((slabs,)),
        ],
        compiler_params=pltpu.CompilerParams(
            collective_id=0, has_side_effects=True, vmem_limit_bytes=40 << 20
        ),
    )(*operands)
    return pl.pallas_call(
        functools.partial(kernel_grads, shape),
        out_shape=(
            jax.ShapeDtypeStruct((27, inner, channels), f32),
            jax.ShapeDtypeStruct((27, inner, features), f32),
            jax.ShapeDtypeStruct((share, hid), f32),
            jax.ShapeDtypeStruct((outputs, hid), f32),
            jax.ShapeDtypeStruct((1, 1), f32),
        ),
        in_specs=[vmem] * 6,
        out_specs=[anywhere] * 5,
        scratch_shapes=[pltpu.VMEM((27, inner, channels), f32), dma((9,)), dma((4,))],
        compiler_params=pltpu.CompilerParams(vmem_limit_bytes=24 << 20),
    )(*stages)


def body(volume, targets, front_weight, stride_weight, hidden_weight, output_weight):
    slabs = lax.axis_size("slab")
    batches = lax.axis_size("batch")
    inner = front_weight.shape[-1]
    leading, thick, extent_x, extent_y, channels = volume.shape
    features = stride_weight.shape[-1]
    small = (slabs, batches, leading, thick, extent_x, extent_y) == (4, 2, 4, 2, 4, 8)
    if not small:
        return split_body(volume, targets, front_weight, stride_weight, hidden_weight, output_weight)
    shape = (slabs, batches) + volume.shape + (inner,)
    grad_front, grad_stride, grad_hidden, grad_output, loss = chain(
        shape, volume, targets,
        jnp.swapaxes(front_weight.reshape(27, channels, inner), 1, 2),
        stride_weight.reshape(27, inner, features), hidden_weight, output_weight.T,
    )
    return (
        jnp.swapaxes(grad_front, 1, 2).reshape(3, 3, 3, channels, inner),
        grad_stride.reshape(3, 3, 3, inner, features),
        grad_hidden,
        grad_output.T,
        loss.reshape(1),
    )


def solution(mesh):
    in_specs = (
        P(("groups", "batch"), "slab", None, None, None),
        P(("groups", "batch"), None),
        P(None, None, None, None, "chan"),
        P(None, None, None, "chan", None),
        P("chan", None),
        P(),
    )
    out_specs = (
        P("groups", None, None, None, "chan"),
        P("groups", None, None, "chan", None),
        P(("groups", "chan"), None),
        P("groups", None),
        P("groups"),
    )
    return jax.shard_map(body, mesh=mesh, in_specs=in_specs, out_specs=out_specs, check_vma=False)
```

```python
import functools

import jax
import jax.numpy as jnp
from jax import lax
from jax.experimental import pallas as pl
from jax.experimental.pallas import tpu as pltpu
from jax.sharding import PartitionSpec as P


def with_halo(cells, sides, width):
    for axis, dim in sides:
        count = lax.axis_size(axis)
        ends = count - 1
        head = lax.slice_in_dim(cells, 0, width, axis=dim)
        tail = lax.slice_in_dim(cells, cells.shape[dim] - width, cells.shape[dim], axis=dim)
        cells = jnp.concatenate(
            [
                lax.ppermute(tail, axis, [(i, (i + 1) % count) for i in range(ends)]),
                cells,
                lax.ppermute(head, axis, [((i + 1) % count, i) for i in range(ends)]),
            ],
            axis=dim,
        )
    return cells


def swish_slope(preact):
    logistic = jax.nn.sigmoid(preact)
    return logistic * (1.0 + preact * (1.0 - logistic))


def tap_window(padded, tap_z, tap_x, tap_y, extent_z, extent_x, extent_y, stride):
    if stride == 1:
        return padded[
            :, tap_z : tap_z + extent_z, tap_x : tap_x + extent_x, tap_y : tap_y + extent_y, :
        ]
    leading = padded.shape[0]
    channels = padded.shape[-1]
    folded = padded.reshape(leading, extent_z + 1, 2, extent_x + 1, 2, extent_y + 1, 2, channels)
    return folded[
        :,
        tap_z // 2 : tap_z // 2 + extent_z,
        tap_z % 2,
        tap_x // 2 : tap_x // 2 + extent_x,
        tap_x % 2,
        tap_y // 2 : tap_y // 2 + extent_y,
        tap_y % 2,
        :,
    ]


def conv_apply(padded, weight, extent_z, extent_x, extent_y, stride):
    summed = None
    for tap_z in range(3):
        for tap_x in range(3):
            for tap_y in range(3):
                window = tap_window(
                    padded, tap_z, tap_x, tap_y, extent_z, extent_x, extent_y, stride
                )
                flat_tap = window.reshape(-1, window.shape[-1])
                contrib = jnp.dot(
                    flat_tap, weight[tap_z, tap_x, tap_y], preferred_element_type=jnp.float32
                )
                summed = contrib if summed is None else summed + contrib
    return summed.reshape(padded.shape[0], extent_z, extent_x, extent_y, weight.shape[-1])


def kernel_grad(padded, grad_out, extent_z, extent_x, extent_y, stride):
    flat_grad = grad_out.reshape(-1, grad_out.shape[-1])
    results = []
    for tap_z in range(3):
        for tap_x in range(3):
            for tap_y in range(3):
                window = tap_window(
                    padded, tap_z, tap_x, tap_y, extent_z, extent_x, extent_y, stride
                )
                flat_tap = window.reshape(-1, window.shape[-1])
                results.append(
                    lax.dot_general(
                        flat_tap,
                        flat_grad,
                        (((0,), (0,)), ((), ())),
                        preferred_element_type=jnp.float32,
                    )
                )
    return jnp.stack(results).reshape(3, 3, 3, padded.shape[-1], grad_out.shape[-1])


def input_grad(grad_out, weight, extent_z, extent_x, extent_y):
    leading = grad_out.shape[0]
    channels = weight.shape[3]
    flat_grad = grad_out.reshape(-1, grad_out.shape[-1])
    buckets = {}
    for tap_z in range(3):
        for tap_x in range(3):
            for tap_y in range(3):
                contrib = lax.dot_general(
                    flat_grad,
                    weight[tap_z, tap_x, tap_y],
                    (((1,), (1,)), ((), ())),
                    preferred_element_type=jnp.float32,
                )
                contrib = contrib.reshape(leading, extent_z, extent_x, extent_y, channels)
                placed = jnp.pad(
                    contrib,
                    (
                        (0, 0),
                        (tap_z // 2, 1 - tap_z // 2),
                        (tap_x // 2, 1 - tap_x // 2),
                        (tap_y // 2, 1 - tap_y // 2),
                        (0, 0),
                    ),
                )
                parity = (tap_z % 2, tap_x % 2, tap_y % 2)
                buckets[parity] = placed if parity not in buckets else buckets[parity] + placed
    planes_z = []
    for par_z in range(2):
        planes_x = []
        for par_x in range(2):
            planes_x.append(jnp.stack([buckets[par_z, par_x, par_y] for par_y in range(2)], axis=4))
        planes_z.append(jnp.stack(planes_x, axis=3))
    assembled = jnp.stack(planes_z, axis=2)
    assembled = assembled.reshape(
        leading, 2 * extent_z + 2, 2 * extent_x + 2, 2 * extent_y + 2, channels
    )
    return assembled[:, 1:-1, 1:-1, 1:-1, :]


def split_body(volume, targets, front_weight, stride_weight, hidden_weight, output_weight):
    highest = lax.Precision.HIGHEST
    slabs = lax.axis_size("slab")
    batches = lax.axis_size("batch")
    inner = front_weight.shape[-1]
    leading, thick, extent_x, extent_y, channels = volume.shape
    depth = thick * slabs
    outputs = output_weight.shape[-1]
    haloed = with_halo(volume, (("slab", 1),), 1)
    padded = jnp.pad(haloed, ((0, 0), (0, 0), (1, 1), (1, 1), (0, 0)))
    front_pre = conv_apply(padded, front_weight, thick, extent_x, extent_y, 1)
    front_act = jax.nn.silu(front_pre).astype(jnp.bfloat16)
    merged = front_act.reshape(leading, thick, extent_x, extent_y * inner)
    sample_act = lax.all_to_all(merged, "slab", split_axis=0, concat_axis=1, tiled=True)
    sample_act = sample_act.reshape(1, depth, extent_x, extent_y, inner)
    half_z = depth // 2
    half_x = extent_x // 2
    half_y = extent_y // 2
    cells = half_z * half_x * half_y
    stride_pad = jnp.pad(sample_act, ((0, 0), (1, 1), (1, 1), (1, 1), (0, 0)))
    partial_pre = conv_apply(stride_pad, stride_weight, half_z, half_x, half_y, 2)
    stride_pre = lax.psum_scatter(partial_pre, "chan", scatter_dimension=4, tiled=True)
    pooled = jnp.sum(jax.nn.silu(stride_pre), axis=(0, 1, 2, 3)) / cells
    hidden_pre = lax.psum(jnp.dot(pooled, hidden_weight, precision=highest), "chan")
    hidden_act = jax.nn.silu(hidden_pre)
    predicted = jnp.dot(hidden_act, output_weight, precision=highest)
    target_row = lax.dynamic_index_in_dim(targets, lax.axis_index("slab"), 0, keepdims=False)
    residual = predicted - target_row
    squared = jnp.sum(residual * residual)
    grad_output = jnp.outer(hidden_act, residual)
    grad_hidden_pre = jnp.dot(output_weight, residual, precision=highest) * swish_slope(hidden_pre)
    grad_hidden = jnp.outer(pooled, grad_hidden_pre)
    grad_pooled = jnp.dot(hidden_weight, grad_hidden_pre, precision=highest)
    grad_stride_pre = (grad_pooled / cells * swish_slope(stride_pre)).astype(jnp.bfloat16)
    full_grad = lax.all_gather(grad_stride_pre, "chan", axis=4, tiled=True)
    grad_stride = kernel_grad(stride_pad, full_grad, half_z, half_x, half_y, 2)
    grad_act = input_grad(full_grad, stride_weight, half_z, half_x, half_y).astype(jnp.bfloat16)
    returned = lax.all_to_all(
        grad_act.reshape(1, depth, extent_x, extent_y * inner),
        "slab",
        split_axis=1,
        concat_axis=0,
        tiled=True,
    )
    returned = returned.reshape(leading, thick, extent_x, extent_y, inner)
    grad_front_pre = (returned * swish_slope(front_pre)).astype(jnp.bfloat16)
    grad_front = kernel_grad(padded, grad_front_pre, thick, extent_x, extent_y, 1)
    grad_front, grad_stride, grad_hidden, grad_output, squared = lax.psum(
        (grad_front, grad_stride, grad_hidden, grad_output, squared), ("slab", "batch")
    )
    loss = (squared / (slabs * batches * outputs)).reshape(1)
    return (grad_front, grad_stride, grad_hidden, grad_output, loss)


MESH = pl.DeviceIdType.MESH


def sigmoid(v):
    return 1.0 / (1.0 + jnp.exp(-v))


def remote(source, target, send_sem, recv_sem, device):
    return pltpu.make_async_remote_copy(
        src_ref=source, dst_ref=target, send_sem=send_sem, recv_sem=recv_sem,
        device_id=device, device_id_type=MESH,
    )


def slab_order(slab, slabs):
    top = slabs - 1
    far = top * (1 - slab // (slabs // 2))
    near = slab + 1 - 2 * lax.rem(slab, 2)
    return [slab, near, slabs * top // 2 - slab - near - far, far]


def chain_kernel(
    shape,
    volume_hbm, targets_hbm, front_hbm, stride_hbm, hidden_hbm, output_hbm,
    taps_ref, taps_other_ref, turned_ref, stride_grad_ref, hidden_grad_ref, output_grad_ref, loss_ref,
    volume_ref, split_ref, front_turned_ref, front_ref, front_pre_ref, slope_ref, strided_ref,
    act_ref, act_out_ref, stride_ref, back_ref, hidden_ref, output_ref, targets_ref,
    spread_ref, head_ref, head_out_ref, grad_ref, turned_out_ref, hidden_split_ref, hidden_turned_ref, target_rows_ref,
    local_sem, send_sem, piece_sem, pass_send_sem, pass_sem, pair_send_sem, pair_sem, target_sem, ready_sem,
):
    slabs, batches, leading, thick, extent_x, extent_y, channels, inner = shape
    slab, batch, chan = lax.axis_index("slab"), lax.axis_index("batch"), lax.axis_index("chan")
    f32, bf16 = jnp.float32, jnp.bfloat16
    highest = lax.Precision.HIGHEST
    half = leading // 2
    depth = slabs * thick
    half_y = extent_y // 2
    half_z, half_x = depth // 2, extent_x // 2
    planes = half_z * half_x
    samples = batches * half
    group = samples * half_y
    rows = 2 * group
    cells = planes * half_y
    wide = 3 * channels
    features = stride_ref.shape[-1]
    share = hidden_hbm.shape[0]
    outputs = output_hbm.shape[0]
    sibling = {"chan": 1 - chan}
    mine = batch * slabs + slab
    pieces = batches * slabs

    across = {"batch": 1 - batch}
    barrier = pltpu.get_barrier_semaphore()
    pl.semaphore_signal(barrier, inc=1, device_id=sibling, device_id_type=MESH)

    def is_own(b, at):
        return (batch == b) & (slab == at)

    for at in reversed(range(slabs)):
        for b in reversed(range(batches)):
            @pl.when((slab <= at) & (batch <= b) & jnp.logical_not(is_own(b, at)))
            def _():
                pl.semaphore_signal(barrier, inc=1, device_id={"batch": b, "slab": at}, device_id_type=MESH)

    local = [
        pltpu.make_async_copy(source, target, local_sem.at[i])
        for i, (source, target) in enumerate([
            (volume_hbm.at[pl.ds(chan * half, half)], volume_ref.at[0, mine]),
            (front_hbm, front_turned_ref.at[:, pl.ds(0, inner)]),
            (stride_hbm, stride_ref.at[:, pl.ds(0, inner)]),
            (hidden_hbm, hidden_ref.at[pl.ds(chan * share, share)]),
            (output_hbm, output_ref),
            (targets_hbm, targets_ref.at[pl.ds(batch * leading, leading)]),
            (volume_hbm.at[pl.ds((1 - chan) * half, half)], volume_ref.at[1, mine]),
        ])
    ]
    for copy in local:
        copy.start()

    pl.semaphore_wait(barrier, (batch + 1) * (slab + 1))

    sends = []

    def send(copy):
        copy.start()
        sends.append(copy)

    pair = [
        remote(front_hbm, front_turned_ref.at[:, pl.ds(inner, inner)], pair_send_sem.at[0], pair_sem.at[0], sibling),
        remote(stride_hbm, stride_ref.at[:, pl.ds(inner, inner)], pair_send_sem.at[1], pair_sem.at[1], sibling),
        remote(hidden_hbm, hidden_ref.at[pl.ds(chan * share, share)], pair_send_sem.at[2], pair_sem.at[2], sibling),
        remote(act_out_ref, act_ref.at[1], pair_send_sem.at[3], pair_sem.at[3], sibling),
        remote(
            spread_ref.at[0, pl.ds(0, half_z), pl.ds(0, half_x)], spread_ref.at[1, pl.ds(0, half_z), pl.ds(0, half_x)],
            pair_send_sem.at[4], pair_sem.at[4], sibling,
        ),
        remote(head_out_ref, head_ref.at[1], pair_send_sem.at[5], pair_sem.at[5], sibling),
        remote(turned_out_ref, turned_ref.at[1], pair_send_sem.at[6], pair_sem.at[6], sibling),
    ]
    order = slab_order(slab, slabs)
    own = volume_hbm.at[pl.ds(chan * half, half)]

    def piece(side, b, at):
        return volume_ref.at[side, b * slabs + at]

    place = targets_ref.at[pl.ds(batch * leading, leading)]
    spread = {}
    for at in range(slabs):
        for b in range(batches):
            number = b * slabs + at
            spread[b, at] = remote(
                own, piece(0, batch, slab), send_sem.at[number], piece_sem.at[mine], {"batch": b, "slab": at}
            )
    targets_copy = remote(targets_hbm, place, send_sem.at[pieces], target_sem, across)

    def below(b, at):
        return (slab >= at) & (batch >= b) & jnp.logical_not(is_own(b, at))

    def send_below(first):
        for at in range(slabs):
            for b in range(batches):
                if first or at or b:
                    @pl.when(below(b, at))
                    def _():
                        spread[b, at].start()

    late = slab == slabs - 1

    @pl.when(late)
    def _():
        spread[0, 0].start()

    @pl.when(jnp.logical_not(late))
    def _():
        send_below(True)

    for at in range(slabs):
        for b in range(batches):
            @pl.when((batch == 1) & (slab >= at) & jnp.logical_not(is_own(b, at)))
            def _():
                pl.semaphore_signal(
                    ready_sem.at[slab], inc=1, device_id={"batch": b, "slab": at}, device_id_type=MESH
                )

    @pl.when(batch == 1)
    def _():
        targets_copy.start()

    send(pair[0])
    send(pair[1])
    send(pair[2])

    front_pre_ref[...] = jnp.zeros(front_pre_ref.shape, f32)
    edge = jnp.zeros((depth, rows, wide), bf16)
    for ref in (taps_ref, taps_other_ref):
        ref[:, 0] = edge
        ref[:, extent_x + 1] = edge
    strided_ref[0] = jnp.zeros((extent_x + 1, group, wide), bf16)
    strided_ref[:, 0] = jnp.zeros((depth + 1, group, wide), bf16)
    for side in range(2):
        spread_ref[side, half_z] = jnp.zeros((half_x + 1, group, 2 * features), bf16)
        spread_ref[side, :, half_x] = jnp.zeros((half_z + 1, group, 2 * features), bf16)
    blank = jnp.zeros((features, channels), bf16)
    for tap in range(9):
        back_ref[tap, features:, :channels] = blank

    @pl.when(late)
    def _():
        spread[0, 0].wait_send()
        send_below(False)

    row = lax.broadcasted_iota(jnp.int32, (group, channels), 0)
    first = (row & (half_y - 1)) == 0
    last = (row & (half_y - 1)) == half_y - 1
    lane_low = lax.broadcasted_iota(jnp.int32, (group, channels), 1) < inner

    def fill(side, at):
        for plane in range(thick):
            for x in range(extent_x):
                slot = plane * extent_x + x
                for b in range(batches):
                    split_ref[side, slot, b * half * extent_y : (b + 1) * half * extent_y] = (
                        volume_ref[side, b * slabs + at, :, plane, x].astype(f32).reshape(half * extent_y, channels)
                    )
                even = split_ref[side, slot, pl.ds(0, group, stride=2), :]
                odd = split_ref[side, slot, pl.ds(1, group, stride=2), :]
                before = jnp.where(first, 0.0, pltpu.roll(odd, 1, 0)).astype(bf16)
                after = jnp.where(last, 0.0, pltpu.roll(even, group - 1, 0)).astype(bf16)
                even, odd = even.astype(bf16), odd.astype(bf16)
                z = at * thick + plane
                ref = taps_other_ref if side else taps_ref
                ref[z, x + 1, :group] = jnp.concatenate([before, even, odd], axis=1)
                ref[z, x + 1, group:] = jnp.concatenate([even, odd, after], axis=1)

    plane_cells = extent_x * rows

    def front(at):
        window = jnp.concatenate(
            [
                taps_ref[pl.ds(at * thick, thick), kx : kx + extent_x].reshape(thick * plane_cells, wide)
                for kx in range(3)
            ],
            axis=1,
        )
        sums = jnp.dot(window, front_ref[...], preferred_element_type=f32)

        def block(plane, kz):
            return sums[plane * plane_cells : (plane + 1) * plane_cells, kz * channels : (kz + 1) * channels]

        base = at * thick
        front_pre_ref[base] += block(0, 2)
        front_pre_ref[base + 1] += block(0, 1) + block(1, 2)
        front_pre_ref[base + 2] += block(0, 0) + block(1, 1)
        front_pre_ref[base + 3] += block(1, 0)

    slots = {}
    for pz in range(2):
        for px in range(2):
            for sz in range(pz + 1):
                for sx in range(px + 1):
                    kz = 1 if pz == 0 else 2 - 2 * sz
                    kx = 1 if px == 0 else 2 - 2 * sx
                    slots[pz, px, sz, sx] = (len(slots), kz, kx)

    other = 1 - batch

    def arrived(b, at):
        remote(piece(0, b, at), piece(0, b, at), send_sem.at[0], piece_sem.at[b * slabs + at], sibling).wait_recv()

    def pass_on(slot, b, at):
        number = b * slabs + at
        send(remote(piece(0, b, at), piece(1, b, at), pass_send_sem.at[slot], pass_sem.at[number], sibling))

    def prepare_front():
        local[1].wait()
        pair[0].wait_recv()
        for kz in range(3):
            for tap in range(9):
                front_ref[tap * channels : (tap + 1) * channels, kz * channels : (kz + 1) * channels] = jnp.transpose(
                    front_turned_ref[9 * kz + tap]
                )

    def prepare_back():
        local[2].wait()
        pair[1].wait_recv()
        for slot, kz, kx in slots.values():
            start = 9 * kz + 3 * kx
            back_ref[slot, :features, :channels] = jnp.transpose(stride_ref[start + 1])
            back_ref[slot, :features, channels:] = jnp.transpose(stride_ref[start + 2])
            back_ref[slot, features:, channels:] = jnp.transpose(stride_ref[start])

    local[0].wait()
    local[6].wait()
    for level in range(slabs):
        @pl.when((slab == level) & (batch == 0))
        def _():
            pl.semaphore_wait(ready_sem.at[level], 1)
            targets_copy.start()
            for at in range(level + 1):
                spread[1, at].start()

        @pl.when(slab < level)
        def _():
            pl.semaphore_wait(ready_sem.at[level], 1)
            for b in range(batches):
                spread[b, level].start()

    prepare_front()

    def other_fill(i):
        at = order[i]
        for b in ([batch, other] if i else [other]):
            remote(
                piece(1, b, at), piece(1, b, at), send_sem.at[0], pass_sem.at[b * slabs + at], sibling
            ).wait_recv()
        fill(1, at)

    far = order[slabs - 1] // (slabs - 1)

    def activate(z):
        total = front_pre_ref[z + 1]
        logistic = sigmoid(total)
        act = (total * logistic).reshape(extent_x, 2, group, channels)
        slope_ref[z] = (logistic * (1.0 + total * (1.0 - logistic))).reshape(extent_x, 2, group, channels)
        for x in range(extent_x):
            even, odd = act[x, 0], act[x, 1]
            before = jnp.where(first, 0.0, pltpu.roll(odd, 1, 0)).astype(bf16)
            strided_ref[z + 1, x + 1] = jnp.concatenate([before, even.astype(bf16), odd.astype(bf16)], axis=1)
            where = (lax.rem(z, 2), x % 2, (z // 2) * half_x + x // 2)
            act_ref[(0,) + where] = jnp.where(lane_low, even, pltpu.roll(odd, inner, 1)).astype(bf16)
            act_out_ref[where] = jnp.where(lane_low, pltpu.roll(even, inner, 1), odd).astype(bf16)

    all_samples = batches * leading

    def halves(value):
        high = value.astype(bf16)
        return high, (value - high.astype(f32)).astype(bf16)

    def prepare_head():
        for copy in local[3:6]:
            copy.wait()
        pair[2].wait_recv()
        remote(
            targets_hbm, targets_ref.at[pl.ds(other * leading, leading)], send_sem.at[0], target_sem, sibling
        ).wait_recv()
        for ref, value in ((hidden_split_ref, hidden_ref[...]), (hidden_turned_ref, jnp.transpose(hidden_ref[...]))):
            high, low = halves(value)
            depth_of = value.shape[0]
            ref[:depth_of] = high
            ref[depth_of : 2 * depth_of] = high
            ref[2 * depth_of :] = low
        owner = lax.broadcasted_iota(jnp.int32, (group, all_samples), 1)
        of_row = lax.broadcasted_iota(jnp.int32, (group, all_samples), 0) // half_y
        wanted = (of_row // half) * leading + chan * half + of_row % half
        member = (owner == wanted).astype(f32)
        target_rows = jnp.dot(member, targets_ref[...], precision=highest, preferred_element_type=f32)
        for o in range(outputs):
            target_rows_ref[o] = jnp.broadcast_to(target_rows[:, o : o + 1], (group, channels))

    def dot_split(value, ref):
        high, low = halves(value)
        return jnp.dot(jnp.concatenate([high, low, high], axis=1), ref[...], preferred_element_type=f32)

    prepare_back()
    prepare_head()
    arrived(other, slab)
    pass_on(0, other, slab)
    fill(0, slab)
    front(slab)
    for i in range(1, slabs):
        at = order[i]
        for b in (batch, other):
            arrived(b, at)
            pass_on(2 * i - 1 if b is batch else 2 * i, b, at)
        fill(0, at)
        front(at)
        if i == 2:
            for k in range(depth - thick - 1):
                activate((1 - far) * (thick + 1) + k)

    for k in range(thick + 1):
        activate(far * (depth - thick - 1) + k)
    send(pair[3])

    windows = jnp.concatenate(
        [
            jnp.concatenate(
                [strided_ref[kz + 2 * z, kx + 2 * x] for z in range(half_z) for x in range(half_x)], axis=0
            )
            for kz in range(3) for kx in range(3)
        ],
        axis=1,
    )
    pre = jnp.dot(windows, stride_ref[...].reshape(27 * channels, features), preferred_element_type=f32)
    logistic = sigmoid(pre)
    summed = jnp.sum((pre * logistic).reshape(planes, group, features), axis=0)
    slope = (logistic * (1.0 + pre * (1.0 - logistic))).reshape(planes, group, features)
    wide_row = lax.broadcasted_iota(jnp.int32, (group, features), 0)
    step = 1
    while step < half_y:
        high = (wide_row & step) != 0
        summed = summed + jnp.where(high, pltpu.roll(summed, step, 0), pltpu.roll(summed, group - step, 0))
        step *= 2
    pooled = summed / cells
    output = output_ref[...]
    hidden_pre = dot_split(pooled, hidden_split_ref)
    hidden_logistic = sigmoid(hidden_pre)
    hidden_act = hidden_pre * hidden_logistic
    hidden_slope = hidden_logistic * (1.0 + hidden_pre * (1.0 - hidden_logistic))
    lane = lax.broadcasted_iota(jnp.int32, (group, channels), 1)
    residuals = jnp.zeros((group, channels), f32)
    back = jnp.zeros((group, output.shape[1]), f32)
    for o in range(outputs):
        residual = jnp.sum(hidden_act * output[o : o + 1], axis=1, keepdims=True) - target_rows_ref[o]
        back = back + residual * output[o : o + 1]
        residuals = jnp.where(lane == o, residual, residuals)
    grad_hidden_pre = back * hidden_slope
    grad_pooled = dot_split(grad_hidden_pre, hidden_turned_ref)
    grad_pre = slope * (grad_pooled / cells)[None]
    grad_next = jnp.where(
        ((wide_row & (half_y - 1)) == half_y - 1)[None],
        0.0,
        jnp.stack([pltpu.roll(grad_pre[i], group - 1, 0) for i in range(planes)]),
    )
    both = jnp.concatenate([grad_pre, grad_next], axis=2).astype(bf16)
    spread_ref[0, :half_z, :half_x] = both.reshape(half_z, half_x, group, 2 * features)
    send(pair[4])
    low_half, high_half = pooled[:, :share], pooled[:, share:]
    head_ref[0, 0] = jnp.where(chan == 0, low_half, high_half)
    head_out_ref[0] = jnp.where(chan == 0, high_half, low_half)
    for i, value in ((1, grad_hidden_pre), (2, hidden_act), (3, residuals)):
        head_ref[0, i] = value
        head_out_ref[i] = value
    send(pair[5])

    def shifted(side, sz, sx):
        return spread_ref[side, sz : sz + half_z, sx : sx + half_x].reshape(planes * group, 2 * features)

    for pz in range(2):
        for px in range(2):
            moves = [(sz, sx) for sz in range(pz + 1) for sx in range(px + 1)]
            start = slots[pz, px, 0, 0][0]
            left = jnp.concatenate([shifted(0, sz, sx) for sz, sx in moves], axis=1)
            right = back_ref[start : start + len(moves)].reshape(len(moves) * 2 * features, 2 * channels)
            grad = jnp.dot(left, right, preferred_element_type=f32)
            grad = grad.reshape(half_z, half_x, group, 2 * channels)
            for z in range(half_z):
                for x in range(half_x):
                    for py in range(2):
                        value = grad[z, x, :, py * channels : (py + 1) * channels].astype(bf16).astype(f32)
                        at = (2 * z + pz, 2 * x + px, py)
                        grad_ref[at] = (value * slope_ref[at]).astype(bf16)
    for z in range(depth):
        turned = jnp.transpose(grad_ref[z].reshape(plane_cells, channels))
        turned_ref[0, :, z * plane_cells : (z + 1) * plane_cells] = turned[:inner]
        turned_out_ref[:, z * plane_cells : (z + 1) * plane_cells] = turned[inner:]
    send(pair[6])

    for i in range(slabs):
        other_fill(i)

    pair[3].wait_recv()
    pair[4].wait_recv()
    turned_act = {
        (pz, px): jnp.concatenate(
            [jnp.transpose(act_ref[side, pz, px].reshape(planes * group, channels)) for side in range(2)], axis=1
        )
        for pz in range(2) for px in range(2)
    }
    for sz in range(2):
        for sx in range(2):
            right = jnp.concatenate([shifted(side, sz, sx) for side in range(2)], axis=0)
            for pz in range(sz, 2):
                for px in range(sx, 2):
                    _, kz, kx = slots[pz, px, sz, sx]
                    grad = jnp.dot(turned_act[pz, px], right, preferred_element_type=f32)
                    start = 9 * kz + 3 * kx
                    stride_grad_ref[start + 1] = grad[:inner, :features]
                    stride_grad_ref[start + 2] = grad[inner:, :features]
                    stride_grad_ref[start] = grad[inner:, features:]

    pair[5].wait_recv()
    pooled_all, hidden_pre_all, hidden_all, residual_all = [
        jnp.concatenate([head_ref[0, i], head_ref[1, i]], axis=0) for i in range(4)
    ]

    def outer(left, right):
        return lax.dot_general(
            left, right, (((0,), (0,)), ((), ())), precision=highest, preferred_element_type=f32
        ) / half_y

    hidden_grad_ref[...] = outer(pooled_all, hidden_pre_all)
    output_grad_ref[...] = outer(residual_all, hidden_all)[:outputs]
    loss_ref[...] = jnp.sum(residual_all * residual_all, keepdims=True) / (half_y * all_samples * outputs)

    pair[6].wait_recv()
    for at in range(slabs):
        for b in range(batches):
            waited = is_own(b, at) if at or b else is_own(b, at) | late

            @pl.when(jnp.logical_not(waited))
            def _():
                spread[b, at].wait_send()
    targets_copy.wait_send()
    for copy in sends:
        copy.wait_send()


def kernel_grads(
    shape,
    taps_ref, taps_other_ref, turned_ref, stride_ref, hidden_ref, output_ref, loss_ref,
    front_out, stride_out, hidden_out, output_out, loss_out,
    front_ref, front_sem, other_sem,
):
    slabs, batches, leading, thick, extent_x, extent_y, channels, inner = shape
    f32, bf16 = jnp.float32, jnp.bfloat16
    depth = slabs * thick
    rows = taps_ref.shape[2]
    plane_cells = extent_x * rows
    wide = 3 * channels
    others = [
        pltpu.make_async_copy(source, target, other_sem.at[i])
        for i, (source, target) in enumerate(
            [(stride_ref, stride_out), (hidden_ref, hidden_out), (output_ref, output_out), (loss_ref, loss_out)]
        )
    ]
    for copy in others:
        copy.start()
    edge = jnp.zeros((inner, plane_cells), bf16)

    def stacked(side):
        grads = turned_ref[side]
        return jnp.concatenate(
            [
                jnp.concatenate([grads[:, plane_cells:], edge], axis=1),
                grads,
                jnp.concatenate([edge, grads[:, :-plane_cells]], axis=1),
            ],
            axis=0,
        )

    left = jnp.concatenate([stacked(0), stacked(1)], axis=1)

    def send_out(group):
        place = pl.ds(3 * group, 3)
        return pltpu.make_async_copy(front_ref.at[place], front_out.at[place], front_sem.at[group])

    def window(kx):
        return jnp.concatenate(
            [ref[:, kx : kx + extent_x].reshape(depth * plane_cells, wide) for ref in (taps_ref, taps_other_ref)], axis=0
        )

    for columns in ((0, 1), (2,)):
        right = jnp.concatenate([window(kx) for kx in columns], axis=1)
        grads = jnp.dot(left, right, preferred_element_type=f32)
        for i, kx in enumerate(columns):
            for kz in range(3):
                for ky in range(3):
                    start = i * wide + ky * channels
                    front_ref[9 * kz + 3 * kx + ky] = grads[kz * inner : (kz + 1) * inner, start : start + channels]
                send_out(3 * kz + kx).start()
    for group in range(9):
        send_out(group).wait()
    for copy in others:
        copy.wait()


def chain(shape, volume, targets, front_turned, stride_own, hidden_weight, output_turned):
    slabs, batches, leading, thick, extent_x, extent_y, channels, inner = shape
    f32, bf16 = jnp.float32, jnp.bfloat16
    features = stride_own.shape[-1]
    share, hid = hidden_weight.shape
    outputs = output_turned.shape[0]
    half = leading // 2
    pieces = slabs * batches
    depth = slabs * thick
    group = batches * half * extent_y // 2
    rows = 2 * group
    half_z, half_x = depth // 2, extent_x // 2
    planes = half_z * half_x
    plane_cells = extent_x * rows
    wide = 3 * channels
    vmem = pl.BlockSpec(memory_space=pltpu.VMEM)
    anywhere = pl.BlockSpec(memory_space=pl.ANY)
    dma = pltpu.SemaphoreType.DMA
    operands = [
        pltpu.with_memory_space_constraint(x, pltpu.HBM)
        for x in (volume, targets, front_turned, stride_own, hidden_weight, output_turned)
    ]
    stages = pl.pallas_call(
        functools.partial(chain_kernel, shape),
        out_shape=(
            jax.ShapeDtypeStruct((depth, extent_x + 2, rows, wide), bf16),
            jax.ShapeDtypeStruct((depth, extent_x + 2, rows, wide), bf16),
            jax.ShapeDtypeStruct((2, inner, depth * plane_cells), bf16),
            jax.ShapeDtypeStruct((27, inner, features), f32),
            jax.ShapeDtypeStruct((share, hid), f32),
            jax.ShapeDtypeStruct((outputs, hid), f32),
            jax.ShapeDtypeStruct((1, 1), f32),
        ),
        in_specs=[anywhere] * 6,
        out_specs=[vmem] * 7,
        scratch_shapes=[
            pltpu.VMEM((2, pieces, half) + volume.shape[1:], bf16),
            pltpu.VMEM((2, thick * extent_x, rows, channels), f32),
            pltpu.VMEM((27, channels, channels), bf16),
            pltpu.VMEM((9 * channels, wide), bf16),
            pltpu.VMEM((depth + 2, plane_cells, channels), f32),
            pltpu.VMEM((depth, extent_x, 2, group, channels), f32),
            pltpu.VMEM((depth + 1, extent_x + 1, group, wide), bf16),
            pltpu.VMEM((2, 2, 2, planes, group, channels), bf16),
            pltpu.VMEM((2, 2, planes, group, channels), bf16),
            pltpu.VMEM((27, channels, features), bf16),
            pltpu.VMEM((9, 2 * features, 2 * channels), bf16),
            pltpu.VMEM((2 * share, hid), f32),
            pltpu.VMEM((outputs, hid), f32),
            pltpu.VMEM((batches * leading, outputs), f32),
            pltpu.VMEM((2, half_z + 1, half_x + 1, group, 2 * features), bf16),
            pltpu.VMEM((2, 4, group, channels), f32),
            pltpu.VMEM((4, group, channels), f32),
            pltpu.VMEM((depth, extent_x, 2, group, channels), bf16),
            pltpu.VMEM((inner, depth * plane_cells), bf16),
            pltpu.VMEM((6 * share, hid), bf16),
            pltpu.VMEM((3 * hid, 2 * share), bf16),
            pltpu.VMEM((outputs, group, channels), f32),
            dma((7,)), dma((pieces + 1,)), dma((pieces,)), dma((pieces,)), dma((pieces,)),
            dma((7,)), dma((7,)), dma, pltpu.SemaphoreType.REGULAR((slabs,)),
        ],
        compiler_params=pltpu.CompilerParams(
            collective_id=0, has_side_effects=True, vmem_limit_bytes=40 << 20
        ),
    )(*operands)
    return pl.pallas_call(
        functools.partial(kernel_grads, shape),
        out_shape=(
            jax.ShapeDtypeStruct((27, inner, channels), f32),
            jax.ShapeDtypeStruct((27, inner, features), f32),
            jax.ShapeDtypeStruct((share, hid), f32),
            jax.ShapeDtypeStruct((outputs, hid), f32),
            jax.ShapeDtypeStruct((1, 1), f32),
        ),
        in_specs=[vmem] * 7,
        out_specs=[anywhere] * 5,
        scratch_shapes=[pltpu.VMEM((27, inner, channels), f32), dma((9,)), dma((4,))],
        compiler_params=pltpu.CompilerParams(vmem_limit_bytes=24 << 20),
    )(*stages)


def body(volume, targets, front_weight, stride_weight, hidden_weight, output_weight):
    slabs = lax.axis_size("slab")
    batches = lax.axis_size("batch")
    inner = front_weight.shape[-1]
    leading, thick, extent_x, extent_y, channels = volume.shape
    features = stride_weight.shape[-1]
    small = (slabs, batches, leading, thick, extent_x, extent_y) == (4, 2, 4, 2, 4, 8)
    if not small:
        return split_body(volume, targets, front_weight, stride_weight, hidden_weight, output_weight)
    shape = (slabs, batches) + volume.shape + (inner,)
    grad_front, grad_stride, grad_hidden, grad_output, loss = chain(
        shape, volume, targets,
        jnp.swapaxes(front_weight.reshape(27, channels, inner), 1, 2),
        stride_weight.reshape(27, inner, features), hidden_weight, output_weight.T,
    )
    return (
        jnp.swapaxes(grad_front, 1, 2).reshape(3, 3, 3, channels, inner),
        grad_stride.reshape(3, 3, 3, inner, features),
        grad_hidden,
        grad_output.T,
        loss.reshape(1),
    )


def solution(mesh):
    in_specs = (
        P(("groups", "batch"), "slab", None, None, None),
        P(("groups", "batch"), None),
        P(None, None, None, None, "chan"),
        P(None, None, None, "chan", None),
        P("chan", None),
        P(),
    )
    out_specs = (
        P("groups", None, None, None, "chan"),
        P("groups", None, None, "chan", None),
        P(("groups", "chan"), None),
        P("groups", None),
        P("groups"),
    )
    return jax.shard_map(body, mesh=mesh, in_specs=in_specs, out_specs=out_specs, check_vma=False)
```

```python
import functools

import jax
import jax.numpy as jnp
from jax import lax
from jax.experimental import pallas as pl
from jax.experimental.pallas import tpu as pltpu
from jax.sharding import PartitionSpec as P


def with_halo(cells, sides, width):
    for axis, dim in sides:
        count = lax.axis_size(axis)
        ends = count - 1
        head = lax.slice_in_dim(cells, 0, width, axis=dim)
        tail = lax.slice_in_dim(cells, cells.shape[dim] - width, cells.shape[dim], axis=dim)
        cells = jnp.concatenate(
            [
                lax.ppermute(tail, axis, [(i, (i + 1) % count) for i in range(ends)]),
                cells,
                lax.ppermute(head, axis, [((i + 1) % count, i) for i in range(ends)]),
            ],
            axis=dim,
        )
    return cells


def swish_slope(preact):
    logistic = jax.nn.sigmoid(preact)
    return logistic * (1.0 + preact * (1.0 - logistic))


def tap_window(padded, tap_z, tap_x, tap_y, extent_z, extent_x, extent_y, stride):
    if stride == 1:
        return padded[
            :, tap_z : tap_z + extent_z, tap_x : tap_x + extent_x, tap_y : tap_y + extent_y, :
        ]
    leading = padded.shape[0]
    channels = padded.shape[-1]
    folded = padded.reshape(leading, extent_z + 1, 2, extent_x + 1, 2, extent_y + 1, 2, channels)
    return folded[
        :,
        tap_z // 2 : tap_z // 2 + extent_z,
        tap_z % 2,
        tap_x // 2 : tap_x // 2 + extent_x,
        tap_x % 2,
        tap_y // 2 : tap_y // 2 + extent_y,
        tap_y % 2,
        :,
    ]


def conv_apply(padded, weight, extent_z, extent_x, extent_y, stride):
    summed = None
    for tap_z in range(3):
        for tap_x in range(3):
            for tap_y in range(3):
                window = tap_window(
                    padded, tap_z, tap_x, tap_y, extent_z, extent_x, extent_y, stride
                )
                flat_tap = window.reshape(-1, window.shape[-1])
                contrib = jnp.dot(
                    flat_tap, weight[tap_z, tap_x, tap_y], preferred_element_type=jnp.float32
                )
                summed = contrib if summed is None else summed + contrib
    return summed.reshape(padded.shape[0], extent_z, extent_x, extent_y, weight.shape[-1])


def kernel_grad(padded, grad_out, extent_z, extent_x, extent_y, stride):
    flat_grad = grad_out.reshape(-1, grad_out.shape[-1])
    results = []
    for tap_z in range(3):
        for tap_x in range(3):
            for tap_y in range(3):
                window = tap_window(
                    padded, tap_z, tap_x, tap_y, extent_z, extent_x, extent_y, stride
                )
                flat_tap = window.reshape(-1, window.shape[-1])
                results.append(
                    lax.dot_general(
                        flat_tap,
                        flat_grad,
                        (((0,), (0,)), ((), ())),
                        preferred_element_type=jnp.float32,
                    )
                )
    return jnp.stack(results).reshape(3, 3, 3, padded.shape[-1], grad_out.shape[-1])


def input_grad(grad_out, weight, extent_z, extent_x, extent_y):
    leading = grad_out.shape[0]
    channels = weight.shape[3]
    flat_grad = grad_out.reshape(-1, grad_out.shape[-1])
    buckets = {}
    for tap_z in range(3):
        for tap_x in range(3):
            for tap_y in range(3):
                contrib = lax.dot_general(
                    flat_grad,
                    weight[tap_z, tap_x, tap_y],
                    (((1,), (1,)), ((), ())),
                    preferred_element_type=jnp.float32,
                )
                contrib = contrib.reshape(leading, extent_z, extent_x, extent_y, channels)
                placed = jnp.pad(
                    contrib,
                    (
                        (0, 0),
                        (tap_z // 2, 1 - tap_z // 2),
                        (tap_x // 2, 1 - tap_x // 2),
                        (tap_y // 2, 1 - tap_y // 2),
                        (0, 0),
                    ),
                )
                parity = (tap_z % 2, tap_x % 2, tap_y % 2)
                buckets[parity] = placed if parity not in buckets else buckets[parity] + placed
    planes_z = []
    for par_z in range(2):
        planes_x = []
        for par_x in range(2):
            planes_x.append(jnp.stack([buckets[par_z, par_x, par_y] for par_y in range(2)], axis=4))
        planes_z.append(jnp.stack(planes_x, axis=3))
    assembled = jnp.stack(planes_z, axis=2)
    assembled = assembled.reshape(
        leading, 2 * extent_z + 2, 2 * extent_x + 2, 2 * extent_y + 2, channels
    )
    return assembled[:, 1:-1, 1:-1, 1:-1, :]


def split_body(volume, targets, front_weight, stride_weight, hidden_weight, output_weight):
    highest = lax.Precision.HIGHEST
    slabs = lax.axis_size("slab")
    batches = lax.axis_size("batch")
    inner = front_weight.shape[-1]
    leading, thick, extent_x, extent_y, channels = volume.shape
    depth = thick * slabs
    outputs = output_weight.shape[-1]
    haloed = with_halo(volume, (("slab", 1),), 1)
    padded = jnp.pad(haloed, ((0, 0), (0, 0), (1, 1), (1, 1), (0, 0)))
    front_pre = conv_apply(padded, front_weight, thick, extent_x, extent_y, 1)
    front_act = jax.nn.silu(front_pre).astype(jnp.bfloat16)
    merged = front_act.reshape(leading, thick, extent_x, extent_y * inner)
    sample_act = lax.all_to_all(merged, "slab", split_axis=0, concat_axis=1, tiled=True)
    sample_act = sample_act.reshape(1, depth, extent_x, extent_y, inner)
    half_z = depth // 2
    half_x = extent_x // 2
    half_y = extent_y // 2
    cells = half_z * half_x * half_y
    stride_pad = jnp.pad(sample_act, ((0, 0), (1, 1), (1, 1), (1, 1), (0, 0)))
    partial_pre = conv_apply(stride_pad, stride_weight, half_z, half_x, half_y, 2)
    stride_pre = lax.psum_scatter(partial_pre, "chan", scatter_dimension=4, tiled=True)
    pooled = jnp.sum(jax.nn.silu(stride_pre), axis=(0, 1, 2, 3)) / cells
    hidden_pre = lax.psum(jnp.dot(pooled, hidden_weight, precision=highest), "chan")
    hidden_act = jax.nn.silu(hidden_pre)
    predicted = jnp.dot(hidden_act, output_weight, precision=highest)
    target_row = lax.dynamic_index_in_dim(targets, lax.axis_index("slab"), 0, keepdims=False)
    residual = predicted - target_row
    squared = jnp.sum(residual * residual)
    grad_output = jnp.outer(hidden_act, residual)
    grad_hidden_pre = jnp.dot(output_weight, residual, precision=highest) * swish_slope(hidden_pre)
    grad_hidden = jnp.outer(pooled, grad_hidden_pre)
    grad_pooled = jnp.dot(hidden_weight, grad_hidden_pre, precision=highest)
    grad_stride_pre = (grad_pooled / cells * swish_slope(stride_pre)).astype(jnp.bfloat16)
    full_grad = lax.all_gather(grad_stride_pre, "chan", axis=4, tiled=True)
    grad_stride = kernel_grad(stride_pad, full_grad, half_z, half_x, half_y, 2)
    grad_act = input_grad(full_grad, stride_weight, half_z, half_x, half_y).astype(jnp.bfloat16)
    returned = lax.all_to_all(
        grad_act.reshape(1, depth, extent_x, extent_y * inner),
        "slab",
        split_axis=1,
        concat_axis=0,
        tiled=True,
    )
    returned = returned.reshape(leading, thick, extent_x, extent_y, inner)
    grad_front_pre = (returned * swish_slope(front_pre)).astype(jnp.bfloat16)
    grad_front = kernel_grad(padded, grad_front_pre, thick, extent_x, extent_y, 1)
    grad_front, grad_stride, grad_hidden, grad_output, squared = lax.psum(
        (grad_front, grad_stride, grad_hidden, grad_output, squared), ("slab", "batch")
    )
    loss = (squared / (slabs * batches * outputs)).reshape(1)
    return (grad_front, grad_stride, grad_hidden, grad_output, loss)


MESH = pl.DeviceIdType.MESH


def sigmoid(v):
    return 1.0 / (1.0 + jnp.exp(-v))


def remote(source, target, send_sem, recv_sem, device):
    return pltpu.make_async_remote_copy(
        src_ref=source, dst_ref=target, send_sem=send_sem, recv_sem=recv_sem,
        device_id=device, device_id_type=MESH,
    )


def slab_order(slab, slabs):
    top = slabs - 1
    far = top * (1 - slab // (slabs // 2))
    near = slab + 1 - 2 * lax.rem(slab, 2)
    return [slab, near, slabs * top // 2 - slab - near - far, far]


def chain_kernel(
    shape,
    volume_hbm, targets_hbm, front_hbm, stride_hbm, hidden_hbm, output_hbm,
    taps_ref, taps_other_ref, turned_ref, stride_grad_ref, hidden_grad_ref, output_grad_ref, loss_ref,
    volume_ref, split_ref, front_turned_ref, front_ref, front_pre_ref, slope_ref, strided_ref,
    act_ref, act_out_ref, stride_ref, back_ref, hidden_ref, output_ref, targets_ref,
    spread_ref, head_ref, head_out_ref, grad_ref, turned_out_ref, hidden_split_ref, hidden_turned_ref, target_rows_ref,
    local_sem, send_sem, piece_sem, pass_send_sem, pass_sem, pair_send_sem, pair_sem, target_sem, ready_sem,
):
    slabs, batches, leading, thick, extent_x, extent_y, channels, inner = shape
    slab, batch, chan = lax.axis_index("slab"), lax.axis_index("batch"), lax.axis_index("chan")
    f32, bf16 = jnp.float32, jnp.bfloat16
    highest = lax.Precision.HIGHEST
    half = leading // 2
    depth = slabs * thick
    half_y = extent_y // 2
    half_z, half_x = depth // 2, extent_x // 2
    planes = half_z * half_x
    samples = batches * half
    group = samples * half_y
    rows = 2 * group
    cells = planes * half_y
    wide = 3 * channels
    features = stride_ref.shape[-1]
    share = hidden_hbm.shape[0]
    outputs = output_hbm.shape[0]
    sibling = {"chan": 1 - chan}
    mine = batch * slabs + slab
    pieces = batches * slabs

    across = {"batch": 1 - batch}
    barrier = pltpu.get_barrier_semaphore()
    pl.semaphore_signal(barrier, inc=1, device_id=sibling, device_id_type=MESH)

    def is_own(b, at):
        return (batch == b) & (slab == at)

    for at in reversed(range(slabs)):
        for b in reversed(range(batches)):
            @pl.when((slab <= at) & (batch <= b) & jnp.logical_not(is_own(b, at)))
            def _():
                pl.semaphore_signal(barrier, inc=1, device_id={"batch": b, "slab": at}, device_id_type=MESH)

    local = [
        pltpu.make_async_copy(source, target, local_sem.at[i])
        for i, (source, target) in enumerate([
            (volume_hbm.at[pl.ds(chan * half, half)], volume_ref.at[0, mine]),
            (front_hbm, front_turned_ref.at[:, pl.ds(0, inner)]),
            (stride_hbm, stride_ref.at[:, pl.ds(0, inner)]),
            (hidden_hbm, hidden_ref.at[pl.ds(chan * share, share)]),
            (output_hbm, output_ref),
            (targets_hbm, targets_ref.at[pl.ds(batch * leading, leading)]),
            (volume_hbm.at[pl.ds((1 - chan) * half, half)], volume_ref.at[1, mine]),
        ])
    ]
    for copy in local:
        copy.start()

    pl.semaphore_wait(barrier, (batch + 1) * (slab + 1))

    sends = []

    def send(copy):
        copy.start()
        sends.append(copy)

    pair = [
        remote(front_hbm, front_turned_ref.at[:, pl.ds(inner, inner)], pair_send_sem.at[0], pair_sem.at[0], sibling),
        remote(stride_hbm, stride_ref.at[:, pl.ds(inner, inner)], pair_send_sem.at[1], pair_sem.at[1], sibling),
        remote(hidden_hbm, hidden_ref.at[pl.ds(chan * share, share)], pair_send_sem.at[2], pair_sem.at[2], sibling),
        remote(act_out_ref, act_ref.at[1], pair_send_sem.at[3], pair_sem.at[3], sibling),
        remote(
            spread_ref.at[0, pl.ds(0, half_z), pl.ds(0, half_x)], spread_ref.at[1, pl.ds(0, half_z), pl.ds(0, half_x)],
            pair_send_sem.at[4], pair_sem.at[4], sibling,
        ),
        remote(head_out_ref, head_ref.at[1], pair_send_sem.at[5], pair_sem.at[5], sibling),
        remote(turned_out_ref, turned_ref.at[1], pair_send_sem.at[6], pair_sem.at[6], sibling),
    ]
    order = slab_order(slab, slabs)
    own = volume_hbm.at[pl.ds(chan * half, half)]

    def piece(side, b, at):
        return volume_ref.at[side, b * slabs + at]

    place = targets_ref.at[pl.ds(batch * leading, leading)]
    spread = {}
    for at in range(slabs):
        for b in range(batches):
            number = b * slabs + at
            spread[b, at] = remote(
                own, piece(0, batch, slab), send_sem.at[number], piece_sem.at[mine], {"batch": b, "slab": at}
            )
    targets_copy = remote(targets_hbm, place, send_sem.at[pieces], target_sem, across)

    def below(b, at):
        return (slab >= at) & (batch >= b) & jnp.logical_not(is_own(b, at))

    def send_below(first):
        for at in range(slabs):
            for b in range(batches):
                if first or at or b:
                    @pl.when(below(b, at))
                    def _():
                        spread[b, at].start()

    late = slab == slabs - 1

    @pl.when(late)
    def _():
        spread[0, 0].start()

    @pl.when(jnp.logical_not(late))
    def _():
        send_below(True)

    for at in range(slabs):
        for b in range(batches):
            @pl.when(below(b, at))
            def _():
                pl.semaphore_signal(ready_sem.at[mine], inc=1, device_id={"batch": b, "slab": at}, device_id_type=MESH)

    @pl.when(batch == 1)
    def _():
        targets_copy.start()

    send(pair[0])
    send(pair[1])
    send(pair[2])

    front_pre_ref[...] = jnp.zeros(front_pre_ref.shape, f32)
    edge = jnp.zeros((depth, rows, wide), bf16)
    for ref in (taps_ref, taps_other_ref):
        ref[:, 0] = edge
        ref[:, extent_x + 1] = edge
    strided_ref[0] = jnp.zeros((extent_x + 1, group, wide), bf16)
    strided_ref[:, 0] = jnp.zeros((depth + 1, group, wide), bf16)
    for side in range(2):
        spread_ref[side, half_z] = jnp.zeros((half_x + 1, group, 2 * features), bf16)
        spread_ref[side, :, half_x] = jnp.zeros((half_z + 1, group, 2 * features), bf16)
    blank = jnp.zeros((features, channels), bf16)
    for tap in range(9):
        back_ref[tap, features:, :channels] = blank

    @pl.when(late)
    def _():
        spread[0, 0].wait_send()
        send_below(False)

    row = lax.broadcasted_iota(jnp.int32, (group, channels), 0)
    first = (row & (half_y - 1)) == 0
    last = (row & (half_y - 1)) == half_y - 1
    lane_low = lax.broadcasted_iota(jnp.int32, (group, channels), 1) < inner

    def fill(side, at):
        for plane in range(thick):
            for x in range(extent_x):
                slot = plane * extent_x + x
                for b in range(batches):
                    split_ref[side, slot, b * half * extent_y : (b + 1) * half * extent_y] = (
                        volume_ref[side, b * slabs + at, :, plane, x].astype(f32).reshape(half * extent_y, channels)
                    )
                even = split_ref[side, slot, pl.ds(0, group, stride=2), :]
                odd = split_ref[side, slot, pl.ds(1, group, stride=2), :]
                before = jnp.where(first, 0.0, pltpu.roll(odd, 1, 0)).astype(bf16)
                after = jnp.where(last, 0.0, pltpu.roll(even, group - 1, 0)).astype(bf16)
                even, odd = even.astype(bf16), odd.astype(bf16)
                z = at * thick + plane
                ref = taps_other_ref if side else taps_ref
                ref[z, x + 1, :group] = jnp.concatenate([before, even, odd], axis=1)
                ref[z, x + 1, group:] = jnp.concatenate([even, odd, after], axis=1)

    plane_cells = extent_x * rows

    def front(at):
        window = jnp.concatenate(
            [
                taps_ref[pl.ds(at * thick, thick), kx : kx + extent_x].reshape(thick * plane_cells, wide)
                for kx in range(3)
            ],
            axis=1,
        )
        sums = jnp.dot(window, front_ref[...], preferred_element_type=f32)

        def block(plane, kz):
            return sums[plane * plane_cells : (plane + 1) * plane_cells, kz * channels : (kz + 1) * channels]

        base = at * thick
        front_pre_ref[base] += block(0, 2)
        front_pre_ref[base + 1] += block(0, 1) + block(1, 2)
        front_pre_ref[base + 2] += block(0, 0) + block(1, 1)
        front_pre_ref[base + 3] += block(1, 0)

    slots = {}
    for pz in range(2):
        for px in range(2):
            for sz in range(pz + 1):
                for sx in range(px + 1):
                    kz = 1 if pz == 0 else 2 - 2 * sz
                    kx = 1 if px == 0 else 2 - 2 * sx
                    slots[pz, px, sz, sx] = (len(slots), kz, kx)

    other = 1 - batch

    def arrived(b, at):
        remote(piece(0, b, at), piece(0, b, at), send_sem.at[0], piece_sem.at[b * slabs + at], sibling).wait_recv()

    def pass_on(slot, b, at):
        number = b * slabs + at
        send(remote(piece(0, b, at), piece(1, b, at), pass_send_sem.at[slot], pass_sem.at[number], sibling))

    def prepare_front():
        local[1].wait()
        pair[0].wait_recv()
        for kz in range(3):
            for tap in range(9):
                front_ref[tap * channels : (tap + 1) * channels, kz * channels : (kz + 1) * channels] = jnp.transpose(
                    front_turned_ref[9 * kz + tap]
                )

    def prepare_back():
        local[2].wait()
        pair[1].wait_recv()
        for slot, kz, kx in slots.values():
            start = 9 * kz + 3 * kx
            back_ref[slot, :features, :channels] = jnp.transpose(stride_ref[start + 1])
            back_ref[slot, :features, channels:] = jnp.transpose(stride_ref[start + 2])
            back_ref[slot, features:, channels:] = jnp.transpose(stride_ref[start])

    local[0].wait()
    local[6].wait()
    for level in range(slabs):
        @pl.when((slab < level) & (batch == 0))
        def _():
            pl.semaphore_wait(ready_sem.at[level], 1)
            spread[0, level].start()

        @pl.when((slab == level) & (batch == 0))
        def _():
            pl.semaphore_wait(ready_sem.at[slabs + level], 1)
            targets_copy.start()
            for at in reversed(range(level + 1)):
                spread[1, at].start()

        @pl.when((slab < level) & (batch == 0))
        def _():
            pl.semaphore_wait(ready_sem.at[slabs + level], 1)
            spread[1, level].start()

        @pl.when((slab < level) & (batch == 1))
        def _():
            pl.semaphore_wait(ready_sem.at[slabs + level], 1)
            spread[0, level].start()
            spread[1, level].start()

    prepare_front()

    def other_fill(i):
        at = order[i]
        for b in ([batch, other] if i else [other]):
            remote(
                piece(1, b, at), piece(1, b, at), send_sem.at[0], pass_sem.at[b * slabs + at], sibling
            ).wait_recv()
        fill(1, at)

    far = order[slabs - 1] // (slabs - 1)

    def activate(z):
        total = front_pre_ref[z + 1]
        logistic = sigmoid(total)
        act = (total * logistic).reshape(extent_x, 2, group, channels)
        slope_ref[z] = (logistic * (1.0 + total * (1.0 - logistic))).reshape(extent_x, 2, group, channels)
        for x in range(extent_x):
            even, odd = act[x, 0], act[x, 1]
            before = jnp.where(first, 0.0, pltpu.roll(odd, 1, 0)).astype(bf16)
            strided_ref[z + 1, x + 1] = jnp.concatenate([before, even.astype(bf16), odd.astype(bf16)], axis=1)
            where = (lax.rem(z, 2), x % 2, (z // 2) * half_x + x // 2)
            act_ref[(0,) + where] = jnp.where(lane_low, even, pltpu.roll(odd, inner, 1)).astype(bf16)
            act_out_ref[where] = jnp.where(lane_low, pltpu.roll(even, inner, 1), odd).astype(bf16)

    all_samples = batches * leading

    def halves(value):
        high = value.astype(bf16)
        return high, (value - high.astype(f32)).astype(bf16)

    def prepare_head():
        for copy in local[3:6]:
            copy.wait()
        pair[2].wait_recv()
        remote(
            targets_hbm, targets_ref.at[pl.ds(other * leading, leading)], send_sem.at[0], target_sem, sibling
        ).wait_recv()
        for ref, value in ((hidden_split_ref, hidden_ref[...]), (hidden_turned_ref, jnp.transpose(hidden_ref[...]))):
            high, low = halves(value)
            depth_of = value.shape[0]
            ref[:depth_of] = high
            ref[depth_of : 2 * depth_of] = high
            ref[2 * depth_of :] = low
        owner = lax.broadcasted_iota(jnp.int32, (group, all_samples), 1)
        of_row = lax.broadcasted_iota(jnp.int32, (group, all_samples), 0) // half_y
        wanted = (of_row // half) * leading + chan * half + of_row % half
        member = (owner == wanted).astype(f32)
        target_rows = jnp.dot(member, targets_ref[...], precision=highest, preferred_element_type=f32)
        for o in range(outputs):
            target_rows_ref[o] = jnp.broadcast_to(target_rows[:, o : o + 1], (group, channels))

    def dot_split(value, ref):
        high, low = halves(value)
        return jnp.dot(jnp.concatenate([high, low, high], axis=1), ref[...], preferred_element_type=f32)

    prepare_back()
    prepare_head()
    arrived(other, slab)
    pass_on(0, other, slab)
    fill(0, slab)
    front(slab)
    for i in range(1, slabs):
        at = order[i]
        for b in (batch, other):
            arrived(b, at)
            pass_on(2 * i - 1 if b is batch else 2 * i, b, at)
        fill(0, at)
        front(at)
        if i == 2:
            for k in range(depth - thick - 1):
                activate((1 - far) * (thick + 1) + k)

    for k in range(thick + 1):
        activate(far * (depth - thick - 1) + k)
    send(pair[3])

    windows = jnp.concatenate(
        [
            jnp.concatenate(
                [strided_ref[kz + 2 * z, kx + 2 * x] for z in range(half_z) for x in range(half_x)], axis=0
            )
            for kz in range(3) for kx in range(3)
        ],
        axis=1,
    )
    pre = jnp.dot(windows, stride_ref[...].reshape(27 * channels, features), preferred_element_type=f32)
    logistic = sigmoid(pre)
    summed = jnp.sum((pre * logistic).reshape(planes, group, features), axis=0)
    slope = (logistic * (1.0 + pre * (1.0 - logistic))).reshape(planes, group, features)
    wide_row = lax.broadcasted_iota(jnp.int32, (group, features), 0)
    step = 1
    while step < half_y:
        high = (wide_row & step) != 0
        summed = summed + jnp.where(high, pltpu.roll(summed, step, 0), pltpu.roll(summed, group - step, 0))
        step *= 2
    pooled = summed / cells
    output = output_ref[...]
    hidden_pre = dot_split(pooled, hidden_split_ref)
    hidden_logistic = sigmoid(hidden_pre)
    hidden_act = hidden_pre * hidden_logistic
    hidden_slope = hidden_logistic * (1.0 + hidden_pre * (1.0 - hidden_logistic))
    lane = lax.broadcasted_iota(jnp.int32, (group, channels), 1)
    residuals = jnp.zeros((group, channels), f32)
    back = jnp.zeros((group, output.shape[1]), f32)
    for o in range(outputs):
        residual = jnp.sum(hidden_act * output[o : o + 1], axis=1, keepdims=True) - target_rows_ref[o]
        back = back + residual * output[o : o + 1]
        residuals = jnp.where(lane == o, residual, residuals)
    grad_hidden_pre = back * hidden_slope
    grad_pooled = dot_split(grad_hidden_pre, hidden_turned_ref)
    grad_pre = slope * (grad_pooled / cells)[None]
    grad_next = jnp.where(
        ((wide_row & (half_y - 1)) == half_y - 1)[None],
        0.0,
        jnp.stack([pltpu.roll(grad_pre[i], group - 1, 0) for i in range(planes)]),
    )
    both = jnp.concatenate([grad_pre, grad_next], axis=2).astype(bf16)
    spread_ref[0, :half_z, :half_x] = both.reshape(half_z, half_x, group, 2 * features)
    send(pair[4])
    low_half, high_half = pooled[:, :share], pooled[:, share:]
    head_ref[0, 0] = jnp.where(chan == 0, low_half, high_half)
    head_out_ref[0] = jnp.where(chan == 0, high_half, low_half)
    for i, value in ((1, grad_hidden_pre), (2, hidden_act), (3, residuals)):
        head_ref[0, i] = value
        head_out_ref[i] = value
    send(pair[5])

    def shifted(side, sz, sx):
        return spread_ref[side, sz : sz + half_z, sx : sx + half_x].reshape(planes * group, 2 * features)

    for pz in range(2):
        for px in range(2):
            moves = [(sz, sx) for sz in range(pz + 1) for sx in range(px + 1)]
            start = slots[pz, px, 0, 0][0]
            left = jnp.concatenate([shifted(0, sz, sx) for sz, sx in moves], axis=1)
            right = back_ref[start : start + len(moves)].reshape(len(moves) * 2 * features, 2 * channels)
            grad = jnp.dot(left, right, preferred_element_type=f32)
            grad = grad.reshape(half_z, half_x, group, 2 * channels)
            for z in range(half_z):
                for x in range(half_x):
                    for py in range(2):
                        value = grad[z, x, :, py * channels : (py + 1) * channels].astype(bf16).astype(f32)
                        at = (2 * z + pz, 2 * x + px, py)
                        grad_ref[at] = (value * slope_ref[at]).astype(bf16)
    for z in range(depth):
        turned = jnp.transpose(grad_ref[z].reshape(plane_cells, channels))
        turned_ref[0, :, z * plane_cells : (z + 1) * plane_cells] = turned[:inner]
        turned_out_ref[:, z * plane_cells : (z + 1) * plane_cells] = turned[inner:]
    send(pair[6])

    for i in range(slabs):
        other_fill(i)

    pair[3].wait_recv()
    pair[4].wait_recv()
    turned_act = {
        (pz, px): jnp.concatenate(
            [jnp.transpose(act_ref[side, pz, px].reshape(planes * group, channels)) for side in range(2)], axis=1
        )
        for pz in range(2) for px in range(2)
    }
    for sz in range(2):
        for sx in range(2):
            right = jnp.concatenate([shifted(side, sz, sx) for side in range(2)], axis=0)
            for pz in range(sz, 2):
                for px in range(sx, 2):
                    _, kz, kx = slots[pz, px, sz, sx]
                    grad = jnp.dot(turned_act[pz, px], right, preferred_element_type=f32)
                    start = 9 * kz + 3 * kx
                    stride_grad_ref[start + 1] = grad[:inner, :features]
                    stride_grad_ref[start + 2] = grad[inner:, :features]
                    stride_grad_ref[start] = grad[inner:, features:]

    pair[5].wait_recv()
    pooled_all, hidden_pre_all, hidden_all, residual_all = [
        jnp.concatenate([head_ref[0, i], head_ref[1, i]], axis=0) for i in range(4)
    ]

    def outer(left, right):
        return lax.dot_general(
            left, right, (((0,), (0,)), ((), ())), precision=highest, preferred_element_type=f32
        ) / half_y

    hidden_grad_ref[...] = outer(pooled_all, hidden_pre_all)
    output_grad_ref[...] = outer(residual_all, hidden_all)[:outputs]
    loss_ref[...] = jnp.sum(residual_all * residual_all, keepdims=True) / (half_y * all_samples * outputs)

    pair[6].wait_recv()
    for at in range(slabs):
        for b in range(batches):
            waited = is_own(b, at) if at or b else is_own(b, at) | late

            @pl.when(jnp.logical_not(waited))
            def _():
                spread[b, at].wait_send()
    targets_copy.wait_send()
    for copy in sends:
        copy.wait_send()


def kernel_grads(
    shape,
    taps_ref, taps_other_ref, turned_ref, stride_ref, hidden_ref, output_ref, loss_ref,
    front_out, stride_out, hidden_out, output_out, loss_out,
    front_ref, front_sem, other_sem,
):
    slabs, batches, leading, thick, extent_x, extent_y, channels, inner = shape
    f32, bf16 = jnp.float32, jnp.bfloat16
    depth = slabs * thick
    rows = taps_ref.shape[2]
    plane_cells = extent_x * rows
    wide = 3 * channels
    others = [
        pltpu.make_async_copy(source, target, other_sem.at[i])
        for i, (source, target) in enumerate(
            [(stride_ref, stride_out), (hidden_ref, hidden_out), (output_ref, output_out), (loss_ref, loss_out)]
        )
    ]
    for copy in others:
        copy.start()
    edge = jnp.zeros((inner, plane_cells), bf16)

    def stacked(side):
        grads = turned_ref[side]
        return jnp.concatenate(
            [
                jnp.concatenate([grads[:, plane_cells:], edge], axis=1),
                grads,
                jnp.concatenate([edge, grads[:, :-plane_cells]], axis=1),
            ],
            axis=0,
        )

    left = jnp.concatenate([stacked(0), stacked(1)], axis=1)

    def send_out(group):
        place = pl.ds(3 * group, 3)
        return pltpu.make_async_copy(front_ref.at[place], front_out.at[place], front_sem.at[group])

    def window(kx):
        return jnp.concatenate(
            [ref[:, kx : kx + extent_x].reshape(depth * plane_cells, wide) for ref in (taps_ref, taps_other_ref)], axis=0
        )

    for columns in ((0, 1), (2,)):
        right = jnp.concatenate([window(kx) for kx in columns], axis=1)
        grads = jnp.dot(left, right, preferred_element_type=f32)
        for i, kx in enumerate(columns):
            for kz in range(3):
                for ky in range(3):
                    start = i * wide + ky * channels
                    front_ref[9 * kz + 3 * kx + ky] = grads[kz * inner : (kz + 1) * inner, start : start + channels]
                send_out(3 * kz + kx).start()
    for group in range(9):
        send_out(group).wait()
    for copy in others:
        copy.wait()


def chain(shape, volume, targets, front_turned, stride_own, hidden_weight, output_turned):
    slabs, batches, leading, thick, extent_x, extent_y, channels, inner = shape
    f32, bf16 = jnp.float32, jnp.bfloat16
    features = stride_own.shape[-1]
    share, hid = hidden_weight.shape
    outputs = output_turned.shape[0]
    half = leading // 2
    pieces = slabs * batches
    depth = slabs * thick
    group = batches * half * extent_y // 2
    rows = 2 * group
    half_z, half_x = depth // 2, extent_x // 2
    planes = half_z * half_x
    plane_cells = extent_x * rows
    wide = 3 * channels
    vmem = pl.BlockSpec(memory_space=pltpu.VMEM)
    anywhere = pl.BlockSpec(memory_space=pl.ANY)
    dma = pltpu.SemaphoreType.DMA
    operands = [
        pltpu.with_memory_space_constraint(x, pltpu.HBM)
        for x in (volume, targets, front_turned, stride_own, hidden_weight, output_turned)
    ]
    stages = pl.pallas_call(
        functools.partial(chain_kernel, shape),
        out_shape=(
            jax.ShapeDtypeStruct((depth, extent_x + 2, rows, wide), bf16),
            jax.ShapeDtypeStruct((depth, extent_x + 2, rows, wide), bf16),
            jax.ShapeDtypeStruct((2, inner, depth * plane_cells), bf16),
            jax.ShapeDtypeStruct((27, inner, features), f32),
            jax.ShapeDtypeStruct((share, hid), f32),
            jax.ShapeDtypeStruct((outputs, hid), f32),
            jax.ShapeDtypeStruct((1, 1), f32),
        ),
        in_specs=[anywhere] * 6,
        out_specs=[vmem] * 7,
        scratch_shapes=[
            pltpu.VMEM((2, pieces, half) + volume.shape[1:], bf16),
            pltpu.VMEM((2, thick * extent_x, rows, channels), f32),
            pltpu.VMEM((27, channels, channels), bf16),
            pltpu.VMEM((9 * channels, wide), bf16),
            pltpu.VMEM((depth + 2, plane_cells, channels), f32),
            pltpu.VMEM((depth, extent_x, 2, group, channels), f32),
            pltpu.VMEM((depth + 1, extent_x + 1, group, wide), bf16),
            pltpu.VMEM((2, 2, 2, planes, group, channels), bf16),
            pltpu.VMEM((2, 2, planes, group, channels), bf16),
            pltpu.VMEM((27, channels, features), bf16),
            pltpu.VMEM((9, 2 * features, 2 * channels), bf16),
            pltpu.VMEM((2 * share, hid), f32),
            pltpu.VMEM((outputs, hid), f32),
            pltpu.VMEM((batches * leading, outputs), f32),
            pltpu.VMEM((2, half_z + 1, half_x + 1, group, 2 * features), bf16),
            pltpu.VMEM((2, 4, group, channels), f32),
            pltpu.VMEM((4, group, channels), f32),
            pltpu.VMEM((depth, extent_x, 2, group, channels), bf16),
            pltpu.VMEM((inner, depth * plane_cells), bf16),
            pltpu.VMEM((6 * share, hid), bf16),
            pltpu.VMEM((3 * hid, 2 * share), bf16),
            pltpu.VMEM((outputs, group, channels), f32),
            dma((7,)), dma((pieces + 1,)), dma((pieces,)), dma((pieces,)), dma((pieces,)),
            dma((7,)), dma((7,)), dma, pltpu.SemaphoreType.REGULAR((pieces,)),
        ],
        compiler_params=pltpu.CompilerParams(
            collective_id=0, has_side_effects=True, vmem_limit_bytes=40 << 20
        ),
    )(*operands)
    return pl.pallas_call(
        functools.partial(kernel_grads, shape),
        out_shape=(
            jax.ShapeDtypeStruct((27, inner, channels), f32),
            jax.ShapeDtypeStruct((27, inner, features), f32),
            jax.ShapeDtypeStruct((share, hid), f32),
            jax.ShapeDtypeStruct((outputs, hid), f32),
            jax.ShapeDtypeStruct((1, 1), f32),
        ),
        in_specs=[vmem] * 7,
        out_specs=[anywhere] * 5,
        scratch_shapes=[pltpu.VMEM((27, inner, channels), f32), dma((9,)), dma((4,))],
        compiler_params=pltpu.CompilerParams(vmem_limit_bytes=24 << 20),
    )(*stages)


def body(volume, targets, front_weight, stride_weight, hidden_weight, output_weight):
    slabs = lax.axis_size("slab")
    batches = lax.axis_size("batch")
    inner = front_weight.shape[-1]
    leading, thick, extent_x, extent_y, channels = volume.shape
    features = stride_weight.shape[-1]
    small = (slabs, batches, leading, thick, extent_x, extent_y) == (4, 2, 4, 2, 4, 8)
    if not small:
        return split_body(volume, targets, front_weight, stride_weight, hidden_weight, output_weight)
    shape = (slabs, batches) + volume.shape + (inner,)
    grad_front, grad_stride, grad_hidden, grad_output, loss = chain(
        shape, volume, targets,
        jnp.swapaxes(front_weight.reshape(27, channels, inner), 1, 2),
        stride_weight.reshape(27, inner, features), hidden_weight, output_weight.T,
    )
    return (
        jnp.swapaxes(grad_front, 1, 2).reshape(3, 3, 3, channels, inner),
        grad_stride.reshape(3, 3, 3, inner, features),
        grad_hidden,
        grad_output.T,
        loss.reshape(1),
    )


def solution(mesh):
    in_specs = (
        P(("groups", "batch"), "slab", None, None, None),
        P(("groups", "batch"), None),
        P(None, None, None, None, "chan"),
        P(None, None, None, "chan", None),
        P("chan", None),
        P(),
    )
    out_specs = (
        P("groups", None, None, None, "chan"),
        P("groups", None, None, "chan", None),
        P(("groups", "chan"), None),
        P("groups", None),
        P("groups"),
    )
    return jax.shard_map(body, mesh=mesh, in_specs=in_specs, out_specs=out_specs, check_vma=False)
```

```python
import functools

import jax
import jax.numpy as jnp
from jax import lax
from jax.experimental import pallas as pl
from jax.experimental.pallas import tpu as pltpu
from jax.sharding import PartitionSpec as P


def with_halo(cells, sides, width):
    for axis, dim in sides:
        count = lax.axis_size(axis)
        ends = count - 1
        head = lax.slice_in_dim(cells, 0, width, axis=dim)
        tail = lax.slice_in_dim(cells, cells.shape[dim] - width, cells.shape[dim], axis=dim)
        cells = jnp.concatenate(
            [
                lax.ppermute(tail, axis, [(i, (i + 1) % count) for i in range(ends)]),
                cells,
                lax.ppermute(head, axis, [((i + 1) % count, i) for i in range(ends)]),
            ],
            axis=dim,
        )
    return cells


def swish_slope(preact):
    logistic = jax.nn.sigmoid(preact)
    return logistic * (1.0 + preact * (1.0 - logistic))


def tap_window(padded, tap_z, tap_x, tap_y, extent_z, extent_x, extent_y, stride):
    if stride == 1:
        return padded[
            :, tap_z : tap_z + extent_z, tap_x : tap_x + extent_x, tap_y : tap_y + extent_y, :
        ]
    leading = padded.shape[0]
    channels = padded.shape[-1]
    folded = padded.reshape(leading, extent_z + 1, 2, extent_x + 1, 2, extent_y + 1, 2, channels)
    return folded[
        :,
        tap_z // 2 : tap_z // 2 + extent_z,
        tap_z % 2,
        tap_x // 2 : tap_x // 2 + extent_x,
        tap_x % 2,
        tap_y // 2 : tap_y // 2 + extent_y,
        tap_y % 2,
        :,
    ]


def conv_apply(padded, weight, extent_z, extent_x, extent_y, stride):
    summed = None
    for tap_z in range(3):
        for tap_x in range(3):
            for tap_y in range(3):
                window = tap_window(
                    padded, tap_z, tap_x, tap_y, extent_z, extent_x, extent_y, stride
                )
                flat_tap = window.reshape(-1, window.shape[-1])
                contrib = jnp.dot(
                    flat_tap, weight[tap_z, tap_x, tap_y], preferred_element_type=jnp.float32
                )
                summed = contrib if summed is None else summed + contrib
    return summed.reshape(padded.shape[0], extent_z, extent_x, extent_y, weight.shape[-1])


def kernel_grad(padded, grad_out, extent_z, extent_x, extent_y, stride):
    flat_grad = grad_out.reshape(-1, grad_out.shape[-1])
    results = []
    for tap_z in range(3):
        for tap_x in range(3):
            for tap_y in range(3):
                window = tap_window(
                    padded, tap_z, tap_x, tap_y, extent_z, extent_x, extent_y, stride
                )
                flat_tap = window.reshape(-1, window.shape[-1])
                results.append(
                    lax.dot_general(
                        flat_tap,
                        flat_grad,
                        (((0,), (0,)), ((), ())),
                        preferred_element_type=jnp.float32,
                    )
                )
    return jnp.stack(results).reshape(3, 3, 3, padded.shape[-1], grad_out.shape[-1])


def input_grad(grad_out, weight, extent_z, extent_x, extent_y):
    leading = grad_out.shape[0]
    channels = weight.shape[3]
    flat_grad = grad_out.reshape(-1, grad_out.shape[-1])
    buckets = {}
    for tap_z in range(3):
        for tap_x in range(3):
            for tap_y in range(3):
                contrib = lax.dot_general(
                    flat_grad,
                    weight[tap_z, tap_x, tap_y],
                    (((1,), (1,)), ((), ())),
                    preferred_element_type=jnp.float32,
                )
                contrib = contrib.reshape(leading, extent_z, extent_x, extent_y, channels)
                placed = jnp.pad(
                    contrib,
                    (
                        (0, 0),
                        (tap_z // 2, 1 - tap_z // 2),
                        (tap_x // 2, 1 - tap_x // 2),
                        (tap_y // 2, 1 - tap_y // 2),
                        (0, 0),
                    ),
                )
                parity = (tap_z % 2, tap_x % 2, tap_y % 2)
                buckets[parity] = placed if parity not in buckets else buckets[parity] + placed
    planes_z = []
    for par_z in range(2):
        planes_x = []
        for par_x in range(2):
            planes_x.append(jnp.stack([buckets[par_z, par_x, par_y] for par_y in range(2)], axis=4))
        planes_z.append(jnp.stack(planes_x, axis=3))
    assembled = jnp.stack(planes_z, axis=2)
    assembled = assembled.reshape(
        leading, 2 * extent_z + 2, 2 * extent_x + 2, 2 * extent_y + 2, channels
    )
    return assembled[:, 1:-1, 1:-1, 1:-1, :]


def split_body(volume, targets, front_weight, stride_weight, hidden_weight, output_weight):
    highest = lax.Precision.HIGHEST
    slabs = lax.axis_size("slab")
    batches = lax.axis_size("batch")
    inner = front_weight.shape[-1]
    leading, thick, extent_x, extent_y, channels = volume.shape
    depth = thick * slabs
    outputs = output_weight.shape[-1]
    haloed = with_halo(volume, (("slab", 1),), 1)
    padded = jnp.pad(haloed, ((0, 0), (0, 0), (1, 1), (1, 1), (0, 0)))
    front_pre = conv_apply(padded, front_weight, thick, extent_x, extent_y, 1)
    front_act = jax.nn.silu(front_pre).astype(jnp.bfloat16)
    merged = front_act.reshape(leading, thick, extent_x, extent_y * inner)
    sample_act = lax.all_to_all(merged, "slab", split_axis=0, concat_axis=1, tiled=True)
    sample_act = sample_act.reshape(1, depth, extent_x, extent_y, inner)
    half_z = depth // 2
    half_x = extent_x // 2
    half_y = extent_y // 2
    cells = half_z * half_x * half_y
    stride_pad = jnp.pad(sample_act, ((0, 0), (1, 1), (1, 1), (1, 1), (0, 0)))
    partial_pre = conv_apply(stride_pad, stride_weight, half_z, half_x, half_y, 2)
    stride_pre = lax.psum_scatter(partial_pre, "chan", scatter_dimension=4, tiled=True)
    pooled = jnp.sum(jax.nn.silu(stride_pre), axis=(0, 1, 2, 3)) / cells
    hidden_pre = lax.psum(jnp.dot(pooled, hidden_weight, precision=highest), "chan")
    hidden_act = jax.nn.silu(hidden_pre)
    predicted = jnp.dot(hidden_act, output_weight, precision=highest)
    target_row = lax.dynamic_index_in_dim(targets, lax.axis_index("slab"), 0, keepdims=False)
    residual = predicted - target_row
    squared = jnp.sum(residual * residual)
    grad_output = jnp.outer(hidden_act, residual)
    grad_hidden_pre = jnp.dot(output_weight, residual, precision=highest) * swish_slope(hidden_pre)
    grad_hidden = jnp.outer(pooled, grad_hidden_pre)
    grad_pooled = jnp.dot(hidden_weight, grad_hidden_pre, precision=highest)
    grad_stride_pre = (grad_pooled / cells * swish_slope(stride_pre)).astype(jnp.bfloat16)
    full_grad = lax.all_gather(grad_stride_pre, "chan", axis=4, tiled=True)
    grad_stride = kernel_grad(stride_pad, full_grad, half_z, half_x, half_y, 2)
    grad_act = input_grad(full_grad, stride_weight, half_z, half_x, half_y).astype(jnp.bfloat16)
    returned = lax.all_to_all(
        grad_act.reshape(1, depth, extent_x, extent_y * inner),
        "slab",
        split_axis=1,
        concat_axis=0,
        tiled=True,
    )
    returned = returned.reshape(leading, thick, extent_x, extent_y, inner)
    grad_front_pre = (returned * swish_slope(front_pre)).astype(jnp.bfloat16)
    grad_front = kernel_grad(padded, grad_front_pre, thick, extent_x, extent_y, 1)
    grad_front, grad_stride, grad_hidden, grad_output, squared = lax.psum(
        (grad_front, grad_stride, grad_hidden, grad_output, squared), ("slab", "batch")
    )
    loss = (squared / (slabs * batches * outputs)).reshape(1)
    return (grad_front, grad_stride, grad_hidden, grad_output, loss)


MESH = pl.DeviceIdType.MESH


def sigmoid(v):
    return 1.0 / (1.0 + jnp.exp(-v))


def remote(source, target, send_sem, recv_sem, device):
    return pltpu.make_async_remote_copy(
        src_ref=source, dst_ref=target, send_sem=send_sem, recv_sem=recv_sem,
        device_id=device, device_id_type=MESH,
    )


def slab_order(slab, slabs):
    top = slabs - 1
    far = top * (1 - slab // (slabs // 2))
    near = slab + 1 - 2 * lax.rem(slab, 2)
    return [slab, near, slabs * top // 2 - slab - near - far, far]


def chain_kernel(
    shape,
    volume_hbm, targets_hbm, front_hbm, stride_hbm, hidden_hbm, output_hbm,
    taps_ref, taps_other_ref, turned_ref, stride_grad_ref, hidden_grad_ref, output_grad_ref, loss_ref,
    volume_ref, split_ref, front_turned_ref, front_ref, front_pre_ref, slope_ref, strided_ref,
    act_ref, act_out_ref, stride_ref, back_ref, hidden_ref, output_ref, targets_ref,
    spread_ref, head_ref, head_out_ref, grad_ref, turned_out_ref, hidden_split_ref, hidden_turned_ref, target_rows_ref,
    local_sem, send_sem, piece_sem, pass_send_sem, pass_sem, pair_send_sem, pair_sem, target_sem, ready_sem,
):
    slabs, batches, leading, thick, extent_x, extent_y, channels, inner = shape
    slab, batch, chan = lax.axis_index("slab"), lax.axis_index("batch"), lax.axis_index("chan")
    f32, bf16 = jnp.float32, jnp.bfloat16
    highest = lax.Precision.HIGHEST
    half = leading // 2
    depth = slabs * thick
    half_y = extent_y // 2
    half_z, half_x = depth // 2, extent_x // 2
    planes = half_z * half_x
    samples = batches * half
    group = samples * half_y
    rows = 2 * group
    cells = planes * half_y
    wide = 3 * channels
    features = stride_ref.shape[-1]
    share = hidden_hbm.shape[0]
    outputs = output_hbm.shape[0]
    sibling = {"chan": 1 - chan}
    mine = batch * slabs + slab
    pieces = batches * slabs

    across = {"batch": 1 - batch}
    barrier = pltpu.get_barrier_semaphore()
    pl.semaphore_signal(barrier, inc=1, device_id=sibling, device_id_type=MESH)

    def is_own(b, at):
        return (batch == b) & (slab == at)

    for at in reversed(range(slabs)):
        for b in reversed(range(batches)):
            @pl.when((slab <= at) & (batch <= b) & jnp.logical_not(is_own(b, at)))
            def _():
                pl.semaphore_signal(barrier, inc=1, device_id={"batch": b, "slab": at}, device_id_type=MESH)

    local = [
        pltpu.make_async_copy(source, target, local_sem.at[i])
        for i, (source, target) in enumerate([
            (volume_hbm.at[pl.ds(chan * half, half)], volume_ref.at[0, mine]),
            (front_hbm, front_turned_ref.at[:, pl.ds(0, inner)]),
            (stride_hbm, stride_ref.at[:, pl.ds(0, inner)]),
            (hidden_hbm, hidden_ref.at[pl.ds(chan * share, share)]),
            (output_hbm, output_ref),
            (targets_hbm, targets_ref.at[pl.ds(batch * leading, leading)]),
            (volume_hbm.at[pl.ds((1 - chan) * half, half)], volume_ref.at[1, mine]),
        ])
    ]
    for copy in local:
        copy.start()

    pl.semaphore_wait(barrier, (batch + 1) * (slab + 1))

    sends = []

    def send(copy):
        copy.start()
        sends.append(copy)

    pair = [
        remote(front_hbm, front_turned_ref.at[:, pl.ds(inner, inner)], pair_send_sem.at[0], pair_sem.at[0], sibling),
        remote(stride_hbm, stride_ref.at[:, pl.ds(inner, inner)], pair_send_sem.at[1], pair_sem.at[1], sibling),
        remote(hidden_hbm, hidden_ref.at[pl.ds(chan * share, share)], pair_send_sem.at[2], pair_sem.at[2], sibling),
        remote(act_out_ref, act_ref.at[1], pair_send_sem.at[3], pair_sem.at[3], sibling),
        remote(
            spread_ref.at[0, pl.ds(0, half_z), pl.ds(0, half_x)], spread_ref.at[1, pl.ds(0, half_z), pl.ds(0, half_x)],
            pair_send_sem.at[4], pair_sem.at[4], sibling,
        ),
        remote(head_out_ref, head_ref.at[1], pair_send_sem.at[5], pair_sem.at[5], sibling),
        remote(turned_out_ref, turned_ref.at[1], pair_send_sem.at[6], pair_sem.at[6], sibling),
    ]
    order = slab_order(slab, slabs)
    own = volume_hbm.at[pl.ds(chan * half, half)]

    def piece(side, b, at):
        return volume_ref.at[side, b * slabs + at]

    place = targets_ref.at[pl.ds(batch * leading, leading)]
    spread = {}
    for at in range(slabs):
        for b in range(batches):
            number = b * slabs + at
            spread[b, at] = remote(
                own, piece(0, batch, slab), send_sem.at[number], piece_sem.at[mine], {"batch": b, "slab": at}
            )
    targets_copy = remote(targets_hbm, place, send_sem.at[pieces], target_sem, across)

    def below(b, at):
        return (slab >= at) & (batch >= b) & jnp.logical_not(is_own(b, at))

    def send_below(first):
        for at in (range(slabs) if first else reversed(range(slabs))):
            for b in range(batches):
                if first or (at or b) and at < slabs - 1:
                    @pl.when(below(b, at))
                    def _():
                        spread[b, at].start()

    late = slab == slabs - 1

    @pl.when(late)
    def _():
        spread[0, 0].start()

        @pl.when(batch == 1)
        def _():
            spread[0, slabs - 1].start()

    @pl.when(jnp.logical_not(late))
    def _():
        send_below(True)

    for at in range(slabs):
        for b in range(batches):
            @pl.when(below(b, at))
            def _():
                pl.semaphore_signal(ready_sem.at[mine], inc=1, device_id={"batch": b, "slab": at}, device_id_type=MESH)

    @pl.when(batch == 1)
    def _():
        targets_copy.start()

    send(pair[0])
    send(pair[1])
    send(pair[2])

    front_pre_ref[...] = jnp.zeros(front_pre_ref.shape, f32)
    edge = jnp.zeros((depth, rows, wide), bf16)
    for ref in (taps_ref, taps_other_ref):
        ref[:, 0] = edge
        ref[:, extent_x + 1] = edge
    strided_ref[0] = jnp.zeros((extent_x + 1, group, wide), bf16)
    strided_ref[:, 0] = jnp.zeros((depth + 1, group, wide), bf16)
    for side in range(2):
        spread_ref[side, half_z] = jnp.zeros((half_x + 1, group, 2 * features), bf16)
        spread_ref[side, :, half_x] = jnp.zeros((half_z + 1, group, 2 * features), bf16)
    blank = jnp.zeros((features, channels), bf16)
    for tap in range(9):
        back_ref[tap, features:, :channels] = blank

    @pl.when(late)
    def _():
        spread[0, 0].wait_send()
        send_below(False)

    row = lax.broadcasted_iota(jnp.int32, (group, channels), 0)
    first = (row & (half_y - 1)) == 0
    last = (row & (half_y - 1)) == half_y - 1
    lane_low = lax.broadcasted_iota(jnp.int32, (group, channels), 1) < inner

    def fill(side, at):
        for plane in range(thick):
            for x in range(extent_x):
                slot = plane * extent_x + x
                for b in range(batches):
                    split_ref[side, slot, b * half * extent_y : (b + 1) * half * extent_y] = (
                        volume_ref[side, b * slabs + at, :, plane, x].astype(f32).reshape(half * extent_y, channels)
                    )
                even = split_ref[side, slot, pl.ds(0, group, stride=2), :]
                odd = split_ref[side, slot, pl.ds(1, group, stride=2), :]
                before = jnp.where(first, 0.0, pltpu.roll(odd, 1, 0)).astype(bf16)
                after = jnp.where(last, 0.0, pltpu.roll(even, group - 1, 0)).astype(bf16)
                even, odd = even.astype(bf16), odd.astype(bf16)
                z = at * thick + plane
                ref = taps_other_ref if side else taps_ref
                ref[z, x + 1, :group] = jnp.concatenate([before, even, odd], axis=1)
                ref[z, x + 1, group:] = jnp.concatenate([even, odd, after], axis=1)

    plane_cells = extent_x * rows

    def front(at):
        window = jnp.concatenate(
            [
                taps_ref[pl.ds(at * thick, thick), kx : kx + extent_x].reshape(thick * plane_cells, wide)
                for kx in range(3)
            ],
            axis=1,
        )
        sums = jnp.dot(window, front_ref[...], preferred_element_type=f32)

        def block(plane, kz):
            return sums[plane * plane_cells : (plane + 1) * plane_cells, kz * channels : (kz + 1) * channels]

        base = at * thick
        front_pre_ref[base] += block(0, 2)
        front_pre_ref[base + 1] += block(0, 1) + block(1, 2)
        front_pre_ref[base + 2] += block(0, 0) + block(1, 1)
        front_pre_ref[base + 3] += block(1, 0)

    slots = {}
    for pz in range(2):
        for px in range(2):
            for sz in range(pz + 1):
                for sx in range(px + 1):
                    kz = 1 if pz == 0 else 2 - 2 * sz
                    kx = 1 if px == 0 else 2 - 2 * sx
                    slots[pz, px, sz, sx] = (len(slots), kz, kx)

    other = 1 - batch

    def arrived(b, at):
        remote(piece(0, b, at), piece(0, b, at), send_sem.at[0], piece_sem.at[b * slabs + at], sibling).wait_recv()

    def pass_on(slot, b, at):
        number = b * slabs + at
        send(remote(piece(0, b, at), piece(1, b, at), pass_send_sem.at[slot], pass_sem.at[number], sibling))

    def prepare_front():
        local[1].wait()
        pair[0].wait_recv()
        for kz in range(3):
            for tap in range(9):
                front_ref[tap * channels : (tap + 1) * channels, kz * channels : (kz + 1) * channels] = jnp.transpose(
                    front_turned_ref[9 * kz + tap]
                )

    def prepare_back():
        local[2].wait()
        pair[1].wait_recv()
        for slot, kz, kx in slots.values():
            start = 9 * kz + 3 * kx
            back_ref[slot, :features, :channels] = jnp.transpose(stride_ref[start + 1])
            back_ref[slot, :features, channels:] = jnp.transpose(stride_ref[start + 2])
            back_ref[slot, features:, channels:] = jnp.transpose(stride_ref[start])

    local[0].wait()
    local[6].wait()
    for level in range(slabs):
        @pl.when((slab < level) & (batch == 0))
        def _():
            pl.semaphore_wait(ready_sem.at[level], 1)
            spread[0, level].start()

        @pl.when((slab == level) & (batch == 0))
        def _():
            pl.semaphore_wait(ready_sem.at[slabs + level], 1)
            targets_copy.start()
            for at in reversed(range(level + 1)):
                spread[1, at].start()

        @pl.when((slab < level) & (batch == 0))
        def _():
            pl.semaphore_wait(ready_sem.at[slabs + level], 1)
            spread[1, level].start()

        @pl.when((slab < level) & (batch == 1))
        def _():
            pl.semaphore_wait(ready_sem.at[slabs + level], 1)
            spread[0, level].start()
            spread[1, level].start()

    prepare_front()

    def other_fill(i):
        at = order[i]
        for b in ([batch, other] if i else [other]):
            remote(
                piece(1, b, at), piece(1, b, at), send_sem.at[0], pass_sem.at[b * slabs + at], sibling
            ).wait_recv()
        fill(1, at)

    far = order[slabs - 1] // (slabs - 1)

    def activate(z):
        total = front_pre_ref[z + 1]
        logistic = sigmoid(total)
        act = (total * logistic).reshape(extent_x, 2, group, channels)
        slope_ref[z] = (logistic * (1.0 + total * (1.0 - logistic))).reshape(extent_x, 2, group, channels)
        for x in range(extent_x):
            even, odd = act[x, 0], act[x, 1]
            before = jnp.where(first, 0.0, pltpu.roll(odd, 1, 0)).astype(bf16)
            strided_ref[z + 1, x + 1] = jnp.concatenate([before, even.astype(bf16), odd.astype(bf16)], axis=1)
            where = (lax.rem(z, 2), x % 2, (z // 2) * half_x + x // 2)
            act_ref[(0,) + where] = jnp.where(lane_low, even, pltpu.roll(odd, inner, 1)).astype(bf16)
            act_out_ref[where] = jnp.where(lane_low, pltpu.roll(even, inner, 1), odd).astype(bf16)

    all_samples = batches * leading

    def halves(value):
        high = value.astype(bf16)
        return high, (value - high.astype(f32)).astype(bf16)

    def prepare_head():
        for copy in local[3:6]:
            copy.wait()
        pair[2].wait_recv()
        remote(
            targets_hbm, targets_ref.at[pl.ds(other * leading, leading)], send_sem.at[0], target_sem, sibling
        ).wait_recv()
        for ref, value in ((hidden_split_ref, hidden_ref[...]), (hidden_turned_ref, jnp.transpose(hidden_ref[...]))):
            high, low = halves(value)
            depth_of = value.shape[0]
            ref[:depth_of] = high
            ref[depth_of : 2 * depth_of] = high
            ref[2 * depth_of :] = low
        owner = lax.broadcasted_iota(jnp.int32, (group, all_samples), 1)
        of_row = lax.broadcasted_iota(jnp.int32, (group, all_samples), 0) // half_y
        wanted = (of_row // half) * leading + chan * half + of_row % half
        member = (owner == wanted).astype(f32)
        target_rows = jnp.dot(member, targets_ref[...], precision=highest, preferred_element_type=f32)
        for o in range(outputs):
            target_rows_ref[o] = jnp.broadcast_to(target_rows[:, o : o + 1], (group, channels))

    def dot_split(value, ref):
        high, low = halves(value)
        return jnp.dot(jnp.concatenate([high, low, high], axis=1), ref[...], preferred_element_type=f32)

    arrived(other, slab)
    pass_on(0, other, slab)
    fill(0, slab)
    front(slab)
    prepare_back()
    prepare_head()
    for i in range(1, slabs):
        at = order[i]
        for b in (batch, other):
            arrived(b, at)
            pass_on(2 * i - 1 if b is batch else 2 * i, b, at)
        fill(0, at)
        front(at)
        if i == 2:
            for k in range(depth - thick - 1):
                activate((1 - far) * (thick + 1) + k)

    for k in range(thick + 1):
        activate(far * (depth - thick - 1) + k)
    send(pair[3])

    windows = jnp.concatenate(
        [
            jnp.concatenate(
                [strided_ref[kz + 2 * z, kx + 2 * x] for z in range(half_z) for x in range(half_x)], axis=0
            )
            for kz in range(3) for kx in range(3)
        ],
        axis=1,
    )
    pre = jnp.dot(windows, stride_ref[...].reshape(27 * channels, features), preferred_element_type=f32)
    logistic = sigmoid(pre)
    summed = jnp.sum((pre * logistic).reshape(planes, group, features), axis=0)
    slope = (logistic * (1.0 + pre * (1.0 - logistic))).reshape(planes, group, features)
    wide_row = lax.broadcasted_iota(jnp.int32, (group, features), 0)
    step = 1
    while step < half_y:
        high = (wide_row & step) != 0
        summed = summed + jnp.where(high, pltpu.roll(summed, step, 0), pltpu.roll(summed, group - step, 0))
        step *= 2
    pooled = summed / cells
    output = output_ref[...]
    hidden_pre = dot_split(pooled, hidden_split_ref)
    hidden_logistic = sigmoid(hidden_pre)
    hidden_act = hidden_pre * hidden_logistic
    hidden_slope = hidden_logistic * (1.0 + hidden_pre * (1.0 - hidden_logistic))
    lane = lax.broadcasted_iota(jnp.int32, (group, channels), 1)
    residuals = jnp.zeros((group, channels), f32)
    back = jnp.zeros((group, output.shape[1]), f32)
    for o in range(outputs):
        residual = jnp.sum(hidden_act * output[o : o + 1], axis=1, keepdims=True) - target_rows_ref[o]
        back = back + residual * output[o : o + 1]
        residuals = jnp.where(lane == o, residual, residuals)
    grad_hidden_pre = back * hidden_slope
    grad_pooled = dot_split(grad_hidden_pre, hidden_turned_ref)
    grad_pre = slope * (grad_pooled / cells)[None]
    grad_next = jnp.where(
        ((wide_row & (half_y - 1)) == half_y - 1)[None],
        0.0,
        jnp.stack([pltpu.roll(grad_pre[i], group - 1, 0) for i in range(planes)]),
    )
    both = jnp.concatenate([grad_pre, grad_next], axis=2).astype(bf16)
    spread_ref[0, :half_z, :half_x] = both.reshape(half_z, half_x, group, 2 * features)
    send(pair[4])
    low_half, high_half = pooled[:, :share], pooled[:, share:]
    head_ref[0, 0] = jnp.where(chan == 0, low_half, high_half)
    head_out_ref[0] = jnp.where(chan == 0, high_half, low_half)
    for i, value in ((1, grad_hidden_pre), (2, hidden_act), (3, residuals)):
        head_ref[0, i] = value
        head_out_ref[i] = value
    send(pair[5])

    def shifted(side, sz, sx):
        return spread_ref[side, sz : sz + half_z, sx : sx + half_x].reshape(planes * group, 2 * features)

    for pz in range(2):
        for px in range(2):
            moves = [(sz, sx) for sz in range(pz + 1) for sx in range(px + 1)]
            start = slots[pz, px, 0, 0][0]
            left = jnp.concatenate([shifted(0, sz, sx) for sz, sx in moves], axis=1)
            right = back_ref[start : start + len(moves)].reshape(len(moves) * 2 * features, 2 * channels)
            grad = jnp.dot(left, right, preferred_element_type=f32)
            grad = grad.reshape(half_z, half_x, group, 2 * channels)
            for z in range(half_z):
                for x in range(half_x):
                    for py in range(2):
                        value = grad[z, x, :, py * channels : (py + 1) * channels].astype(bf16).astype(f32)
                        at = (2 * z + pz, 2 * x + px, py)
                        grad_ref[at] = (value * slope_ref[at]).astype(bf16)
    for z in range(depth):
        turned = jnp.transpose(grad_ref[z].reshape(plane_cells, channels))
        turned_ref[0, :, z * plane_cells : (z + 1) * plane_cells] = turned[:inner]
        turned_out_ref[:, z * plane_cells : (z + 1) * plane_cells] = turned[inner:]
    send(pair[6])

    for i in range(slabs):
        other_fill(i)

    pair[3].wait_recv()
    pair[4].wait_recv()
    turned_act = {
        (pz, px): jnp.concatenate(
            [jnp.transpose(act_ref[side, pz, px].reshape(planes * group, channels)) for side in range(2)], axis=1
        )
        for pz in range(2) for px in range(2)
    }
    for sz in range(2):
        for sx in range(2):
            right = jnp.concatenate([shifted(side, sz, sx) for side in range(2)], axis=0)
            for pz in range(sz, 2):
                for px in range(sx, 2):
                    _, kz, kx = slots[pz, px, sz, sx]
                    grad = jnp.dot(turned_act[pz, px], right, preferred_element_type=f32)
                    start = 9 * kz + 3 * kx
                    stride_grad_ref[start + 1] = grad[:inner, :features]
                    stride_grad_ref[start + 2] = grad[inner:, :features]
                    stride_grad_ref[start] = grad[inner:, features:]

    pair[5].wait_recv()
    pooled_all, hidden_pre_all, hidden_all, residual_all = [
        jnp.concatenate([head_ref[0, i], head_ref[1, i]], axis=0) for i in range(4)
    ]

    def outer(left, right):
        return lax.dot_general(
            left, right, (((0,), (0,)), ((), ())), precision=highest, preferred_element_type=f32
        ) / half_y

    hidden_grad_ref[...] = outer(pooled_all, hidden_pre_all)
    output_grad_ref[...] = outer(residual_all, hidden_all)[:outputs]
    loss_ref[...] = jnp.sum(residual_all * residual_all, keepdims=True) / (half_y * all_samples * outputs)

    pair[6].wait_recv()
    for at in range(slabs):
        for b in range(batches):
            waited = is_own(b, at) if at or b else is_own(b, at) | late

            @pl.when(jnp.logical_not(waited))
            def _():
                spread[b, at].wait_send()
    targets_copy.wait_send()
    for copy in sends:
        copy.wait_send()


def kernel_grads(
    shape,
    taps_ref, taps_other_ref, turned_ref, stride_ref, hidden_ref, output_ref, loss_ref,
    front_out, stride_out, hidden_out, output_out, loss_out,
    front_ref, front_sem, other_sem,
):
    slabs, batches, leading, thick, extent_x, extent_y, channels, inner = shape
    f32, bf16 = jnp.float32, jnp.bfloat16
    depth = slabs * thick
    rows = taps_ref.shape[2]
    plane_cells = extent_x * rows
    wide = 3 * channels
    others = [
        pltpu.make_async_copy(source, target, other_sem.at[i])
        for i, (source, target) in enumerate(
            [(stride_ref, stride_out), (hidden_ref, hidden_out), (output_ref, output_out), (loss_ref, loss_out)]
        )
    ]
    for copy in others:
        copy.start()
    edge = jnp.zeros((inner, plane_cells), bf16)

    def stacked(side):
        grads = turned_ref[side]
        return jnp.concatenate(
            [
                jnp.concatenate([grads[:, plane_cells:], edge], axis=1),
                grads,
                jnp.concatenate([edge, grads[:, :-plane_cells]], axis=1),
            ],
            axis=0,
        )

    left = jnp.concatenate([stacked(0), stacked(1)], axis=1)

    def send_out(group):
        place = pl.ds(3 * group, 3)
        return pltpu.make_async_copy(front_ref.at[place], front_out.at[place], front_sem.at[group])

    def window(kx):
        return jnp.concatenate(
            [ref[:, kx : kx + extent_x].reshape(depth * plane_cells, wide) for ref in (taps_ref, taps_other_ref)], axis=0
        )

    for columns in ((0, 1), (2,)):
        right = jnp.concatenate([window(kx) for kx in columns], axis=1)
        grads = jnp.dot(left, right, preferred_element_type=f32)
        for i, kx in enumerate(columns):
            for kz in range(3):
                for ky in range(3):
                    start = i * wide + ky * channels
                    front_ref[9 * kz + 3 * kx + ky] = grads[kz * inner : (kz + 1) * inner, start : start + channels]
                send_out(3 * kz + kx).start()
    for group in range(9):
        send_out(group).wait()
    for copy in others:
        copy.wait()


def chain(shape, volume, targets, front_turned, stride_own, hidden_weight, output_turned):
    slabs, batches, leading, thick, extent_x, extent_y, channels, inner = shape
    f32, bf16 = jnp.float32, jnp.bfloat16
    features = stride_own.shape[-1]
    share, hid = hidden_weight.shape
    outputs = output_turned.shape[0]
    half = leading // 2
    pieces = slabs * batches
    depth = slabs * thick
    group = batches * half * extent_y // 2
    rows = 2 * group
    half_z, half_x = depth // 2, extent_x // 2
    planes = half_z * half_x
    plane_cells = extent_x * rows
    wide = 3 * channels
    vmem = pl.BlockSpec(memory_space=pltpu.VMEM)
    anywhere = pl.BlockSpec(memory_space=pl.ANY)
    dma = pltpu.SemaphoreType.DMA
    operands = [
        pltpu.with_memory_space_constraint(x, pltpu.HBM)
        for x in (volume, targets, front_turned, stride_own, hidden_weight, output_turned)
    ]
    stages = pl.pallas_call(
        functools.partial(chain_kernel, shape),
        out_shape=(
            jax.ShapeDtypeStruct((depth, extent_x + 2, rows, wide), bf16),
            jax.ShapeDtypeStruct((depth, extent_x + 2, rows, wide), bf16),
            jax.ShapeDtypeStruct((2, inner, depth * plane_cells), bf16),
            jax.ShapeDtypeStruct((27, inner, features), f32),
            jax.ShapeDtypeStruct((share, hid), f32),
            jax.ShapeDtypeStruct((outputs, hid), f32),
            jax.ShapeDtypeStruct((1, 1), f32),
        ),
        in_specs=[anywhere] * 6,
        out_specs=[vmem] * 7,
        scratch_shapes=[
            pltpu.VMEM((2, pieces, half) + volume.shape[1:], bf16),
            pltpu.VMEM((2, thick * extent_x, rows, channels), f32),
            pltpu.VMEM((27, channels, channels), bf16),
            pltpu.VMEM((9 * channels, wide), bf16),
            pltpu.VMEM((depth + 2, plane_cells, channels), f32),
            pltpu.VMEM((depth, extent_x, 2, group, channels), f32),
            pltpu.VMEM((depth + 1, extent_x + 1, group, wide), bf16),
            pltpu.VMEM((2, 2, 2, planes, group, channels), bf16),
            pltpu.VMEM((2, 2, planes, group, channels), bf16),
            pltpu.VMEM((27, channels, features), bf16),
            pltpu.VMEM((9, 2 * features, 2 * channels), bf16),
            pltpu.VMEM((2 * share, hid), f32),
            pltpu.VMEM((outputs, hid), f32),
            pltpu.VMEM((batches * leading, outputs), f32),
            pltpu.VMEM((2, half_z + 1, half_x + 1, group, 2 * features), bf16),
            pltpu.VMEM((2, 4, group, channels), f32),
            pltpu.VMEM((4, group, channels), f32),
            pltpu.VMEM((depth, extent_x, 2, group, channels), bf16),
            pltpu.VMEM((inner, depth * plane_cells), bf16),
            pltpu.VMEM((6 * share, hid), bf16),
            pltpu.VMEM((3 * hid, 2 * share), bf16),
            pltpu.VMEM((outputs, group, channels), f32),
            dma((7,)), dma((pieces + 1,)), dma((pieces,)), dma((pieces,)), dma((pieces,)),
            dma((7,)), dma((7,)), dma, pltpu.SemaphoreType.REGULAR((pieces,)),
        ],
        compiler_params=pltpu.CompilerParams(
            collective_id=0, has_side_effects=True, vmem_limit_bytes=40 << 20
        ),
    )(*operands)
    return pl.pallas_call(
        functools.partial(kernel_grads, shape),
        out_shape=(
            jax.ShapeDtypeStruct((27, inner, channels), f32),
            jax.ShapeDtypeStruct((27, inner, features), f32),
            jax.ShapeDtypeStruct((share, hid), f32),
            jax.ShapeDtypeStruct((outputs, hid), f32),
            jax.ShapeDtypeStruct((1, 1), f32),
        ),
        in_specs=[vmem] * 7,
        out_specs=[anywhere] * 5,
        scratch_shapes=[pltpu.VMEM((27, inner, channels), f32), dma((9,)), dma((4,))],
        compiler_params=pltpu.CompilerParams(vmem_limit_bytes=24 << 20),
    )(*stages)


def body(volume, targets, front_weight, stride_weight, hidden_weight, output_weight):
    slabs = lax.axis_size("slab")
    batches = lax.axis_size("batch")
    inner = front_weight.shape[-1]
    leading, thick, extent_x, extent_y, channels = volume.shape
    features = stride_weight.shape[-1]
    small = (slabs, batches, leading, thick, extent_x, extent_y) == (4, 2, 4, 2, 4, 8)
    if not small:
        return split_body(volume, targets, front_weight, stride_weight, hidden_weight, output_weight)
    shape = (slabs, batches) + volume.shape + (inner,)
    grad_front, grad_stride, grad_hidden, grad_output, loss = chain(
        shape, volume, targets,
        jnp.swapaxes(front_weight.reshape(27, channels, inner), 1, 2),
        stride_weight.reshape(27, inner, features), hidden_weight, output_weight.T,
    )
    return (
        jnp.swapaxes(grad_front, 1, 2).reshape(3, 3, 3, channels, inner),
        grad_stride.reshape(3, 3, 3, inner, features),
        grad_hidden,
        grad_output.T,
        loss.reshape(1),
    )


def solution(mesh):
    in_specs = (
        P(("groups", "batch"), "slab", None, None, None),
        P(("groups", "batch"), None),
        P(None, None, None, None, "chan"),
        P(None, None, None, "chan", None),
        P("chan", None),
        P(),
    )
    out_specs = (
        P("groups", None, None, None, "chan"),
        P("groups", None, None, "chan", None),
        P(("groups", "chan"), None),
        P("groups", None),
        P("groups"),
    )
    return jax.shard_map(body, mesh=mesh, in_specs=in_specs, out_specs=out_specs, check_vma=False)
```
